128 devices in a mesh: dp: 8 (over x_hi, z), fsdp: 8 (over y, core), enc: 2 (over x_lo).
Axes of the slice: x: 4 (x_hi: 2, x_lo: 2; x = x_hi * 2 + x_lo), y: 4, z: 4, core: 2. Of those that a mesh axis runs over, the one named last changes fastest.
Arguments:
- queries: bfloat16 [12288, 4096], P(('dp', 'fsdp'), 'enc'), may hold values from -9 to 9
- nbr_keys: bfloat16 [384, 128, 4096], P('dp', 'fsdp', 'enc'), may hold values from -6 to 6
- nbr_values: bfloat16 [384, 128, 4096], P('dp', 'fsdp', 'enc'), may hold values from -6 to 6
- out_proj: bfloat16 [4096, 8192], P('enc', 'fsdp'), may hold values from -0.09375 to 0.09375
- nbr_source: int32 [192, 2], replicated, may hold values from 0 to 7, as said below
- nbr_index: int32 [192, 2], replicated, may hold values from 0 to 47
- nbr_count: int32 [192], replicated, may hold values from 1 to 2
- cotangent: bfloat16 [12288, 8192], P('dp', 'fsdp'), may hold values from -2.390625 to 2.390625
Outputs:
- attended: bfloat16 [12288, 4096], P(('dp', 'fsdp'), 'enc')
- grad_queries: bfloat16 [12288, 4096], P(('dp', 'fsdp'), 'enc')
- grad_keys: bfloat16 [384, 128, 4096], P('dp', 'fsdp', 'enc')
- grad_values: bfloat16 [384, 128, 4096], P('dp', 'fsdp', 'enc')
- grad_proj: bfloat16 [4096, 8192], P('enc', 'fsdp')
The draws below stay inside these ranges and needn't reach their ends.
Inputs may be any that keep to these rules, and one draw needn't show every extreme that they name: `nbr_source`: among the 6 slots of the spans of one device, no source group is named more than 1 times, and some group exactly 1 times.
All inputs are finite; a program needn't handle non-finite values.
Results may differ from the reference program's by a relative error of at most 0.013.
Values may be sent and summed in bfloat16 or wider, within the bound.
A program may use at most 128 MiB of HBM per device.

```python
import math
import jax
import jax.numpy as jnp
from jax import lax

D = 8192
HEADS = 32
HEAD_DIM = 128
SPAN = 64
NBR_LEN = 128
SLOTS = 2
TOK_DEV = 192
HD = 4096
SPANS_DEV = 3
TOKENS = 12288
SPANS = 192
NB_GROUP = 48
NBRS = 384
N_DP = 8
N_FSDP = 8


def draw_queries(key, part):
    base = jnp.clip(jax.random.normal(jax.random.fold_in(key, 11), (TOKENS, HD), jnp.float32), -6.0, 6.0)
    return base.astype(jnp.bfloat16)


def draw_nbr_keys(key, part):
    base = jnp.clip(jax.random.normal(jax.random.fold_in(key, 21), (NBRS, NBR_LEN, HD), jnp.float32), -6.0, 6.0)
    return base.astype(jnp.bfloat16)


def draw_nbr_source(key, part):
    groups = SPANS // SPANS_DEV
    group_keys = jax.random.split(jax.random.fold_in(key, 31), groups)
    orders = jax.vmap(lambda single: jax.random.permutation(single, N_DP))(group_keys)
    positions = jnp.arange(SLOTS * SPANS_DEV) % N_DP
    return orders[:, positions].reshape(SPANS, SLOTS).astype(jnp.int32)


def draw_nbr_count(key, part):
    document_texts = SPANS // 4 + 1
    levels = jax.random.randint(jax.random.fold_in(key, 41), (document_texts,), 0, 9)
    levels = levels.at[0].set(8).at[1].set(0)
    owner = jnp.arange(SPANS) // 4
    rolls = jax.random.randint(jax.random.fold_in(key, 42), (SPANS,), 0, 8)
    return (1 + (rolls < levels[owner]).astype(jnp.int32)).astype(jnp.int32)


def set_ends(entries, own_key, smallest, top_value):
    extent = entries.shape
    index_at = [jax.random.randint(jax.random.fold_in(own_key, axis), (), 0, extent[axis]) for axis in range(len(extent))]
    entries = entries.at[tuple(index_at)].set(smallest)
    longest = extent.index(max(extent))
    index_at[longest] = (index_at[longest] + 1) % extent[longest]
    return entries.at[tuple(index_at)].set(top_value)


def block_levels(own_key, shape, cuts, smallest, high):
    loudness, own = 1.0, jax.random.fold_in(own_key, 6)
    for dim, parts in cuts:
        heights = jnp.exp(jax.random.uniform(jax.random.fold_in(own, dim), (parts,), jnp.float32, smallest / len(cuts), high / len(cuts)))
        loudness = loudness * jnp.repeat(heights, shape[dim] // parts).reshape([-1 if axis == dim else 1 for axis in range(len(shape))])
    return loudness


def bell_draw(stream_key, dims, width, reach, cuts=(), held_as=jnp.bfloat16):
    result = jax.random.normal(stream_key, dims, jnp.float32) * width
    if len(cuts) > 0:
        result = block_levels(stream_key, dims, cuts, -0.22, 0.18) * result
    return jnp.clip(result, min=-reach, max=reach).astype(held_as)


def setup_inputs(seed: int = 0) -> dict:
    splits = jax.random.split(jax.random.key(seed), 9)
    queries = draw_queries(jax.random.fold_in(splits[8], 71), 0)
    nbr_keys = draw_nbr_keys(jax.random.fold_in(splits[8], 71), 0)
    nbr_values = bell_draw(splits[2], (NBRS, NBR_LEN, HD), 1.0, 6.0, ((0, 8), (1, 8), (2, 2)))
    out_proj = bell_draw(splits[3], (HD, D), HD ** -0.5, 0.09375, ((0, 2), (1, 8)))
    nbr_source = draw_nbr_source(jax.random.fold_in(splits[8], 71), 0)
    nbr_index = set_ends(jax.random.randint(splits[5], (SPANS, SLOTS), 0, NB_GROUP), jax.random.fold_in(splits[5], 1), 0, NB_GROUP - 1).astype(jnp.int32)
    nbr_count = draw_nbr_count(jax.random.fold_in(splits[8], 71), 0)
    cotangent = bell_draw(splits[7], (TOKENS, D), 0.3, 2.390625, ((0, 8), (1, 8)))
    return {"queries": queries, "nbr_keys": nbr_keys, "nbr_values": nbr_values, "out_proj": out_proj, "nbr_source": nbr_source, "nbr_index": nbr_index, "nbr_count": nbr_count, "cotangent": cotangent}


def reference(queries, nbr_keys, nbr_values, out_proj, nbr_source, nbr_index, nbr_count, cotangent):
    scale = 1.0 / math.sqrt(HEAD_DIM)
    ident = (nbr_source * NB_GROUP + nbr_index).astype(jnp.int32)
    upstream = jnp.dot(cotangent, out_proj.T, preferred_element_type=jnp.float32).astype(jnp.bfloat16)
    live_keys = jnp.repeat(jnp.arange(SLOTS)[None, :] < nbr_count[:, None], NBR_LEN, axis=1)

    def per_span(position):
        chosen = ident[position]
        keys_here = jnp.take(nbr_keys, chosen, axis=0).reshape(SLOTS * NBR_LEN, HEADS, HEAD_DIM).astype(jnp.float32)
        values_here = jnp.take(nbr_values, chosen, axis=0).reshape(SLOTS * NBR_LEN, HEADS, HEAD_DIM).astype(jnp.float32)
        first_row = (position * SPAN).astype(jnp.int32)
        query_here = lax.dynamic_slice_in_dim(queries, first_row, SPAN, 0).reshape(SPAN, HEADS, HEAD_DIM).astype(jnp.float32)
        grad_here = lax.dynamic_slice_in_dim(upstream, first_row, SPAN, 0).reshape(SPAN, HEADS, HEAD_DIM).astype(jnp.float32)
        scores = jnp.einsum('qhd,khd->hqk', query_here, keys_here) * scale
        scores = jnp.where(live_keys[position][None, None, :], scores, -1e+30)
        peak = lax.optimization_barrier(jnp.max(scores, axis=-1, keepdims=True))
        expo = jnp.exp(scores - peak)
        probs = expo / lax.optimization_barrier(jnp.sum(expo, axis=-1, keepdims=True))
        probs_b = probs.astype(jnp.bfloat16)
        attended_here = jnp.einsum('hqk,khd->qhd', probs_b.astype(jnp.float32), values_here).astype(jnp.bfloat16)
        probability_gradient = jnp.einsum('qhd,khd->hqk', grad_here, values_here)
        centre = lax.optimization_barrier(jnp.sum(probs * probability_gradient, axis=-1, keepdims=True))
        dscores = (probs * (probability_gradient - centre) * scale).astype(jnp.bfloat16)
        grad_query = jnp.einsum('hqk,khd->qhd', dscores.astype(jnp.float32), keys_here).astype(jnp.bfloat16)
        slot_key = jnp.einsum('hqk,qhd->khd', dscores.astype(jnp.float32), query_here).astype(jnp.bfloat16)
        slot_value = jnp.einsum('hqk,qhd->khd', probs_b.astype(jnp.float32), grad_here).astype(jnp.bfloat16)
        return (attended_here, grad_query, slot_key, slot_value)
    attended, grad_queries, slot_keys, slot_values = lax.map(per_span, jnp.arange(SPANS, dtype=jnp.int32))
    attended = attended.reshape(TOKENS, HD)
    grad_queries = grad_queries.reshape(TOKENS, HD)
    flat_ident = ident.reshape(-1)
    grad_keys = jax.ops.segment_sum(slot_keys.astype(jnp.float32).reshape(SPANS * SLOTS, NBR_LEN, HD), flat_ident, num_segments=NBRS).astype(jnp.bfloat16)
    grad_values = jax.ops.segment_sum(slot_values.astype(jnp.float32).reshape(SPANS * SLOTS, NBR_LEN, HD), flat_ident, num_segments=NBRS).astype(jnp.bfloat16)
    bin_rows = TOK_DEV * N_FSDP

    def add_bin(running, position):
        first_row = (position * bin_rows).astype(jnp.int32)
        rows_att = lax.dynamic_slice_in_dim(attended, first_row, bin_rows, 0)
        rows_cot = lax.dynamic_slice_in_dim(cotangent, first_row, bin_rows, 0)
        term = jnp.dot(rows_att.T, rows_cot, preferred_element_type=jnp.float32).astype(jnp.bfloat16)
        term = lax.optimization_barrier(term)
        return (running + term.astype(jnp.float32), None)
    total, _ = lax.scan(add_bin, jnp.zeros((HD, D), jnp.float32), jnp.arange(N_DP, dtype=jnp.int32))
    grad_proj = total.astype(jnp.bfloat16)
    return (attended, grad_queries, grad_keys, grad_values, grad_proj)
```

```python
import math

import jax
import jax.numpy as jnp
from jax import lax
from jax.experimental import pallas as pl
from jax.experimental.pallas import tpu as pltpu
from jax.sharding import PartitionSpec as P

HEAD_DIM = 128
SPAN = 64
SLOTS = 2
MESH = pl.DeviceIdType.MESH
ANY = pl.BlockSpec(memory_space=pl.ANY)
VM = pl.BlockSpec(memory_space=pltpu.VMEM)
SM = pl.BlockSpec(memory_space=pltpu.SMEM)
NT = (((1,), (1,)), ((), ()))
TN = (((0,), (0,)), ((), ()))
NN = (((1,), (0,)), ((), ()))
SCALE = 1.0 / math.sqrt(HEAD_DIM)
BIG = 60 << 20


def dot(a, b, dims):
    return lax.dot_general(a, b, dims, preferred_element_type=jnp.float32)


def enter(axes):
    barrier = pltpu.get_barrier_semaphore()
    total = 0
    for axis, size in axes:
        here = lax.axis_index(axis)
        for step in range(1, size):
            pl.semaphore_signal(
                barrier, inc=1, device_id={axis: lax.rem(here + step, size)}, device_id_type=MESH
            )
            total += 1
    pl.semaphore_wait(barrier, total)


def remote(src, dst, send, recv, axis, peer):
    return pltpu.make_async_remote_copy(
        src_ref=src, dst_ref=dst, send_sem=send, recv_sem=recv, device_id={axis: peer}, device_id_type=MESH
    )


def upstream_kernel(cot_ref, proj_ref, out_ref):
    rows = 512
    for start in range(0, cot_ref.shape[0], rows):
        out_ref[0, start : start + rows, :] = dot(
            cot_ref[start : start + rows, :], proj_ref[...], NT
        ).astype(jnp.bfloat16)


def project_kernel(att_ref, cot_ref, out_ref):
    out_ref[...] = dot(att_ref[0], cot_ref[...], TN).astype(jnp.bfloat16)


def spread_kernel(
    nd, nf, width, selc, q, k, v, kt, vt, qg, q_heads, q_send, k_own, v_own,
    qs, qr, ks, kr, vs, vr, gs, gr, own,
):
    dp, fs = lax.axis_index("dp"), lax.axis_index("fsdp")
    enter((("dp", nd), ("fsdp", nf)))

    def cols(ref, place):
        return ref.at[:, :, pl.ds(pl.multiple_of(place * width, width), width)]

    q_own = pltpu.make_async_copy(cols(q, fs), q_heads.at[fs], own.at[0])
    q_own.start()
    takes = [
        pltpu.make_async_copy(cols(k, fs), k_own, own.at[1]),
        pltpu.make_async_copy(cols(v, fs), v_own, own.at[2]),
    ]
    for take in takes:
        take.start()
    moves = {}
    for name, ref, out, send, recv in (
        ("q", q, q_heads, qs, qr),
        ("k", k, kt, ks, kr),
        ("v", v, vt, vs, vr),
    ):
        moves[name] = []
        for step in range(1, nf):
            peer = lax.rem(fs + step, nf)
            move = remote(cols(ref, peer), out.at[fs], send.at[step], recv.at[step], "fsdp", peer)
            move.start()
            moves[name].append(move)
    for take in takes:
        take.wait()
    puts = [
        pltpu.make_async_copy(k_own, kt.at[fs], own.at[3]),
        pltpu.make_async_copy(v_own, vt.at[fs], own.at[4]),
    ]
    for put in puts:
        put.start()
    q_own.wait()
    for move in moves["q"]:
        move.wait_recv()

    @pl.loop(0, nd)
    def _(group):
        @pl.loop(0, nf)
        def _(home):
            q_send[group, home] = q_heads[home, selc[group, home]]

    sends = []
    for step in range(1, nd):
        peer = lax.rem(dp + step, nd)
        move = remote(q_send.at[peer], qg.at[dp], gs.at[step], gr.at[step], "dp", peer)
        move.start()
        sends.append(move)
    put = pltpu.make_async_copy(q_send.at[dp], qg.at[dp], own.at[5])
    put.start()
    for move in moves["q"]:
        move.wait_send()
    for move in moves["k"] + moves["v"] + sends:
        move.wait()
    for copy in puts + [put]:
        copy.wait()


def forward_kernel(nf, refs, q, kt, vt, o_ref, st_ref):
    lane = lax.broadcasted_iota(jnp.int32, (SPAN, 128), 1)
    st_ref[...] = jnp.zeros_like(st_ref)
    o_ref[...] = jnp.zeros_like(o_ref)
    length = kt.shape[0] * kt.shape[2]

    @pl.loop(0, refs[0])
    def _(j):
        r, n = refs[1 + 3 * j], refs[2 + 3 * j]
        d, home = r // nf, r % nf
        keys = kt[:, n].reshape(length, -1)
        values = vt[:, n].reshape(length, -1)
        query = q[r]
        stats = st_ref[d]
        outs = []
        for h in range(keys.shape[1] // HEAD_DIM):
            part = slice(h * HEAD_DIM, (h + 1) * HEAD_DIM)
            scores = dot(query[:, part], keys[:, part], NT) * SCALE
            peak = jnp.max(scores, axis=1, keepdims=True)
            expo = jnp.exp(scores - peak)
            total = jnp.sum(expo, axis=1, keepdims=True)
            outs.append(dot(expo.astype(jnp.bfloat16), values[:, part], NN).astype(jnp.bfloat16))
            stats = jnp.where(lane == 4 * home + 2 * h, peak, stats)
            stats = jnp.where(lane == 4 * home + 2 * h + 1, total, stats)
        o_ref[r] = jnp.concatenate(outs, axis=1)
        st_ref[d] = stats


def meet_kernel(
    nd, nf, spans, selc, gsrc, count, u, o, st, ug, hs_out, att, u_send, o_home, st_home, hs, ss, sr, os, orr, us, ur, hsn, hr, own,
):
    dp = lax.axis_index("dp")
    enter((("dp", nd),))
    own_copies = [
        pltpu.make_async_copy(st.at[dp], st_home.at[dp], own.at[0]),
        pltpu.make_async_copy(o.at[dp], o_home.at[dp], own.at[1]),
    ]
    for copy in own_copies:
        copy.start()
    peers = [lax.rem(dp + step, nd) for step in range(1, nd)]
    stats = [
        remote(st.at[p], st_home.at[dp], ss.at[i], sr.at[i], "dp", p) for i, p in enumerate(peers)
    ]
    outs = [
        remote(o.at[p], o_home.at[dp], os.at[i], orr.at[i], "dp", p) for i, p in enumerate(peers)
    ]
    for move in stats + outs:
        move.start()

    @pl.loop(0, nd)
    def _(group):
        @pl.loop(0, nf)
        def _(home):
            u_send[group, home] = u[home * spans + selc[group, home]]

    ups = [
        remote(u_send.at[p], ug.at[dp], us.at[i], ur.at[i], "dp", p) for i, p in enumerate(peers)
    ]
    for move in ups:
        move.start()
    u_own = pltpu.make_async_copy(u_send.at[dp], ug.at[dp], own.at[2])
    u_own.start()
    for copy in own_copies:
        copy.wait()
    for move in stats + outs:
        move.wait_recv()
    lane = lax.broadcasted_iota(jnp.int32, (SPAN, 128), 1)

    def pick(array, at):
        return jnp.sum(jnp.where(lane == at, array, 0.0), axis=1, keepdims=True)

    def combine(i, table):
        home = i // spans
        g0, g1 = gsrc[2 * i], gsrc[2 * i + 1]
        both = count[i] > 1
        s0, s1 = st_home[g0], st_home[g1]
        o0, o1 = o_home[g0, home].astype(jnp.float32), o_home[g1, home].astype(jnp.float32)
        mine = u[i].astype(jnp.float32)
        pieces = []
        for h in range(u.shape[2] // HEAD_DIM):
            part = slice(h * HEAD_DIM, (h + 1) * HEAD_DIM)
            at = 4 * home + 2 * h
            m0, l0 = pick(s0, at), pick(s0, at + 1)
            m1 = jnp.where(both, pick(s1, at), -1e30)
            l1 = jnp.where(both, pick(s1, at + 1), 0.0)
            peak = jnp.maximum(m0, m1)
            a0, a1 = jnp.exp(m0 - peak), jnp.exp(m1 - peak)
            total = a0 * l0 + a1 * l1
            piece = (a0 * o0[:, part] + a1 * jnp.where(both, o1[:, part], 0.0)) / total
            pieces.append(piece.astype(jnp.bfloat16))
            centre = jnp.sum(piece * mine[:, part], axis=1, keepdims=True)
            table = jnp.where(lane == 4 * i + h, peak + jnp.log(total), table)
            table = jnp.where(lane == 4 * i + 2 + h, centre, table)
        att[i] = jnp.concatenate(pieces, axis=1)
        return table

    hs[...] = lax.fori_loop(0, nf * spans, combine, jnp.zeros((SPAN, 128), jnp.float32))
    gives = [
        remote(hs, hs_out.at[dp], hsn.at[i], hr.at[i], "dp", p) for i, p in enumerate(peers)
    ]
    for move in gives:
        move.start()
    hs_own = pltpu.make_async_copy(hs, hs_out.at[dp], own.at[3])
    hs_own.start()
    for move in stats + outs:
        move.wait_send()
    for move in ups + gives:
        move.wait()
    u_own.wait()
    hs_own.wait()


def backward_kernel(nf, spans, refs, q, u, hs, kt, vt, dq_ref, dk_ref, dv_ref, k_acc, v_acc):
    lane = lax.broadcasted_iota(jnp.int32, (SPAN, 128), 1)
    dq_ref[...] = jnp.zeros_like(dq_ref)
    k_acc[...] = jnp.zeros_like(k_acc)
    v_acc[...] = jnp.zeros_like(v_acc)
    pieces, nbrs, piece = kt.shape[0], kt.shape[1], kt.shape[2]
    length = pieces * piece

    def pick(array, at):
        return jnp.sum(jnp.where(lane == at, array, 0.0), axis=1, keepdims=True)

    @pl.loop(0, refs[0])
    def _(j):
        r, n, c = refs[1 + 3 * j], refs[2 + 3 * j], refs[3 + 3 * j]
        d, home = r // nf, r % nf
        keys = kt[:, n].reshape(length, -1)
        values = vt[:, n].reshape(length, -1)
        query, up, table = q[r], u[r], hs[d]
        at = 4 * (home * spans + c)
        dqs = []
        for h in range(keys.shape[1] // HEAD_DIM):
            part = slice(h * HEAD_DIM, (h + 1) * HEAD_DIM)
            scores = dot(query[:, part], keys[:, part], NT) * SCALE
            probs = jnp.exp(scores - pick(table, at + h))
            dprobs = dot(up[:, part], values[:, part], NT)
            ds = (probs * (dprobs - pick(table, at + 2 + h)) * SCALE).astype(jnp.bfloat16)
            dqs.append(dot(ds, keys[:, part], NN).astype(jnp.bfloat16))
            k_acc[n, :, part] += dot(ds, query[:, part], TN)
            v_acc[n, :, part] += dot(probs.astype(jnp.bfloat16), up[:, part], TN)
        dq_ref[r] = jnp.concatenate(dqs, axis=1)

    @pl.loop(0, nbrs)
    def _(n):
        dk_ref[:, n] = k_acc[n].reshape(pieces, piece, -1).astype(jnp.bfloat16)
        dv_ref[:, n] = v_acc[n].reshape(pieces, piece, -1).astype(jnp.bfloat16)


def return_kernel(
    nd, nf, width, spans, gsrc, count, dq, dk, dv, gq, gk, gv, dq_home, dq_sum, k_own, v_own,
    qs, qr, ks, kr, vs, vr, ys, yr, own,
):
    dp, fs = lax.axis_index("dp"), lax.axis_index("fsdp")
    enter((("dp", nd), ("fsdp", nf)))

    def cols(ref, place):
        return ref.at[:, :, pl.ds(pl.multiple_of(place * width, width), width)]

    firsts = [
        pltpu.make_async_copy(dq.at[dp], dq_home.at[dp], own.at[0]),
        pltpu.make_async_copy(dk.at[fs], k_own, own.at[1]),
        pltpu.make_async_copy(dv.at[fs], v_own, own.at[2]),
    ]
    for copy in firsts:
        copy.start()
    backs = []
    for step in range(1, nd):
        peer = lax.rem(dp + step, nd)
        move = remote(dq.at[peer], dq_home.at[dp], qs.at[step], qr.at[step], "dp", peer)
        move.start()
        backs.append(move)
    moves = []
    for ref, out, send, recv in ((dk, gk, ks, kr), (dv, gv, vs, vr)):
        for step in range(1, nf):
            peer = lax.rem(fs + step, nf)
            move = remote(ref.at[peer], cols(out, fs), send.at[step], recv.at[step], "fsdp", peer)
            move.start()
            moves.append(move)
    for copy in firsts:
        copy.wait()
    puts = [
        pltpu.make_async_copy(k_own, cols(gk, fs), own.at[3]),
        pltpu.make_async_copy(v_own, cols(gv, fs), own.at[4]),
    ]
    for put in puts:
        put.start()
    for move in backs:
        move.wait_recv()

    @pl.loop(0, nf)
    def _(home):
        for c in range(spans):
            i = home * spans + c
            d0 = dq_home[gsrc[2 * i], home].astype(jnp.float32)
            d1 = dq_home[gsrc[2 * i + 1], home].astype(jnp.float32)
            dq_sum[home, c] = (d0 + jnp.where(count[i] > 1, d1, 0.0)).astype(jnp.bfloat16)

    for step in range(1, nf):
        peer = lax.rem(fs + step, nf)
        move = remote(dq_sum.at[peer], cols(gq, fs), ys.at[step], yr.at[step], "fsdp", peer)
        move.start()
        moves.append(move)
    put = pltpu.make_async_copy(dq_sum.at[fs], cols(gq, fs), own.at[5])
    put.start()
    for move in backs:
        move.wait_send()
    for move in moves:
        move.wait()
    for copy in puts + [put]:
        copy.wait()


def dma(*shape):
    return pltpu.SemaphoreType.DMA(shape)


def comm(number, mib=BIG):
    return pltpu.CompilerParams(collective_id=number, has_side_effects=True, vmem_limit_bytes=mib)


def local(queries, nbr_keys, nbr_values, out_proj, nbr_source, nbr_index, nbr_count, cotangent):
    nd, nf = lax.axis_size("dp"), lax.axis_size("fsdp")
    bf, f32, i32 = jnp.bfloat16, jnp.float32, jnp.int32
    token_rows, full_width = queries.shape
    spans = token_rows // SPAN
    nbrs, piece, _ = nbr_keys.shape
    width = full_width // nf
    rows, columns = cotangent.shape
    slots = SLOTS * spans
    refs_all = nd * nf
    me = lax.axis_index("dp")

    sources = nbr_source.reshape(nd, nf, slots)
    indices = nbr_index.reshape(nd, nf, slots)
    counts = nbr_count.reshape(nd, nf, spans)
    slot = jnp.arange(slots, dtype=i32)
    my_sources = lax.dynamic_index_in_dim(sources, me, 0, keepdims=False)
    my_counts = lax.dynamic_index_in_dim(counts, me, 0, keepdims=False)
    hit = my_sources[None] == jnp.arange(nd, dtype=i32)[:, None, None]
    selc = jnp.sum(jnp.where(hit, slot // SLOTS, 0), axis=2)
    gsrc = my_sources.reshape(-1)
    count = my_counts.reshape(-1)
    alive = jnp.logical_and(
        sources == me, (slot % SLOTS)[None, None] < jnp.repeat(counts, SLOTS, axis=2)
    ).reshape(refs_all, slots)
    live = jnp.any(alive, axis=1)
    nidx = jnp.sum(jnp.where(alive, indices.reshape(refs_all, slots), 0), axis=1)
    cidx = jnp.sum(jnp.where(alive, slot // SLOTS, 0), axis=1)
    ref_iota = jnp.arange(refs_all, dtype=i32)
    rank = jnp.sum(jnp.logical_and(live[None, :], ref_iota[None, :] < ref_iota[:, None]), axis=1)
    place = jnp.logical_and(live[None, :], rank[None, :] == ref_iota[:, None])
    entry = jnp.stack([ref_iota, nidx, cidx], axis=1)
    listed = jnp.sum(jnp.where(place[:, :, None], entry[None], 0), axis=1)
    refs = jnp.concatenate([jnp.sum(live.astype(i32))[None], listed.reshape(-1)])

    partial = pl.pallas_call(
        upstream_kernel,
        grid=(nf,),
        in_specs=[
            pl.BlockSpec((rows, columns), lambda f: (0, 0), pipeline_mode=pl.Buffered(1)),
            pl.BlockSpec((width, columns), lambda f: (f, 0)),
        ],
        out_specs=pl.BlockSpec((1, rows, width), lambda f: (f, 0, 0)),
        out_shape=jax.ShapeDtypeStruct((nf, rows, width), bf),
        name="upstream",
        cost_estimate=pl.CostEstimate(
            flops=2 * rows * columns * full_width, bytes_accessed=14 << 20, transcendentals=0
        ),
    )(cotangent, out_proj)
    upstream = lax.psum_scatter(
        partial.reshape(nf * rows, width), "fsdp", scatter_dimension=0, tiled=True
    ).reshape(nf * spans, SPAN, width)

    kt, vt, qg = pl.pallas_call(
        lambda *a: spread_kernel(nd, nf, width, *a),
        in_specs=[SM, ANY, ANY, ANY],
        out_specs=[ANY, ANY, ANY],
        out_shape=[
            jax.ShapeDtypeStruct((nf, nbrs, piece, width), bf),
            jax.ShapeDtypeStruct((nf, nbrs, piece, width), bf),
            jax.ShapeDtypeStruct((nd, nf, SPAN, width), bf),
        ],
        scratch_shapes=[
            pltpu.VMEM((nf, spans, SPAN, width), bf),
            pltpu.VMEM((nd, nf, SPAN, width), bf),
            pltpu.VMEM((nbrs, piece, width), bf),
            pltpu.VMEM((nbrs, piece, width), bf),
            dma(nf), dma(nf), dma(nf), dma(nf), dma(nf), dma(nf), dma(nd), dma(nd), dma(6),
        ],
        compiler_params=comm(1),
        name="spread",
        cost_estimate=pl.CostEstimate(flops=0, bytes_accessed=300 << 20, transcendentals=0),
    )(selc, queries.reshape(spans, SPAN, full_width), nbr_keys, nbr_values)
    qr = qg.reshape(refs_all, SPAN, width)

    o, st = pl.pallas_call(
        lambda *a: forward_kernel(nf, *a),
        in_specs=[SM, VM, VM, VM],
        out_specs=[VM, VM],
        out_shape=[
            jax.ShapeDtypeStruct((refs_all, SPAN, width), bf),
            jax.ShapeDtypeStruct((nd, SPAN, 128), f32),
        ],
        compiler_params=pltpu.CompilerParams(vmem_limit_bytes=BIG),
        name="forward",
    )(refs, qr, kt, vt)

    ug, hs, att = pl.pallas_call(
        lambda *a: meet_kernel(nd, nf, spans, *a),
        in_specs=[SM, SM, SM, VM, ANY, ANY],
        out_specs=[ANY, ANY, VM],
        out_shape=[
            jax.ShapeDtypeStruct((nd, nf, SPAN, width), bf),
            jax.ShapeDtypeStruct((nd, SPAN, 128), f32),
            jax.ShapeDtypeStruct((nf * spans, SPAN, width), bf),
        ],
        scratch_shapes=[
            pltpu.VMEM((nd, nf, SPAN, width), bf),
            pltpu.VMEM((nd, nf, SPAN, width), bf),
            pltpu.VMEM((nd, SPAN, 128), f32),
            pltpu.VMEM((SPAN, 128), f32),
            dma(nd), dma(nd), dma(nd), dma(nd), dma(nd), dma(nd), dma(nd), dma(nd), dma(4),
        ],
        compiler_params=comm(2),
        name="meet",
    )(selc, gsrc, count, upstream, o.reshape(nd, nf, SPAN, width), st)

    gathered = lax.all_gather(att.reshape(rows, width), "fsdp", axis=0, tiled=True)
    gathered = gathered.reshape(nf, rows, width)

    dq, dk, dv = pl.pallas_call(
        lambda *a: backward_kernel(nf, spans, *a),
        in_specs=[SM, VM, VM, VM, VM, VM],
        out_specs=[VM, VM, VM],
        out_shape=[
            jax.ShapeDtypeStruct((refs_all, SPAN, width), bf),
            jax.ShapeDtypeStruct((nf, nbrs, piece, width), bf),
            jax.ShapeDtypeStruct((nf, nbrs, piece, width), bf),
        ],
        scratch_shapes=[
            pltpu.VMEM((nbrs, nf * piece, width), f32),
            pltpu.VMEM((nbrs, nf * piece, width), f32),
        ],
        compiler_params=pltpu.CompilerParams(vmem_limit_bytes=BIG),
        name="backward",
        cost_estimate=pl.CostEstimate(flops=10 << 30, bytes_accessed=20 << 20, transcendentals=0),
    )(refs, qr, ug.reshape(refs_all, SPAN, width), hs, kt, vt)

    term = pl.pallas_call(
        project_kernel,
        grid=(nf,),
        in_specs=[
            pl.BlockSpec((1, rows, width), lambda f: (f, 0, 0)),
            pl.BlockSpec((rows, columns), lambda f: (0, 0), pipeline_mode=pl.Buffered(1)),
        ],
        out_specs=pl.BlockSpec((width, columns), lambda f: (f, 0)),
        out_shape=jax.ShapeDtypeStruct((full_width, columns), bf),
        name="project",
        cost_estimate=pl.CostEstimate(
            flops=2 * rows * columns * full_width, bytes_accessed=14 << 20, transcendentals=0
        ),
    )(gathered, cotangent)
    grad_proj = lax.psum(term, "dp")
    my_rows = lax.dynamic_slice_in_dim(
        gathered, lax.axis_index("fsdp") * token_rows, token_rows, axis=1
    )
    attended = jnp.transpose(my_rows, (1, 0, 2)).reshape(token_rows, full_width)

    gq, gk, gv = pl.pallas_call(
        lambda *a: return_kernel(nd, nf, width, spans, *a),
        in_specs=[SM, SM, ANY, ANY, ANY],
        out_specs=[ANY, ANY, ANY],
        out_shape=[
            jax.ShapeDtypeStruct((spans, SPAN, full_width), bf),
            jax.ShapeDtypeStruct((nbrs, piece, full_width), bf),
            jax.ShapeDtypeStruct((nbrs, piece, full_width), bf),
        ],
        scratch_shapes=[
            pltpu.VMEM((nd, nf, SPAN, width), bf),
            pltpu.VMEM((nf, spans, SPAN, width), bf),
            pltpu.VMEM((nbrs, piece, width), bf),
            pltpu.VMEM((nbrs, piece, width), bf),
            dma(nd), dma(nd), dma(nf), dma(nf), dma(nf), dma(nf), dma(nf), dma(nf), dma(6),
        ],
        compiler_params=comm(3),
        name="giveback",
        cost_estimate=pl.CostEstimate(flops=0, bytes_accessed=300 << 20, transcendentals=0),
    )(gsrc, count, dq.reshape(nd, nf, SPAN, width), dk, dv)
    return (attended, gq.reshape(token_rows, full_width), gk, gv, grad_proj)


def solution(mesh):
    placed = (
        P(("dp", "fsdp"), "enc"),
        P("dp", "fsdp", "enc"),
        P("dp", "fsdp", "enc"),
        P("enc", "fsdp"),
        P(),
        P(),
        P(),
        P("dp", "fsdp"),
    )
    return jax.shard_map(
        local,
        mesh=mesh,
        in_specs=placed,
        out_specs=(
            P(("dp", "fsdp"), "enc"),
            P(("dp", "fsdp"), "enc"),
            P("dp", "fsdp", "enc"),
            P("dp", "fsdp", "enc"),
            P("enc", "fsdp"),
        ),
        check_vma=False,
    )
```

```python
import math

import jax
import jax.numpy as jnp
from jax import lax
from jax.experimental import pallas as pl
from jax.experimental.pallas import tpu as pltpu
from jax.sharding import PartitionSpec as P

HEAD_DIM = 128
SPAN = 64
SLOTS = 2
MESH = pl.DeviceIdType.MESH
ANY = pl.BlockSpec(memory_space=pl.ANY)
VM = pl.BlockSpec(memory_space=pltpu.VMEM)
SM = pl.BlockSpec(memory_space=pltpu.SMEM)
NT = (((1,), (1,)), ((), ()))
TN = (((0,), (0,)), ((), ()))
NN = (((1,), (0,)), ((), ()))
SCALE = 1.0 / math.sqrt(HEAD_DIM)
BIG = 60 << 20


def dot(a, b, dims):
    return lax.dot_general(a, b, dims, preferred_element_type=jnp.float32)


def enter(axes):
    barrier = pltpu.get_barrier_semaphore()
    total = 0
    for axis, size in axes:
        here = lax.axis_index(axis)
        for step in range(1, size):
            pl.semaphore_signal(
                barrier, inc=1, device_id={axis: lax.rem(here + step, size)}, device_id_type=MESH
            )
            total += 1
    pl.semaphore_wait(barrier, total)


def remote(src, dst, send, recv, axis, peer):
    return pltpu.make_async_remote_copy(
        src_ref=src, dst_ref=dst, send_sem=send, recv_sem=recv, device_id={axis: peer}, device_id_type=MESH
    )


def cols(ref, place, width):
    return ref.at[:, :, pl.ds(pl.multiple_of(place * width, width), width)]


def spread_kernel(
    nd, nf, width, selc, q, k, v, cot, proj, kt, vt, qg, ug, u_out,
    q_heads, send, k_own, v_own, cot_vm, proj_vm, sib_send, sib_recv, mine, ring_send, ring_recv,
    qs, qr, ks, kr, vs, vr, gs, gr, us, ur, bs, br, rs, rr, own, load,
):
    dp, fs = lax.axis_index("dp"), lax.axis_index("fsdp")
    chips = nf // 2
    chip, core = fs // 2, lax.rem(fs, 2)
    sibling = chip * 2 + 1 - core
    spans = q_heads.shape[1]
    loads = [
        pltpu.make_async_copy(cot, cot_vm, load.at[0]),
        pltpu.make_async_copy(proj, proj_vm, load.at[1]),
    ]
    for copy in loads:
        copy.start()
    enter((("dp", nd), ("fsdp", nf)))
    q_own = pltpu.make_async_copy(cols(q, fs, width), q_heads.at[fs], own.at[0])
    q_own.start()

    def spread(ref, out, s_sem, r_sem):
        moves = []
        for step in range(1, nf):
            peer = lax.rem(fs + step, nf)
            move = remote(cols(ref, peer, width), out.at[fs], s_sem.at[step], r_sem.at[step], "fsdp", peer)
            move.start()
            moves.append(move)
        return moves

    q_moves = spread(q, q_heads, qs, qr)
    k_moves = spread(k, kt, ks, kr)
    takes = [
        pltpu.make_async_copy(cols(k, fs, width), k_own, own.at[1]),
        pltpu.make_async_copy(cols(v, fs, width), v_own, own.at[2]),
    ]
    for take in takes:
        take.start()
    for copy in loads:
        copy.wait()
    rows = cot_vm.shape[0]
    tile = 512
    sib_moves = []
    for step in range(chips):
        there = lax.rem(chip + step + 1, chips)
        for which in (1 - core, core):
            block = pl.multiple_of((there * 2 + which) * width, width)
            first = len(sib_moves) == step

            @pl.loop(0, rows // tile)
            def _(t):
                at = pl.multiple_of(t * tile, tile)
                value = dot(cot_vm[pl.ds(at, tile), :], proj_vm[pl.ds(block, width), :], NT)
                if first:
                    sib_send[step, pl.ds(at, tile), :] = value.astype(jnp.bfloat16)
                else:
                    mine[step, pl.ds(at, tile), :] = value

            if first:
                move = remote(sib_send.at[step], sib_recv.at[step], bs.at[step], br.at[step], "fsdp", sibling)
                move.start()
                sib_moves.append(move)
    ring_moves = []
    for step in range(chips - 1):
        there = lax.rem(chip + step + 1, chips)
        sib_moves[step].wait_recv()

        @pl.loop(0, rows // tile)
        def _(t):
            at = pl.ds(pl.multiple_of(t * tile, tile), tile)
            ring_send[step, at, :] = (
                mine[step, at, :] + sib_recv[step, at, :].astype(jnp.float32)
            ).astype(jnp.bfloat16)

        move = remote(
            ring_send.at[step], ring_recv.at[step], rs.at[step], rr.at[step], "fsdp", there * 2 + core
        )
        move.start()
        ring_moves.append(move)
    v_moves = spread(v, vt, vs, vr)
    for take in takes:
        take.wait()
    puts = [
        pltpu.make_async_copy(k_own, kt.at[fs], own.at[3]),
        pltpu.make_async_copy(v_own, vt.at[fs], own.at[4]),
    ]
    for put in puts:
        put.start()
    q_own.wait()
    for move in q_moves:
        move.wait_recv()

    def deliver(kind, source, out, s_sem, r_sem):
        @pl.loop(0, nd)
        def _(group):
            @pl.loop(0, nf)
            def _(home):
                send[kind, group, home] = source(home, selc[group, home])

        moves = []
        for step in range(1, nd):
            peer = lax.rem(dp + step, nd)
            move = remote(send.at[kind, peer], out.at[dp], s_sem.at[step], r_sem.at[step], "dp", peer)
            move.start()
            moves.append(move)
        put = pltpu.make_async_copy(send.at[kind, dp], out.at[dp], own.at[5 + kind])
        put.start()
        puts.append(put)
        return moves

    moves = deliver(0, lambda home, c: q_heads[home, c], qg, gs, gr)
    sib_moves[chips - 1].wait_recv()
    for move in ring_moves:
        move.wait_recv()

    @pl.loop(0, rows // SPAN)
    def _(i):
        at = pl.ds(pl.multiple_of(i * SPAN, SPAN), SPAN)
        value = mine[chips - 1, at, :] + sib_recv[chips - 1, at, :].astype(jnp.float32)
        for step in range(chips - 1):
            value += ring_recv[step, at, :].astype(jnp.float32)
        u_out[i] = value.astype(jnp.bfloat16)

    moves += deliver(1, lambda home, c: u_out[home * spans + c], ug, us, ur)
    for move in q_moves + sib_moves + ring_moves:
        move.wait_send()
    for move in k_moves + v_moves + moves:
        move.wait()
    for put in puts:
        put.wait()


UNROLL = 4


def forward_kernel(nf, refs, q, kt, vt, o_ref, st_ref):
    lane = lax.broadcasted_iota(jnp.int32, (SPAN, 128), 1)
    length = kt.shape[0] * kt.shape[2]

    @pl.loop(0, (refs[0] + UNROLL - 1) // UNROLL)
    def _(step):
        done = []
        for more in range(UNROLL):
            j = step * UNROLL + more
            r, n = refs[1 + 4 * j], refs[2 + 4 * j]
            keys = kt[:, n].reshape(length, -1)
            values = vt[:, n].reshape(length, -1)
            query = q[r]
            outs, marks = [], []
            for h in range(keys.shape[1] // HEAD_DIM):
                part = slice(h * HEAD_DIM, (h + 1) * HEAD_DIM)
                scores = dot(query[:, part], keys[:, part], NT) * SCALE
                peak = jnp.max(scores, axis=1, keepdims=True)
                expo = jnp.exp(scores - peak)
                total = jnp.sum(expo, axis=1, keepdims=True)
                outs.append(dot(expo.astype(jnp.bfloat16), values[:, part], NN).astype(jnp.bfloat16))
                marks += [peak, total]
            done.append((r, outs, marks))
        for r, outs, marks in done:
            o_ref[r] = jnp.concatenate(outs, axis=1)
            stats = st_ref[r // nf]
            for i, mark in enumerate(marks):
                stats = jnp.where(lane == 4 * (r % nf) + i, mark, stats)
            st_ref[r // nf] = stats


def meet_kernel(
    nd, nf, spans, gsrc, count, u, o, st, hs_out, att, o_home, st_home, hs, ss, sr, os, orr, hsn, hr, own,
):
    dp = lax.axis_index("dp")
    enter((("dp", nd),))
    own_copies = [
        pltpu.make_async_copy(st.at[dp], st_home.at[dp], own.at[0]),
        pltpu.make_async_copy(o.at[dp], o_home.at[dp], own.at[1]),
    ]
    for copy in own_copies:
        copy.start()
    peers = [lax.rem(dp + step, nd) for step in range(1, nd)]
    stats = [
        remote(st.at[p], st_home.at[dp], ss.at[i], sr.at[i], "dp", p) for i, p in enumerate(peers)
    ]
    outs = [
        remote(o.at[p], o_home.at[dp], os.at[i], orr.at[i], "dp", p) for i, p in enumerate(peers)
    ]
    for move in stats + outs:
        move.start()
    for copy in own_copies:
        copy.wait()
    for move in stats + outs:
        move.wait_recv()
    lane = lax.broadcasted_iota(jnp.int32, (SPAN, 128), 1)

    def pick(array, at):
        return jnp.sum(jnp.where(lane == at, array, 0.0), axis=1, keepdims=True)

    def combine(home, table):
        for c in range(spans):
            i = home * spans + c
            g0, g1 = gsrc[2 * i], gsrc[2 * i + 1]
            both = count[i] > 1
            s0, s1 = st_home[g0], st_home[g1]
            o0, o1 = o_home[g0, home].astype(jnp.float32), o_home[g1, home].astype(jnp.float32)
            mine = u[i].astype(jnp.float32)
            pieces = []
            for h in range(u.shape[2] // HEAD_DIM):
                part = slice(h * HEAD_DIM, (h + 1) * HEAD_DIM)
                at = 4 * home + 2 * h
                m0, l0 = pick(s0, at), pick(s0, at + 1)
                m1 = jnp.where(both, pick(s1, at), -1e30)
                l1 = jnp.where(both, pick(s1, at + 1), 0.0)
                peak = jnp.maximum(m0, m1)
                a0, a1 = jnp.exp(m0 - peak), jnp.exp(m1 - peak)
                total = a0 * l0 + a1 * l1
                piece = (a0 / total) * o0[:, part] + (a1 / total) * jnp.where(both, o1[:, part], 0.0)
                pieces.append(piece.astype(jnp.bfloat16))
                centre = jnp.sum(piece * mine[:, part], axis=1, keepdims=True)
                table = jnp.where(lane == 4 * i + h, peak + jnp.log(total), table)
                table = jnp.where(lane == 4 * i + 2 + h, centre, table)
            att[i] = jnp.concatenate(pieces, axis=1)
        return table

    hs[...] = lax.fori_loop(0, nf, combine, jnp.zeros((SPAN, 128), jnp.float32))
    gives = [
        remote(hs, hs_out.at[dp], hsn.at[i], hr.at[i], "dp", p) for i, p in enumerate(peers)
    ]
    for move in gives:
        move.start()
    hs_own = pltpu.make_async_copy(hs, hs_out.at[dp], own.at[2])
    hs_own.start()
    for move in stats + outs:
        move.wait_send()
    for move in gives:
        move.wait()
    hs_own.wait()


def backward_kernel(nf, spans, refs, q, u, hs, kt, vt, dq_ref, dk_ref, dv_ref, k_acc, v_acc):
    lane = lax.broadcasted_iota(jnp.int32, (SPAN, 128), 1)
    pieces, nbrs, piece = kt.shape[0], kt.shape[1], kt.shape[2]
    length = pieces * piece

    @pl.loop(0, nbrs)
    def _(n):
        k_acc[n] = jnp.zeros(k_acc.shape[1:], jnp.float32)
        v_acc[n] = jnp.zeros(v_acc.shape[1:], jnp.float32)

    def pick(array, at):
        return jnp.sum(jnp.where(lane == at, array, 0.0), axis=1, keepdims=True)

    @pl.loop(0, (refs[0] + UNROLL - 1) // UNROLL)
    def _(step):
        done = []
        for more in range(UNROLL):
            j = step * UNROLL + more
            r, n, c, into = (refs[1 + 4 * j + i] for i in range(4))
            keys = kt[:, n].reshape(length, -1)
            values = vt[:, n].reshape(length, -1)
            query, up, table = q[r], u[r], hs[r // nf]
            at = 4 * ((r % nf) * spans + c)
            dqs, dks, dvs = [], [], []
            for h in range(keys.shape[1] // HEAD_DIM):
                part = slice(h * HEAD_DIM, (h + 1) * HEAD_DIM)
                scores = dot(query[:, part], keys[:, part], NT) * SCALE
                probs = jnp.exp(scores - pick(table, at + h))
                dprobs = dot(up[:, part], values[:, part], NT)
                ds = (probs * (dprobs - pick(table, at + 2 + h)) * SCALE).astype(jnp.bfloat16)
                dqs.append(dot(ds, keys[:, part], NN).astype(jnp.bfloat16))
                dks.append(dot(ds, query[:, part], TN))
                dvs.append(dot(probs.astype(jnp.bfloat16), up[:, part], TN))
            done.append((r, into, dqs, dks, dvs))
        for r, into, dqs, dks, dvs in done:
            dq_ref[r] = jnp.concatenate(dqs, axis=1)
            k_acc[into] += jnp.concatenate(dks, axis=1)
            v_acc[into] += jnp.concatenate(dvs, axis=1)

    @pl.loop(0, nbrs)
    def _(n):
        dk_ref[:, n] = k_acc[n].reshape(pieces, piece, -1).astype(jnp.bfloat16)
        dv_ref[:, n] = v_acc[n].reshape(pieces, piece, -1).astype(jnp.bfloat16)


def return_kernel(
    nd, nf, width, spans, gsrc, count, att, cot, dq, dk, dv, gq, gk, gv, gp, att_all,
    dq_home, dq_sum, k_own, v_own, cot_vm, term, shares, total,
    qs, qr, ks, kr, vs, vr, ys, yr, fa, ga, ba, ca, ts, tr, ps, pr, own, load,
):
    dp, fs = lax.axis_index("dp"), lax.axis_index("fsdp")
    chips = nf // 2
    chip, core = fs // 2, lax.rem(fs, 2)
    sibling = chip * 2 + 1 - core
    load_cot = pltpu.make_async_copy(cot, cot_vm, load.at[0])
    load_cot.start()
    enter((("dp", nd), ("fsdp", nf)))
    peers = [lax.rem(dp + step, nd) for step in range(1, nd)]
    firsts = [
        pltpu.make_async_copy(att, att_all.at[fs], own.at[6]),
        pltpu.make_async_copy(dq.at[dp], dq_home.at[dp], own.at[0]),
        pltpu.make_async_copy(dk.at[fs], k_own, own.at[1]),
        pltpu.make_async_copy(dv.at[fs], v_own, own.at[2]),
    ]
    for copy in firsts:
        copy.start()
    backs = [
        remote(dq.at[p], dq_home.at[dp], qs.at[i], qr.at[i], "dp", p) for i, p in enumerate(peers)
    ]
    for move in backs:
        move.start()
    to_sibling = [remote(att, att_all.at[fs], fa.at[chips - 1], ga.at[chips - 1], "fsdp", sibling)]
    to_sibling[0].start()
    around = []
    for step in range(chips - 1):
        there = lax.rem(chip + step + 1, chips) * 2 + core
        move = remote(att, att_all.at[fs], ba.at[step], ca.at[step], "fsdp", there)
        move.start()
        around.append(move)
    moves = []
    for ref, out, s_sem, r_sem in ((dk, gk, ks, kr), (dv, gv, vs, vr)):
        for step in range(1, nf):
            peer = lax.rem(fs + step, nf)
            move = remote(ref.at[peer], cols(out, fs, width), s_sem.at[step], r_sem.at[step], "fsdp", peer)
            move.start()
            moves.append(move)
    for copy in firsts:
        copy.wait()
    puts = [
        pltpu.make_async_copy(k_own, cols(gk, fs, width), own.at[3]),
        pltpu.make_async_copy(v_own, cols(gv, fs, width), own.at[4]),
    ]
    for put in puts:
        put.start()
    load_cot.wait()
    share = width // nd
    columns = cot_vm.shape[1]
    tile = 256

    def add_dq():
        for move in backs:
            move.wait_recv()

        @pl.loop(0, nf)
        def _(home):
            for c in range(spans):
                i = home * spans + c
                d0 = dq_home[gsrc[2 * i], home].astype(jnp.float32)
                d1 = dq_home[gsrc[2 * i + 1], home].astype(jnp.float32)
                dq_sum[home, c] = (d0 + jnp.where(count[i] > 1, d1, 0.0)).astype(jnp.bfloat16)

        for step in range(1, nf):
            peer = lax.rem(fs + step, nf)
            move = remote(dq_sum.at[peer], cols(gq, fs, width), ys.at[step], yr.at[step], "fsdp", peer)
            move.start()
            moves.append(move)
        put = pltpu.make_async_copy(dq_sum.at[fs], cols(gq, fs, width), own.at[5])
        put.start()
        puts.append(put)

    scatters = []

    def project(turn, block):
        @pl.loop(0, columns // tile)
        def _(t):
            at = pl.ds(pl.multiple_of(t * tile, tile), tile)
            value = dot(att_all[block], cot_vm[:, at], TN).astype(jnp.bfloat16)
            term[turn, :, :, at] = value.reshape(nd, share, tile)

        sent = [
            remote(term.at[turn, p], shares.at[turn, i], ts.at[turn, i], tr.at[turn, i], "dp", p)
            for i, p in enumerate(peers)
        ]
        for move in sent:
            move.start()
        scatters.append((block, sent))

    def finish(turn):
        block, sent = scatters[turn]
        for move in sent:
            move.wait_recv()
        value = term[turn, dp].astype(jnp.float32)
        for i in range(nd - 1):
            value += shares[turn, i].astype(jnp.float32)
        total[turn] = value.astype(jnp.bfloat16)
        here = pl.ds(pl.multiple_of(block * width + dp * share, share), share)
        for i, p in enumerate(peers):
            move = remote(total.at[turn], gp.at[here], ps.at[turn, i], pr.at[turn, i], "dp", p)
            move.start()
            moves.append(move)
        put = pltpu.make_async_copy(total.at[turn], gp.at[here], load.at[1 + turn])
        put.start()
        puts.append(put)

    project(0, fs)
    to_sibling[0].wait_recv()
    project(1, sibling)
    turn = 2
    order = [0, chips - 2] + list(range(1, chips - 2))
    for step in order:
        back = lax.rem(chip + chips - step - 1, chips) * 2
        around[step].wait_recv()
        move = remote(
            att_all.at[back + core], att_all.at[back + core], fa.at[step], ga.at[step], "fsdp", sibling
        )
        move.start()
        to_sibling.append(move)
        project(turn, back + core)
        if turn == 2:
            add_dq()
        finish((turn - 2))
        move.wait_recv()
        project(turn + 1, back + 1 - core)
        finish((turn - 1))
        turn += 2
    for last in range(turn - 2, turn):
        finish(last)
    for move in backs + to_sibling + around:
        move.wait_send()
    for _, sent in scatters:
        for move in sent:
            move.wait_send()
    for move in moves:
        move.wait()
    for put in puts:
        put.wait()


def dma(*shape):
    return pltpu.SemaphoreType.DMA(shape)


def comm(number, mib=BIG):
    return pltpu.CompilerParams(collective_id=number, has_side_effects=True, vmem_limit_bytes=mib)


def local(queries, nbr_keys, nbr_values, out_proj, nbr_source, nbr_index, nbr_count, cotangent):
    nd, nf = lax.axis_size("dp"), lax.axis_size("fsdp")
    bf, f32, i32 = jnp.bfloat16, jnp.float32, jnp.int32
    token_rows, full_width = queries.shape
    spans = token_rows // SPAN
    nbrs, piece, _ = nbr_keys.shape
    width = full_width // nf
    rows, columns = cotangent.shape
    slots = SLOTS * spans
    refs_all = nd * nf
    me = lax.axis_index("dp")

    sources = nbr_source.reshape(nd, nf, slots)
    indices = nbr_index.reshape(nd, nf, slots)
    counts = nbr_count.reshape(nd, nf, spans)
    slot = jnp.arange(slots, dtype=i32)
    my_sources = lax.dynamic_index_in_dim(sources, me, 0, keepdims=False)
    my_counts = lax.dynamic_index_in_dim(counts, me, 0, keepdims=False)
    hit = my_sources[None] == jnp.arange(nd, dtype=i32)[:, None, None]
    selc = jnp.sum(jnp.where(hit, slot // SLOTS, 0), axis=2)
    gsrc = my_sources.reshape(-1)
    count = my_counts.reshape(-1)
    alive = jnp.logical_and(
        sources == me, (slot % SLOTS)[None, None] < jnp.repeat(counts, SLOTS, axis=2)
    ).reshape(refs_all, slots)
    live = jnp.any(alive, axis=1)
    nidx = jnp.sum(jnp.where(alive, indices.reshape(refs_all, slots), 0), axis=1)
    cidx = jnp.sum(jnp.where(alive, slot // SLOTS, 0), axis=1)
    ref_iota = jnp.arange(refs_all, dtype=i32)
    key = jnp.where(live, 0, refs_all) + ref_iota
    rank = jnp.sum(key[None, :] < key[:, None], axis=1)
    place = rank[None, :] == ref_iota[:, None]
    entry = jnp.stack([ref_iota, nidx, cidx, jnp.where(live, nidx, nbrs)], axis=1)
    listed = jnp.sum(jnp.where(place[:, :, None], entry[None], 0), axis=1)
    refs = jnp.concatenate([jnp.sum(live.astype(i32))[None], listed.reshape(-1)])

    chips = nf // 2
    kt, vt, qg, ug, upstream = pl.pallas_call(
        lambda *a: spread_kernel(nd, nf, width, *a),
        in_specs=[SM, ANY, ANY, ANY, ANY, ANY],
        out_specs=[ANY, ANY, ANY, ANY, VM],
        out_shape=[
            jax.ShapeDtypeStruct((nf, nbrs, piece, width), bf),
            jax.ShapeDtypeStruct((nf, nbrs, piece, width), bf),
            jax.ShapeDtypeStruct((nd, nf, SPAN, width), bf),
            jax.ShapeDtypeStruct((nd, nf, SPAN, width), bf),
            jax.ShapeDtypeStruct((nf * spans, SPAN, width), bf),
        ],
        scratch_shapes=[
            pltpu.VMEM((nf, spans, SPAN, width), bf),
            pltpu.VMEM((2, nd, nf, SPAN, width), bf),
            pltpu.VMEM((nbrs, piece, width), bf),
            pltpu.VMEM((nbrs, piece, width), bf),
            pltpu.VMEM((rows, columns), bf),
            pltpu.VMEM((full_width, columns), bf),
            pltpu.VMEM((chips, rows, width), bf),
            pltpu.VMEM((chips, rows, width), bf),
            pltpu.VMEM((chips, rows, width), f32),
            pltpu.VMEM((chips - 1, rows, width), bf),
            pltpu.VMEM((chips - 1, rows, width), bf),
            dma(nf), dma(nf), dma(nf), dma(nf), dma(nf), dma(nf), dma(nd), dma(nd), dma(nd), dma(nd),
            dma(chips), dma(chips), dma(chips), dma(chips), dma(7), dma(2),
        ],
        compiler_params=comm(1),
        name="spread",
    )(selc, queries.reshape(spans, SPAN, full_width), nbr_keys, nbr_values, cotangent, out_proj)
    qr = qg.reshape(refs_all, SPAN, width)

    o, st = pl.pallas_call(
        lambda *a: forward_kernel(nf, *a),
        in_specs=[SM, VM, VM, VM],
        out_specs=[VM, VM],
        out_shape=[
            jax.ShapeDtypeStruct((refs_all, SPAN, width), bf),
            jax.ShapeDtypeStruct((nd, SPAN, 128), f32),
        ],
        compiler_params=pltpu.CompilerParams(vmem_limit_bytes=BIG),
        name="forward",
    )(refs, qr, kt, vt)

    hs, att = pl.pallas_call(
        lambda *a: meet_kernel(nd, nf, spans, *a),
        in_specs=[SM, SM, VM, ANY, ANY],
        out_specs=[ANY, VM],
        out_shape=[
            jax.ShapeDtypeStruct((nd, SPAN, 128), f32),
            jax.ShapeDtypeStruct((nf * spans, SPAN, width), bf),
        ],
        scratch_shapes=[
            pltpu.VMEM((nd, nf, SPAN, width), bf),
            pltpu.VMEM((nd, SPAN, 128), f32),
            pltpu.VMEM((SPAN, 128), f32),
            dma(nd), dma(nd), dma(nd), dma(nd), dma(nd), dma(nd), dma(3),
        ],
        compiler_params=comm(2),
        name="meet",
    )(gsrc, count, upstream, o.reshape(nd, nf, SPAN, width), st)

    dq, dk, dv = pl.pallas_call(
        lambda *a: backward_kernel(nf, spans, *a),
        in_specs=[SM, VM, VM, VM, VM, VM],
        out_specs=[VM, VM, VM],
        out_shape=[
            jax.ShapeDtypeStruct((refs_all, SPAN, width), bf),
            jax.ShapeDtypeStruct((nf, nbrs, piece, width), bf),
            jax.ShapeDtypeStruct((nf, nbrs, piece, width), bf),
        ],
        scratch_shapes=[
            pltpu.VMEM((nbrs + 1, nf * piece, width), f32),
            pltpu.VMEM((nbrs + 1, nf * piece, width), f32),
        ],
        compiler_params=pltpu.CompilerParams(vmem_limit_bytes=BIG),
        name="backward",
    )(refs, qr, ug.reshape(refs_all, SPAN, width), hs, kt, vt)

    gq, gk, gv, grad_proj, gathered = pl.pallas_call(
        lambda *a: return_kernel(nd, nf, width, spans, *a),
        in_specs=[SM, SM, ANY, ANY, ANY, ANY, ANY],
        out_specs=[ANY, ANY, ANY, ANY, VM],
        out_shape=[
            jax.ShapeDtypeStruct((spans, SPAN, full_width), bf),
            jax.ShapeDtypeStruct((nbrs, piece, full_width), bf),
            jax.ShapeDtypeStruct((nbrs, piece, full_width), bf),
            jax.ShapeDtypeStruct((full_width, columns), bf),
            jax.ShapeDtypeStruct((nf, rows, width), bf),
        ],
        scratch_shapes=[
            pltpu.VMEM((nd, nf, SPAN, width), bf),
            pltpu.VMEM((nf, spans, SPAN, width), bf),
            pltpu.VMEM((nbrs, piece, width), bf),
            pltpu.VMEM((nbrs, piece, width), bf),
            pltpu.VMEM((rows, columns), bf),
            pltpu.VMEM((nf, nd, width // nd, columns), bf),
            pltpu.VMEM((nf, nd - 1, width // nd, columns), bf),
            pltpu.VMEM((nf, width // nd, columns), bf),
            dma(nd), dma(nd), dma(nf), dma(nf), dma(nf), dma(nf), dma(nf), dma(nf),
            dma(chips), dma(chips), dma(chips), dma(chips),
            dma(nf, nd), dma(nf, nd), dma(nf, nd), dma(nf, nd), dma(7), dma(1 + nf),
        ],
        compiler_params=comm(3),
        name="giveback",
    )(gsrc, count, att.reshape(rows, width), cotangent, dq.reshape(nd, nf, SPAN, width), dk, dv)
    my_rows = lax.dynamic_slice_in_dim(
        gathered, lax.axis_index("fsdp") * token_rows, token_rows, axis=1
    )
    attended = jnp.transpose(my_rows, (1, 0, 2)).reshape(token_rows, full_width)
    return (attended, gq.reshape(token_rows, full_width), gk, gv, grad_proj)


def solution(mesh):
    placed = (
        P(("dp", "fsdp"), "enc"),
        P("dp", "fsdp", "enc"),
        P("dp", "fsdp", "enc"),
        P("enc", "fsdp"),
        P(),
        P(),
        P(),
        P("dp", "fsdp"),
    )
    return jax.shard_map(
        local,
        mesh=mesh,
        in_specs=placed,
        out_specs=(
            P(("dp", "fsdp"), "enc"),
            P(("dp", "fsdp"), "enc"),
            P("dp", "fsdp", "enc"),
            P("dp", "fsdp", "enc"),
            P("enc", "fsdp"),
        ),
        check_vma=False,
    )
```

```python
import math

import jax
import jax.numpy as jnp
from jax import lax
from jax.experimental import pallas as pl
from jax.experimental.pallas import tpu as pltpu
from jax.sharding import PartitionSpec as P

HEAD_DIM = 128
SPAN = 64
SLOTS = 2
MESH = pl.DeviceIdType.MESH
ANY = pl.BlockSpec(memory_space=pl.ANY)
VM = pl.BlockSpec(memory_space=pltpu.VMEM)
SM = pl.BlockSpec(memory_space=pltpu.SMEM)
NT = (((1,), (1,)), ((), ()))
TN = (((0,), (0,)), ((), ()))
NN = (((1,), (0,)), ((), ()))
SCALE = 1.0 / math.sqrt(HEAD_DIM)
BIG = 60 << 20


def dot(a, b, dims):
    return lax.dot_general(a, b, dims, preferred_element_type=jnp.float32)


def enter(axes):
    barrier = pltpu.get_barrier_semaphore()
    total = 0
    for axis, size in axes:
        here = lax.axis_index(axis)
        for step in range(1, size):
            pl.semaphore_signal(
                barrier, inc=1, device_id={axis: lax.rem(here + step, size)}, device_id_type=MESH
            )
            total += 1
    pl.semaphore_wait(barrier, total)


def remote(src, dst, send, recv, axis, peer):
    return pltpu.make_async_remote_copy(
        src_ref=src, dst_ref=dst, send_sem=send, recv_sem=recv, device_id={axis: peer}, device_id_type=MESH
    )


def cols(ref, place, width):
    return ref.at[:, :, pl.ds(pl.multiple_of(place * width, width), width)]


def spread_kernel(
    nd, nf, width, src, idx, cnt, q, k, v, cot, proj, kt, vt, qg, ug, hs_out, tab,
    q_heads, send, kt_vm, vt_a, vt_b, qg_vm, ug_vm, u_vm, cot_vm, proj_vm, sib_send, sib_recv, mine, ring_send,
    ring_recv, probs, st, st_home, hs, sel,
    qs, qr, ks, kr, vs, vr, gs, gr, us, ur, bs, br, rs, rr, ss, sr, hsn, hr, own, load,
):
    dp, fs = lax.axis_index("dp"), lax.axis_index("fsdp")
    chips = nf // 2
    chip, core = fs // 2, lax.rem(fs, 2)
    sibling = chip * 2 + 1 - core
    spans = q_heads.shape[1]
    slots = SLOTS * spans
    heads = width // HEAD_DIM
    peers = [lax.rem(dp + step, nd) for step in range(1, nd)]
    loads = [
        pltpu.make_async_copy(cot, cot_vm, load.at[0]),
        pltpu.make_async_copy(proj, proj_vm, load.at[1]),
    ]
    for copy in loads:
        copy.start()
    enter((("dp", nd), ("fsdp", nf)))
    vt_vm = (vt_a, vt_b)

    def v_part(place, head):
        at = pl.multiple_of(place * width + head * HEAD_DIM, HEAD_DIM)
        return v.at[:, :, pl.ds(at, HEAD_DIM)]

    owns = [
        pltpu.make_async_copy(cols(q, fs, width), q_heads.at[fs], own.at[0]),
        pltpu.make_async_copy(cols(k, fs, width), kt_vm.at[fs], own.at[1]),
    ] + [
        pltpu.make_async_copy(v_part(fs, head), vt_vm[head].at[fs], own.at[(2, 11)[head]]) for head in range(heads)
    ]
    for copy in owns:
        copy.start()

    def spread(ref, out, s_sem, r_sem, head=None):
        moves = []
        for step in range(1, nf):
            peer = lax.rem(fs + step, nf)
            if head is None:
                source, target, place = cols(ref, peer, width), out.at[fs], step
            else:
                source, target = v_part(peer, head), vt_vm[head].at[fs]
                place = head * nf + step
            move = remote(source, target, s_sem.at[place], r_sem.at[place], "fsdp", peer)
            move.start()
            moves.append(move)
        return moves

    q_moves = spread(q, q_heads, qs, qr)
    k_moves = spread(k, kt_vm, ks, kr)
    for copy in loads:
        copy.wait()
    rows = cot_vm.shape[0]
    tile = 512
    sib_moves = []
    for step in range(chips):
        there = lax.rem(chip + step + 1, chips)
        for which in (1 - core, core):
            block = pl.multiple_of((there * 2 + which) * width, width)
            first = len(sib_moves) == step

            @pl.loop(0, rows // tile)
            def _(t):
                at = pl.multiple_of(t * tile, tile)
                value = dot(cot_vm[pl.ds(at, tile), :], proj_vm[pl.ds(block, width), :], NT)
                if first:
                    sib_send[step, pl.ds(at, tile), :] = value.astype(jnp.bfloat16)
                else:
                    mine[step, pl.ds(at, tile), :] = value

            if first:
                move = remote(sib_send.at[step], sib_recv.at[step], bs.at[step], br.at[step], "fsdp", sibling)
                move.start()
                sib_moves.append(move)
    ring_moves = []
    for step in range(chips - 1):
        there = lax.rem(chip + step + 1, chips)
        sib_moves[step].wait_recv()

        @pl.loop(0, rows // tile)
        def _(t):
            at = pl.ds(pl.multiple_of(t * tile, tile), tile)
            ring_send[step, at, :] = (
                mine[step, at, :] + sib_recv[step, at, :].astype(jnp.float32)
            ).astype(jnp.bfloat16)

        move = remote(
            ring_send.at[step], ring_recv.at[step], rs.at[step], rr.at[step], "fsdp", there * 2 + core
        )
        move.start()
        ring_moves.append(move)
    v_moves = [spread(v, None, vs, vr, head) for head in range(heads)]

    @pl.loop(0, nd)
    def _(group):
        @pl.loop(0, nf)
        def _(home):
            base = (dp * nf + home) * slots
            span = jnp.int32(0)
            for t in range(slots):
                span = jnp.where(src[base + t] == group, t // SLOTS, span)
            sel[group * nf + home] = span
            r = group * nf + home
            number, where, live = jnp.int32(0), jnp.int32(0), jnp.int32(0)
            for t in range(slots):
                hit = jnp.logical_and(
                    src[r * slots + t] == dp, t % SLOTS < cnt[r * spans + t // SLOTS]
                )
                number = jnp.where(hit, idx[r * slots + t], number)
                where = jnp.where(hit, t // SLOTS, where)
                live = jnp.where(hit, 1, live)
            tab[r] = number
            tab[nd * nf + r] = where
            tab[2 * nd * nf + r] = live

    owns[0].wait()
    for move in q_moves:
        move.wait_recv()
    puts = []

    def deliver(kind, source, out, s_sem, r_sem):
        @pl.loop(0, nd)
        def _(group):
            @pl.loop(0, nf)
            def _(home):
                send[kind, group, home] = source(home, sel[group * nf + home])

        moves = [
            remote(send.at[kind, p], out.at[dp], s_sem.at[i], r_sem.at[i], "dp", p)
            for i, p in enumerate(peers)
        ]
        for move in moves:
            move.start()
        put = pltpu.make_async_copy(send.at[kind, dp], out.at[dp], own.at[3 + kind])
        put.start()
        return moves, put

    def store(source, out, number):
        put = pltpu.make_async_copy(source, out, own.at[number])
        put.start()
        puts.append(put)

    q_there, q_put = deliver(0, lambda home, c: q_heads[home, c], qg_vm, gs, gr)
    q_put.wait()
    for move in q_there:
        move.wait_recv()
    owns[1].wait()
    for move in k_moves:
        move.wait_recv()
    store(qg_vm, qg, 5)
    store(kt_vm, kt, 6)
    lane = lax.broadcasted_iota(jnp.int32, (SPAN, 128), 1)
    length = kt_vm.shape[0] * kt_vm.shape[2]
    group_lanes = heads * nf

    @pl.loop(0, nd)
    def _(d):
        marks = jnp.zeros((SPAN, 128), jnp.float32)
        for f in range(nf):
            n = tab[d * nf + f]
            for h in range(heads):
                part = slice(h * HEAD_DIM, (h + 1) * HEAD_DIM)
                keys = kt_vm[:, n, :, part].reshape(length, HEAD_DIM)
                scores = dot(qg_vm[d, f, :, part], keys, NT) * SCALE
                peak = jnp.max(scores, axis=1, keepdims=True)
                expo = jnp.exp(scores - peak)
                probs[h, d * nf + f] = expo
                marks = jnp.where(lane == heads * f + h, peak, marks)
                total = jnp.sum(expo, axis=1, keepdims=True)
                marks = jnp.where(lane == group_lanes + heads * f + h, total, marks)
        st[d] = marks

    sib_moves[chips - 1].wait_recv()
    for move in ring_moves:
        move.wait_recv()

    @pl.loop(0, rows // SPAN)
    def _(i):
        at = pl.ds(pl.multiple_of(i * SPAN, SPAN), SPAN)
        value = mine[chips - 1, at, :] + sib_recv[chips - 1, at, :].astype(jnp.float32)
        for step in range(chips - 1):
            value += ring_recv[step, at, :].astype(jnp.float32)
        u_vm[i] = value.astype(jnp.bfloat16)

    u_there, u_put = deliver(1, lambda home, c: u_vm[home * spans + c], ug_vm, us, ur)
    u_put.wait()
    for move in u_there:
        move.wait_recv()
    store(ug_vm, ug, 7)
    for h in range(heads):
        owns[2 + h].wait()
        for move in v_moves[h]:
            move.wait_recv()
        part = slice(h * HEAD_DIM, (h + 1) * HEAD_DIM)

        @pl.loop(0, nd)
        def _(d):
            marks = st[d]
            for f in range(nf):
                n = tab[d * nf + f]
                values = vt_vm[h][:, n].reshape(length, HEAD_DIM)
                dprobs = dot(ug_vm[d, f, :, part], values, NT)
                mean = jnp.sum(probs[h, d * nf + f] * dprobs, axis=1, keepdims=True)
                marks = jnp.where(lane == 2 * group_lanes + heads * f + h, mean, marks)
            st[d] = marks

    for h in range(heads):
        store(vt_vm[h], vt.at[:, :, :, pl.ds(h * HEAD_DIM, HEAD_DIM)], 8 + 4 * h)
    stats = [
        remote(st.at[p], st_home.at[dp], ss.at[i], sr.at[i], "dp", p) for i, p in enumerate(peers)
    ]
    for move in stats:
        move.start()
    st_put = pltpu.make_async_copy(st.at[dp], st_home.at[dp], own.at[9])
    st_put.start()
    row = lax.broadcasted_iota(jnp.int32, (1, 128), 1)
    place = lax.rem(row, group_lanes) // heads
    sources = []
    both = []
    for t in range(slots):
        values = jnp.zeros((1, 128), jnp.int32)
        for f in range(nf):
            values = jnp.where(place == f, src[(dp * nf + f) * slots + t], values)
        sources.append(values)
    for c in range(spans):
        values = jnp.zeros((1, 128), jnp.int32)
        for f in range(nf):
            values = jnp.where(place == f, cnt[(dp * nf + f) * spans + c], values)
        both.append(values > 1)
    st_put.wait()
    for move in stats:
        move.wait_recv()
    table = jnp.zeros((SPAN, 128), jnp.float32)
    for c in range(spans):
        pair = []
        for slot in range(SLOTS):
            found = jnp.zeros((SPAN, 128), jnp.float32)
            for g in range(nd):
                found = jnp.where(sources[SLOTS * c + slot] == g, st_home[g], found)
            pair.append(
                [found] + [pltpu.roll(found, 128 - group_lanes * i, axis=1) for i in (1, 2)]
            )
        (m0, l0, e0), (m1, l1, e1) = pair
        m1 = jnp.where(both[c], m1, -1e30)
        l1, e1 = jnp.where(both[c], l1, 0.0), jnp.where(both[c], e1, 0.0)
        peak = jnp.maximum(m0, m1)
        a0, a1 = jnp.exp(m0 - peak), jnp.exp(m1 - peak)
        total = a0 * l0 + a1 * l1
        log_total = peak + jnp.log(total)
        centre = (a0 * e0 + a1 * e1) / total
        for value, at in ((log_total, c * group_lanes), (centre, 64 + c * group_lanes)):
            moved = pltpu.roll(value, at, axis=1) if at else value
            inside = jnp.logical_and(lane >= at, lane < at + group_lanes)
            table = jnp.where(inside, moved, table)
    hs[...] = table
    gives = [
        remote(hs, hs_out.at[dp], hsn.at[i], hr.at[i], "dp", p) for i, p in enumerate(peers)
    ]
    for move in gives:
        move.start()
    store(hs, hs_out.at[dp], 10)
    for move in q_moves + k_moves + sib_moves + ring_moves + q_there + u_there + stats + sum(v_moves, []):
        move.wait_send()
    for move in gives:
        move.wait()
    for put in puts:
        put.wait()


UNROLL = 4


def backward_kernel(nf, tab, q, u, hs, kt, vt, o_ref, dq_ref, dk_ref, dv_ref, k_acc, v_acc, listed):
    lane = lax.broadcasted_iota(jnp.int32, (SPAN, 128), 1)
    pieces, nbrs, piece = kt.shape[0], kt.shape[1], kt.shape[2]
    length = pieces * piece
    heads = kt.shape[3] // HEAD_DIM
    refs = q.shape[0]

    def place(r, ends):
        low, high = ends
        live = tab[2 * refs + r]
        listed[jnp.where(live > 0, low, high)] = r
        return low + live, high - 1 + live

    count, _ = lax.fori_loop(0, refs, place, (jnp.int32(0), jnp.int32(refs - 1)))

    @pl.loop(0, nbrs)
    def _(n):
        k_acc[n] = jnp.zeros(k_acc.shape[1:], jnp.float32)
        v_acc[n] = jnp.zeros(v_acc.shape[1:], jnp.float32)

    def pick(array, at):
        return jnp.sum(jnp.where(lane == at, array, 0.0), axis=1, keepdims=True)

    @pl.loop(0, (count + UNROLL - 1) // UNROLL)
    def _(step):
        done = []
        for more in range(UNROLL):
            r = listed[step * UNROLL + more]
            n, c, live = tab[r], tab[refs + r], tab[2 * refs + r]
            into = jnp.where(live > 0, n, nbrs)
            keys = kt[:, n].reshape(length, -1)
            values = vt[:, n].reshape(length, -1)
            query, up, table = q[r], u[r], hs[r // nf]
            at = heads * (nf * c + r % nf)
            outs, dqs, dks, dvs = [], [], [], []
            for h in range(heads):
                part = slice(h * HEAD_DIM, (h + 1) * HEAD_DIM)
                scores = dot(query[:, part], keys[:, part], NT) * SCALE
                probs = jnp.exp(scores - pick(table, at + h))
                rounded = probs.astype(jnp.bfloat16)
                dprobs = dot(up[:, part], values[:, part], NT)
                ds = (probs * (dprobs - pick(table, 64 + at + h)) * SCALE).astype(jnp.bfloat16)
                outs.append(dot(rounded, values[:, part], NN).astype(jnp.bfloat16))
                dqs.append(dot(ds, keys[:, part], NN).astype(jnp.bfloat16))
                dks.append(dot(ds, query[:, part], TN))
                dvs.append(dot(rounded, up[:, part], TN))
            done.append((r, into, outs, dqs, dks, dvs))
        for r, into, outs, dqs, dks, dvs in done:
            o_ref[r] = jnp.concatenate(outs, axis=1)
            dq_ref[r] = jnp.concatenate(dqs, axis=1)
            k_acc[into] += jnp.concatenate(dks, axis=1)
            v_acc[into] += jnp.concatenate(dvs, axis=1)

    @pl.loop(0, nbrs)
    def _(n):
        dk_ref[:, n] = k_acc[n].reshape(pieces, piece, -1).astype(jnp.bfloat16)
        dv_ref[:, n] = v_acc[n].reshape(pieces, piece, -1).astype(jnp.bfloat16)


def return_kernel(
    nd, nf, width, spans, src, cnt, o, cot, dq, dk, dv, ga_out, gq, gk, gv, gp, att_all,
    o_home, dq_home, dq_sum, k_own, v_own, cot_vm, term, shares, total,
    os, orr, qs, qr, ks, kr, vs, vr, ys, yr, fa, ga, ba, ca, ts, tr, ps, pr, own, load, last_sem,
):
    dp, fs = lax.axis_index("dp"), lax.axis_index("fsdp")
    chips = nf // 2
    chip, core = fs // 2, lax.rem(fs, 2)
    sibling = chip * 2 + 1 - core
    load_cot = pltpu.make_async_copy(cot, cot_vm, load.at[0])
    load_cot.start()
    enter((("dp", nd), ("fsdp", nf)))
    peers = [lax.rem(dp + step, nd) for step in range(1, nd)]
    firsts = [
        pltpu.make_async_copy(o.at[dp], o_home.at[dp], own.at[6]),
        pltpu.make_async_copy(dq.at[dp], dq_home.at[dp], own.at[0]),
        pltpu.make_async_copy(dk.at[fs], k_own, own.at[1]),
        pltpu.make_async_copy(dv.at[fs], v_own, own.at[2]),
    ]
    for copy in firsts:
        copy.start()
    outs = [
        remote(o.at[p], o_home.at[dp], os.at[i], orr.at[i], "dp", p) for i, p in enumerate(peers)
    ]
    backs = [
        remote(dq.at[p], dq_home.at[dp], qs.at[i], qr.at[i], "dp", p) for i, p in enumerate(peers)
    ]
    for move in outs + backs:
        move.start()
    moves = []

    def give(ref, out, s_sem, r_sem):
        for step in range(1, nf):
            peer = lax.rem(fs + step, nf)
            move = remote(ref.at[peer], cols(out, fs, width), s_sem.at[step], r_sem.at[step], "fsdp", peer)
            move.start()
            moves.append(move)

    give(dk, gk, ks, kr)
    for copy in firsts:
        copy.wait()
    puts = [
        pltpu.make_async_copy(k_own, cols(gk, fs, width), own.at[3]),
        pltpu.make_async_copy(v_own, cols(gv, fs, width), own.at[4]),
    ]
    for put in puts:
        put.start()

    def add_slots(home, c, parts):
        base = (dp * nf + home) * SLOTS * spans + SLOTS * c
        first = parts[src[base], home].astype(jnp.float32)
        second = parts[src[base + 1], home].astype(jnp.float32)
        both = cnt[(dp * nf + home) * spans + c] > 1
        return (first + jnp.where(both, second, 0.0)).astype(jnp.bfloat16)

    for move in outs:
        move.wait_recv()

    @pl.loop(0, nf)
    def _(home):
        for c in range(spans):
            at = pl.multiple_of((home * spans + c) * SPAN, SPAN)
            att_all[fs, pl.ds(at, SPAN), :] = add_slots(home, c, o_home)

    att = att_all.at[fs]
    to_sibling = [remote(att, att, fa.at[chips - 1], ga.at[chips - 1], "fsdp", sibling)]
    to_sibling[0].start()
    around = []
    for step in range(chips - 1):
        there = lax.rem(chip + step + 1, chips) * 2 + core
        move = remote(att, att, ba.at[step], ca.at[step], "fsdp", there)
        move.start()
        around.append(move)
    give(dv, gv, vs, vr)
    load_cot.wait()
    share = width // nd
    columns = cot_vm.shape[1]
    tile = 256

    def add_dq():
        for move in backs:
            move.wait_recv()

        @pl.loop(0, nf)
        def _(home):
            for c in range(spans):
                dq_sum[home, c] = add_slots(home, c, dq_home)

        for step in range(1, nf):
            peer = lax.rem(fs + step, nf)
            move = remote(dq_sum.at[peer], cols(gq, fs, width), ys.at[step], yr.at[step], "fsdp", peer)
            move.start()
            moves.append(move)
        put = pltpu.make_async_copy(dq_sum.at[fs], cols(gq, fs, width), own.at[5])
        put.start()
        puts.append(put)

    scatters = []

    def project(turn, block):
        @pl.loop(0, columns // tile)
        def _(t):
            at = pl.ds(pl.multiple_of(t * tile, tile), tile)
            value = dot(att_all[block], cot_vm[:, at], TN).astype(jnp.bfloat16)
            term[turn, :, :, at] = value.reshape(nd, share, tile)

        sent = [
            remote(term.at[turn, p], shares.at[turn, i], ts.at[turn, i], tr.at[turn, i], "dp", p)
            for i, p in enumerate(peers)
        ]
        for move in sent:
            move.start()
        scatters.append((block, sent))

    def finish(turn):
        block, sent = scatters[turn]
        for move in sent:
            move.wait_recv()
        value = term[turn, dp].astype(jnp.float32)
        for i in range(nd - 1):
            value += shares[turn, i].astype(jnp.float32)
        total[turn] = value.astype(jnp.bfloat16)
        here = pl.ds(pl.multiple_of(block * width + dp * share, share), share)
        for i, p in enumerate(peers):
            move = remote(total.at[turn], gp.at[here], ps.at[turn, i], pr.at[turn, i], "dp", p)
            move.start()
            moves.append(move)
        put = pltpu.make_async_copy(total.at[turn], gp.at[here], load.at[1 + turn])
        put.start()
        puts.append(put)

    project(0, fs)
    to_sibling[0].wait_recv()
    project(1, sibling)
    turn = 2
    order = [0, chips - 2] + list(range(1, chips - 2))
    for step in order:
        back = lax.rem(chip + chips - step - 1, chips) * 2
        around[step].wait_recv()
        move = remote(
            att_all.at[back + core], att_all.at[back + core], fa.at[step], ga.at[step], "fsdp", sibling
        )
        move.start()
        to_sibling.append(move)
        project(turn, back + core)
        if turn == 2:
            add_dq()
        finish((turn - 2))
        move.wait_recv()
        project(turn + 1, back + 1 - core)
        finish((turn - 1))
        turn += 2
    for last in range(turn - 2, turn):
        finish(last)
    tokens = spans * SPAN
    for block in range(nf):
        here = pl.ds(pl.multiple_of(fs * tokens, tokens), tokens)
        put = pltpu.make_async_copy(
            att_all.at[block, here], ga_out.at[:, pl.ds(block * width, width)], last_sem.at[block]
        )
        put.start()
        puts.append(put)
    for move in outs + backs + to_sibling + around:
        move.wait_send()
    for _, sent in scatters:
        for move in sent:
            move.wait_send()
    for move in moves:
        move.wait()
    for put in puts:
        put.wait()


def dma(*shape):
    return pltpu.SemaphoreType.DMA(shape)


def comm(number, mib=BIG):
    return pltpu.CompilerParams(collective_id=number, has_side_effects=True, vmem_limit_bytes=mib)


def local(queries, nbr_keys, nbr_values, out_proj, nbr_source, nbr_index, nbr_count, cotangent):
    nd, nf = lax.axis_size("dp"), lax.axis_size("fsdp")
    bf, f32, i32 = jnp.bfloat16, jnp.float32, jnp.int32
    token_rows, full_width = queries.shape
    spans = token_rows // SPAN
    nbrs, piece, _ = nbr_keys.shape
    width = full_width // nf
    rows, columns = cotangent.shape
    refs_all = nd * nf
    chips = nf // 2
    sources, indices = nbr_source.reshape(-1), nbr_index.reshape(-1)
    share = width // nd

    kt, vt, qg, ug, hs, tab = pl.pallas_call(
        lambda *a: spread_kernel(nd, nf, width, *a),
        in_specs=[SM, SM, SM, ANY, ANY, ANY, ANY, ANY],
        out_specs=[ANY, ANY, ANY, ANY, ANY, SM],
        out_shape=[
            jax.ShapeDtypeStruct((nf, nbrs, piece, width), bf),
            jax.ShapeDtypeStruct((nf, nbrs, piece, width), bf),
            jax.ShapeDtypeStruct((nd, nf, SPAN, width), bf),
            jax.ShapeDtypeStruct((nd, nf, SPAN, width), bf),
            jax.ShapeDtypeStruct((nd, SPAN, 128), f32),
            jax.ShapeDtypeStruct((3 * refs_all,), i32),
        ],
        scratch_shapes=[
            pltpu.VMEM((nf, spans, SPAN, width), bf),
            pltpu.VMEM((2, nd, nf, SPAN, width), bf),
            pltpu.VMEM((nf, nbrs, piece, width), bf),
            pltpu.VMEM((nf, nbrs, piece, HEAD_DIM), bf),
            pltpu.VMEM((nf, nbrs, piece, HEAD_DIM), bf),
            pltpu.VMEM((nd, nf, SPAN, width), bf),
            pltpu.VMEM((nd, nf, SPAN, width), bf),
            pltpu.VMEM((nf * spans, SPAN, width), bf),
            pltpu.VMEM((rows, columns), bf),
            pltpu.VMEM((full_width, columns), bf),
            pltpu.VMEM((chips, rows, width), bf),
            pltpu.VMEM((chips, rows, width), bf),
            pltpu.VMEM((chips, rows, width), f32),
            pltpu.VMEM((chips - 1, rows, width), bf),
            pltpu.VMEM((chips - 1, rows, width), bf),
            pltpu.VMEM((width // HEAD_DIM, refs_all, SPAN, nf * piece), f32),
            pltpu.VMEM((nd, SPAN, 128), f32),
            pltpu.VMEM((nd, SPAN, 128), f32),
            pltpu.VMEM((SPAN, 128), f32),
            pltpu.SMEM((refs_all,), i32),
            dma(nf), dma(nf), dma(nf), dma(nf), dma(2 * nf), dma(2 * nf), dma(nd), dma(nd), dma(nd), dma(nd),
            dma(chips), dma(chips), dma(chips), dma(chips), dma(nd), dma(nd), dma(nd), dma(nd), dma(13), dma(2),
        ],
        compiler_params=comm(1),
        name="spread",
    )(
        sources, indices, nbr_count, queries.reshape(spans, SPAN, full_width), nbr_keys, nbr_values,
        cotangent, out_proj,
    )

    o, dq, dk, dv = pl.pallas_call(
        lambda *a: backward_kernel(nf, *a),
        in_specs=[SM, VM, VM, VM, VM, VM],
        out_specs=[VM, VM, VM, VM],
        out_shape=[
            jax.ShapeDtypeStruct((refs_all, SPAN, width), bf),
            jax.ShapeDtypeStruct((refs_all, SPAN, width), bf),
            jax.ShapeDtypeStruct((nf, nbrs, piece, width), bf),
            jax.ShapeDtypeStruct((nf, nbrs, piece, width), bf),
        ],
        scratch_shapes=[
            pltpu.VMEM((nbrs + 1, nf * piece, width), f32),
            pltpu.VMEM((nbrs + 1, nf * piece, width), f32),
            pltpu.SMEM((refs_all,), i32),
        ],
        compiler_params=pltpu.CompilerParams(vmem_limit_bytes=BIG),
        name="backward",
    )(tab, qg.reshape(refs_all, SPAN, width), ug.reshape(refs_all, SPAN, width), hs, kt, vt)

    attended, gq, gk, gv, grad_proj = pl.pallas_call(
        lambda *a: return_kernel(nd, nf, width, spans, *a),
        in_specs=[SM, SM, ANY, ANY, ANY, ANY, ANY],
        out_specs=[ANY, ANY, ANY, ANY, ANY],
        out_shape=[
            jax.ShapeDtypeStruct((token_rows, full_width), bf),
            jax.ShapeDtypeStruct((spans, SPAN, full_width), bf),
            jax.ShapeDtypeStruct((nbrs, piece, full_width), bf),
            jax.ShapeDtypeStruct((nbrs, piece, full_width), bf),
            jax.ShapeDtypeStruct((full_width, columns), bf),
        ],
        scratch_shapes=[
            pltpu.VMEM((nf, rows, width), bf),
            pltpu.VMEM((nd, nf, SPAN, width), bf),
            pltpu.VMEM((nd, nf, SPAN, width), bf),
            pltpu.VMEM((nf, spans, SPAN, width), bf),
            pltpu.VMEM((nbrs, piece, width), bf),
            pltpu.VMEM((nbrs, piece, width), bf),
            pltpu.VMEM((rows, columns), bf),
            pltpu.VMEM((nf, nd, share, columns), bf),
            pltpu.VMEM((nf, nd - 1, share, columns), bf),
            pltpu.VMEM((nf, share, columns), bf),
            dma(nd), dma(nd), dma(nd), dma(nd), dma(nf), dma(nf), dma(nf), dma(nf), dma(nf), dma(nf),
            dma(chips), dma(chips), dma(chips), dma(chips),
            dma(nf, nd), dma(nf, nd), dma(nf, nd), dma(nf, nd), dma(7), dma(1 + nf), dma(nf),
        ],
        compiler_params=comm(3),
        name="giveback",
    )(
        sources, nbr_count, o.reshape(nd, nf, SPAN, width), cotangent,
        dq.reshape(nd, nf, SPAN, width), dk, dv,
    )
    return (attended, gq.reshape(token_rows, full_width), gk, gv, grad_proj)


def solution(mesh):
    placed = (
        P(("dp", "fsdp"), "enc"),
        P("dp", "fsdp", "enc"),
        P("dp", "fsdp", "enc"),
        P("enc", "fsdp"),
        P(),
        P(),
        P(),
        P("dp", "fsdp"),
    )
    return jax.shard_map(
        local,
        mesh=mesh,
        in_specs=placed,
        out_specs=(
            P(("dp", "fsdp"), "enc"),
            P(("dp", "fsdp"), "enc"),
            P("dp", "fsdp", "enc"),
            P("dp", "fsdp", "enc"),
            P("enc", "fsdp"),
        ),
        check_vma=False,
    )
```

```python
import math

import jax
import jax.numpy as jnp
from jax import lax
from jax.experimental import pallas as pl
from jax.experimental.pallas import tpu as pltpu
from jax.sharding import PartitionSpec as P

HEAD_DIM = 128
SPAN = 64
SLOTS = 2
MESH = pl.DeviceIdType.MESH
ANY = pl.BlockSpec(memory_space=pl.ANY)
VM = pl.BlockSpec(memory_space=pltpu.VMEM)
SM = pl.BlockSpec(memory_space=pltpu.SMEM)
NT = (((1,), (1,)), ((), ()))
TN = (((0,), (0,)), ((), ()))
NN = (((1,), (0,)), ((), ()))
SCALE = 1.0 / math.sqrt(HEAD_DIM)
BIG = 60 << 20


def dot(a, b, dims):
    return lax.dot_general(a, b, dims, preferred_element_type=jnp.float32)


def enter(axes):
    barrier = pltpu.get_barrier_semaphore()
    total = 0
    for axis, size in axes:
        here = lax.axis_index(axis)
        for step in range(1, size):
            pl.semaphore_signal(
                barrier, inc=1, device_id={axis: lax.rem(here + step, size)}, device_id_type=MESH
            )
            total += 1
    pl.semaphore_wait(barrier, total)


def remote(src, dst, send, recv, axis, peer):
    return pltpu.make_async_remote_copy(
        src_ref=src, dst_ref=dst, send_sem=send, recv_sem=recv, device_id={axis: peer}, device_id_type=MESH
    )


def cols(ref, place, width):
    return ref.at[:, :, pl.ds(pl.multiple_of(place * width, width), width)]


def spread_kernel(
    nd, nf, width, src, idx, cnt, q, k, v, cot, proj, kt, vt, qg, ug, hs_out, tab,
    q_heads, send, kt_vm, vt_a, vt_b, qg_vm, ug_vm, u_vm, cot_vm, proj_vm, sib_send, sib_recv, mine, ring_send,
    ring_recv, probs, st, st_home, hs, sel,
    qs, qr, ks, kr, vs, vr, gs, gr, us, ur, bs, br, rs, rr, ss, sr, hsn, hr, own, load,
):
    dp, fs = lax.axis_index("dp"), lax.axis_index("fsdp")
    chips = nf // 2
    chip, core = fs // 2, lax.rem(fs, 2)
    sibling = chip * 2 + 1 - core
    spans = q_heads.shape[1]
    slots = SLOTS * spans
    heads = width // HEAD_DIM
    peers = [lax.rem(dp + step, nd) for step in range(1, nd)]
    loads = [
        pltpu.make_async_copy(cot, cot_vm, load.at[0]),
        pltpu.make_async_copy(proj, proj_vm, load.at[1]),
    ]
    for copy in loads:
        copy.start()
    enter((("dp", nd), ("fsdp", nf)))
    vt_vm = (vt_a, vt_b)

    def v_part(place, head):
        at = pl.multiple_of(place * width + head * HEAD_DIM, HEAD_DIM)
        return v.at[:, :, pl.ds(at, HEAD_DIM)]

    owns = [
        pltpu.make_async_copy(cols(q, fs, width), q_heads.at[fs], own.at[0]),
        pltpu.make_async_copy(cols(k, fs, width), kt_vm.at[fs], own.at[1]),
    ] + [
        pltpu.make_async_copy(v_part(fs, head), vt_vm[head].at[fs], own.at[(2, 11)[head]]) for head in range(heads)
    ]
    for copy in owns:
        copy.start()

    def spread(ref, out, s_sem, r_sem, head=None):
        moves = []
        for step in range(1, nf):
            peer = lax.rem(fs + step, nf)
            if head is None:
                source, target, place = cols(ref, peer, width), out.at[fs], step
            else:
                source, target = v_part(peer, head), vt_vm[head].at[fs]
                place = head * nf + step
            move = remote(source, target, s_sem.at[place], r_sem.at[place], "fsdp", peer)
            move.start()
            moves.append(move)
        return moves

    q_moves = spread(q, q_heads, qs, qr)
    k_moves = spread(k, kt_vm, ks, kr)
    for copy in loads:
        copy.wait()
    rows = cot_vm.shape[0]
    tile = 512
    sib_moves = []
    for step in range(chips):
        there = lax.rem(chip + step + 1, chips)
        for which in (1 - core, core):
            block = pl.multiple_of((there * 2 + which) * width, width)
            first = len(sib_moves) == step

            @pl.loop(0, rows // tile)
            def _(t):
                at = pl.multiple_of(t * tile, tile)
                value = dot(cot_vm[pl.ds(at, tile), :], proj_vm[pl.ds(block, width), :], NT)
                if first:
                    sib_send[step, pl.ds(at, tile), :] = value.astype(jnp.bfloat16)
                else:
                    mine[step, pl.ds(at, tile), :] = value

            if first:
                move = remote(sib_send.at[step], sib_recv.at[step], bs.at[step], br.at[step], "fsdp", sibling)
                move.start()
                sib_moves.append(move)
    ring_moves = []
    for step in range(chips - 1):
        there = lax.rem(chip + step + 1, chips)
        sib_moves[step].wait_recv()

        @pl.loop(0, rows // tile)
        def _(t):
            at = pl.ds(pl.multiple_of(t * tile, tile), tile)
            ring_send[step, at, :] = (
                mine[step, at, :] + sib_recv[step, at, :].astype(jnp.float32)
            ).astype(jnp.bfloat16)

        move = remote(
            ring_send.at[step], ring_recv.at[step], rs.at[step], rr.at[step], "fsdp", there * 2 + core
        )
        move.start()
        ring_moves.append(move)
    v_moves = [spread(v, None, vs, vr, head) for head in range(heads)]

    @pl.loop(0, nd)
    def _(group):
        @pl.loop(0, nf)
        def _(home):
            base = (dp * nf + home) * spans
            span = jnp.int32(0)
            for t in range(slots):
                span = jnp.where(src[t % SLOTS, base + t // SLOTS] == group, t // SLOTS, span)
            sel[group * nf + home] = span
            r = group * nf + home
            number, where, live = jnp.int32(0), jnp.int32(0), jnp.int32(0)
            for t in range(slots):
                hit = jnp.logical_and(
                    src[t % SLOTS, r * spans + t // SLOTS] == dp,
                    t % SLOTS < cnt[r * spans + t // SLOTS],
                )
                number = jnp.where(hit, idx[t % SLOTS, r * spans + t // SLOTS], number)
                where = jnp.where(hit, t // SLOTS, where)
                live = jnp.where(hit, 1, live)
            tab[r] = number
            tab[nd * nf + r] = where
            tab[2 * nd * nf + r] = live

    owns[0].wait()
    for move in q_moves:
        move.wait_recv()
    puts = []

    def deliver(kind, source, out, s_sem, r_sem):
        @pl.loop(0, nd)
        def _(group):
            @pl.loop(0, nf)
            def _(home):
                send[kind, group, home] = source(home, sel[group * nf + home])

        moves = [
            remote(send.at[kind, p], out.at[dp], s_sem.at[i], r_sem.at[i], "dp", p)
            for i, p in enumerate(peers)
        ]
        for move in moves:
            move.start()
        put = pltpu.make_async_copy(send.at[kind, dp], out.at[dp], own.at[3 + kind])
        put.start()
        return moves, put

    def store(source, out, number):
        put = pltpu.make_async_copy(source, out, own.at[number])
        put.start()
        puts.append(put)

    q_there, q_put = deliver(0, lambda home, c: q_heads[home, c], qg_vm, gs, gr)
    q_put.wait()
    for move in q_there:
        move.wait_recv()
    owns[1].wait()
    for move in k_moves:
        move.wait_recv()
    store(qg_vm, qg, 5)
    store(kt_vm, kt, 6)
    lane = lax.broadcasted_iota(jnp.int32, (SPAN, 128), 1)
    length = kt_vm.shape[0] * kt_vm.shape[2]
    group_lanes = heads * nf

    @pl.loop(0, nd)
    def _(d):
        marks = jnp.zeros((SPAN, 128), jnp.float32)
        for f in range(nf):
            n = tab[d * nf + f]
            for h in range(heads):
                part = slice(h * HEAD_DIM, (h + 1) * HEAD_DIM)
                keys = kt_vm[:, n, :, part].reshape(length, HEAD_DIM)
                scores = dot(qg_vm[d, f, :, part], keys, NT) * SCALE
                peak = jnp.max(scores, axis=1, keepdims=True)
                expo = jnp.exp(scores - peak)
                probs[h, d * nf + f] = expo
                marks = jnp.where(lane == heads * f + h, peak, marks)
                total = jnp.sum(expo, axis=1, keepdims=True)
                marks = jnp.where(lane == group_lanes + heads * f + h, total, marks)
        st[d] = marks

    sib_moves[chips - 1].wait_recv()
    for move in ring_moves:
        move.wait_recv()

    @pl.loop(0, rows // SPAN)
    def _(i):
        at = pl.ds(pl.multiple_of(i * SPAN, SPAN), SPAN)
        value = mine[chips - 1, at, :] + sib_recv[chips - 1, at, :].astype(jnp.float32)
        for step in range(chips - 1):
            value += ring_recv[step, at, :].astype(jnp.float32)
        u_vm[i] = value.astype(jnp.bfloat16)

    u_there, u_put = deliver(1, lambda home, c: u_vm[home * spans + c], ug_vm, us, ur)
    u_put.wait()
    for move in u_there:
        move.wait_recv()
    store(ug_vm, ug, 7)
    for h in range(heads):
        owns[2 + h].wait()
        for move in v_moves[h]:
            move.wait_recv()
        part = slice(h * HEAD_DIM, (h + 1) * HEAD_DIM)

        @pl.loop(0, nd)
        def _(d):
            marks = st[d]
            for f in range(nf):
                n = tab[d * nf + f]
                values = vt_vm[h][:, n].reshape(length, HEAD_DIM)
                dprobs = dot(ug_vm[d, f, :, part], values, NT)
                mean = jnp.sum(probs[h, d * nf + f] * dprobs, axis=1, keepdims=True)
                marks = jnp.where(lane == 2 * group_lanes + heads * f + h, mean, marks)
            st[d] = marks

    for h in range(heads):
        store(vt_vm[h], vt.at[:, :, :, pl.ds(h * HEAD_DIM, HEAD_DIM)], 8 + 4 * h)
    stats = [
        remote(st.at[p], st_home.at[dp], ss.at[i], sr.at[i], "dp", p) for i, p in enumerate(peers)
    ]
    for move in stats:
        move.start()
    st_put = pltpu.make_async_copy(st.at[dp], st_home.at[dp], own.at[9])
    st_put.start()
    row = lax.broadcasted_iota(jnp.int32, (1, 128), 1)
    place = lax.rem(row, group_lanes) // heads
    sources = []
    both = []
    for t in range(slots):
        values = jnp.zeros((1, 128), jnp.int32)
        for f in range(nf):
            values = jnp.where(place == f, src[t % SLOTS, (dp * nf + f) * spans + t // SLOTS], values)
        sources.append(values)
    for c in range(spans):
        values = jnp.zeros((1, 128), jnp.int32)
        for f in range(nf):
            values = jnp.where(place == f, cnt[(dp * nf + f) * spans + c], values)
        both.append(values > 1)
    st_put.wait()
    for move in stats:
        move.wait_recv()
    table = jnp.zeros((SPAN, 128), jnp.float32)
    for c in range(spans):
        pair = []
        for slot in range(SLOTS):
            found = jnp.zeros((SPAN, 128), jnp.float32)
            for g in range(nd):
                found = jnp.where(sources[SLOTS * c + slot] == g, st_home[g], found)
            pair.append(
                [found] + [pltpu.roll(found, 128 - group_lanes * i, axis=1) for i in (1, 2)]
            )
        (m0, l0, e0), (m1, l1, e1) = pair
        m1 = jnp.where(both[c], m1, -1e30)
        l1, e1 = jnp.where(both[c], l1, 0.0), jnp.where(both[c], e1, 0.0)
        peak = jnp.maximum(m0, m1)
        a0, a1 = jnp.exp(m0 - peak), jnp.exp(m1 - peak)
        total = a0 * l0 + a1 * l1
        log_total = peak + jnp.log(total)
        centre = (a0 * e0 + a1 * e1) / total
        for value, at in ((log_total, c * group_lanes), (centre, 64 + c * group_lanes)):
            moved = pltpu.roll(value, at, axis=1) if at else value
            inside = jnp.logical_and(lane >= at, lane < at + group_lanes)
            table = jnp.where(inside, moved, table)
    hs[...] = table
    gives = [
        remote(hs, hs_out.at[dp], hsn.at[i], hr.at[i], "dp", p) for i, p in enumerate(peers)
    ]
    for move in gives:
        move.start()
    store(hs, hs_out.at[dp], 10)
    for move in q_moves + k_moves + sib_moves + ring_moves + q_there + u_there + stats + sum(v_moves, []):
        move.wait_send()
    for move in gives:
        move.wait()
    for put in puts:
        put.wait()


UNROLL = 4


def backward_kernel(
    nf, tab, q_any, u_any, hs_any, kt_any, vt_any, o_any, dq_any, dk_any, dv_any,
    q, u, hs, kt, vt, o_ref, dq_ref, dk_ref, dv_ref, k_acc, v_acc, listed, sems,
):
    pairs = ((q_any, q), (u_any, u), (hs_any, hs), (kt_any, kt), (vt_any, vt))
    loads = [pltpu.make_async_copy(a, b, sems.at[i]) for i, (a, b) in enumerate(pairs)]
    for copy in loads:
        copy.start()
    lane = lax.broadcasted_iota(jnp.int32, (SPAN, 128), 1)
    pieces, nbrs, piece = kt.shape[0], kt.shape[1], kt.shape[2]
    length = pieces * piece
    heads = kt.shape[3] // HEAD_DIM
    refs = q.shape[0]

    def place(r, ends):
        low, high = ends
        live = tab[2 * refs + r]
        listed[jnp.where(live > 0, low, high)] = r
        return low + live, high - 1 + live

    count, _ = lax.fori_loop(0, refs, place, (jnp.int32(0), jnp.int32(refs - 1)))

    @pl.loop(0, nbrs)
    def _(n):
        k_acc[n] = jnp.zeros(k_acc.shape[1:], jnp.float32)
        v_acc[n] = jnp.zeros(v_acc.shape[1:], jnp.float32)

    for copy in loads:
        copy.wait()

    def pick(array, at):
        return jnp.sum(jnp.where(lane == at, array, 0.0), axis=1, keepdims=True)

    @pl.loop(0, (count + UNROLL - 1) // UNROLL)
    def _(step):
        done = []
        for more in range(UNROLL):
            r = listed[step * UNROLL + more]
            n, c, live = tab[r], tab[refs + r], tab[2 * refs + r]
            into = jnp.where(live > 0, n, nbrs)
            keys = kt[:, n].reshape(length, -1)
            values = vt[:, n].reshape(length, -1)
            query, up, table = q[r], u[r], hs[r // nf]
            at = heads * (nf * c + r % nf)
            outs, dqs, dks, dvs = [], [], [], []
            for h in range(heads):
                part = slice(h * HEAD_DIM, (h + 1) * HEAD_DIM)
                scores = dot(query[:, part], keys[:, part], NT) * SCALE
                probs = jnp.exp(scores - pick(table, at + h))
                rounded = probs.astype(jnp.bfloat16)
                dprobs = dot(up[:, part], values[:, part], NT)
                ds = (probs * (dprobs - pick(table, 64 + at + h)) * SCALE).astype(jnp.bfloat16)
                outs.append(dot(rounded, values[:, part], NN).astype(jnp.bfloat16))
                dqs.append(dot(ds, keys[:, part], NN).astype(jnp.bfloat16))
                dks.append(dot(ds, query[:, part], TN))
                dvs.append(dot(rounded, up[:, part], TN))
            done.append((r, into, outs, dqs, dks, dvs))
        for r, into, outs, dqs, dks, dvs in done:
            o_ref[r] = jnp.concatenate(outs, axis=1)
            dq_ref[r] = jnp.concatenate(dqs, axis=1)
            k_acc[into] += jnp.concatenate(dks, axis=1)
            v_acc[into] += jnp.concatenate(dvs, axis=1)

    puts = [
        pltpu.make_async_copy(o_ref, o_any, sems.at[5]),
        pltpu.make_async_copy(dq_ref, dq_any, sems.at[6]),
    ]
    for put in puts:
        put.start()
    for i, (acc, out, put_to) in enumerate(((k_acc, dk_ref, dk_any), (v_acc, dv_ref, dv_any))):
        @pl.loop(0, nbrs)
        def _(n):
            out[:, n] = acc[n].reshape(pieces, piece, -1).astype(jnp.bfloat16)

        put = pltpu.make_async_copy(out, put_to, sems.at[7 + i])
        put.start()
        puts.append(put)
    for put in puts:
        put.wait()


def finish_kernel(*refs):
    count = len(refs) // 3
    sems = refs[-1]
    takes = []
    for i in range(count):
        source, held = refs[i], refs[2 * count + i]
        pieces = 4 if source.shape[0] % 4 == 0 else 1
        size = source.shape[0] // pieces
        for j in range(pieces):
            part = pl.ds(j * size, size)
            take = pltpu.make_async_copy(source.at[part], held.at[part], sems.at[0, i, j])
            take.start()
            takes.append((i, j, part, take))
    puts = []
    for i, j, part, take in takes:
        take.wait()
        put = pltpu.make_async_copy(refs[2 * count + i].at[part], refs[count + i].at[part], sems.at[1, i, j])
        put.start()
        puts.append(put)
    for put in puts:
        put.wait()


def return_kernel(
    nd, nf, width, spans, src, cnt, o, cot, dq, dk, dv, ga_out, gq, gk, gv, gp, att_all,
    o_home, dq_home, dq_sum, k_own, v_own, cot_vm, term, first_z, first_x, second, middle, keep, total,
    os, orr, qs, qr, ks, kr, vs, vr, ys, yr, fa, ga, ba, ca, ts, tr, own, load, last_sem,
):
    dp, fs = lax.axis_index("dp"), lax.axis_index("fsdp")
    chips = nf // 2
    chip, core = fs // 2, lax.rem(fs, 2)
    sibling = chip * 2 + 1 - core
    load_cot = pltpu.make_async_copy(cot, cot_vm, load.at[0])
    load_cot.start()
    enter((("dp", nd), ("fsdp", nf)))
    peers = [lax.rem(dp + step, nd) for step in range(1, nd)]
    firsts = [
        pltpu.make_async_copy(o.at[dp], o_home.at[dp], own.at[6]),
        pltpu.make_async_copy(dq.at[dp], dq_home.at[dp], own.at[0]),
        pltpu.make_async_copy(dk.at[fs], k_own, own.at[1]),
        pltpu.make_async_copy(dv.at[fs], v_own, own.at[2]),
    ]
    for copy in firsts:
        copy.start()
    outs = [
        remote(o.at[p], o_home.at[dp], os.at[i], orr.at[i], "dp", p) for i, p in enumerate(peers)
    ]
    backs = [
        remote(dq.at[p], dq_home.at[dp], qs.at[i], qr.at[i], "dp", p) for i, p in enumerate(peers)
    ]
    for move in outs:
        move.start()
    moves = []

    def give(ref, out, s_sem, r_sem):
        for step in range(1, nf):
            peer = lax.rem(fs + step, nf)
            move = remote(ref.at[peer], cols(out, fs, width), s_sem.at[step], r_sem.at[step], "fsdp", peer)
            move.start()
            moves.append(move)

    give(dk, gk, ks, kr)
    for copy in firsts:
        copy.wait()
    puts = [
        pltpu.make_async_copy(k_own, cols(gk, fs, width), own.at[3]),
        pltpu.make_async_copy(v_own, cols(gv, fs, width), own.at[4]),
    ]
    for put in puts:
        put.start()

    def add_slots(home, c, parts):
        span = (dp * nf + home) * spans + c
        first = parts[src[0, span], home].astype(jnp.float32)
        second = parts[src[1, span], home].astype(jnp.float32)
        both = cnt[span] > 1
        return (first + jnp.where(both, second, 0.0)).astype(jnp.bfloat16)

    for move in outs:
        move.wait_recv()

    @pl.loop(0, nf)
    def _(home):
        for c in range(spans):
            at = pl.multiple_of((home * spans + c) * SPAN, SPAN)
            att_all[fs, pl.ds(at, SPAN), :] = add_slots(home, c, o_home)

    att = att_all.at[fs]
    to_sibling = [remote(att, att, fa.at[chips - 1], ga.at[chips - 1], "fsdp", sibling)]
    to_sibling[0].start()
    around = []
    for step in range(chips - 1):
        there = lax.rem(chip + step + 1, chips) * 2 + core
        move = remote(att, att, ba.at[step], ca.at[step], "fsdp", there)
        move.start()
        around.append(move)
    give(dv, gv, vs, vr)
    load_cot.wait()
    share = width // nd
    columns = cot_vm.shape[1]
    tile = 256

    def add_dq():
        for move in backs:
            move.wait_recv()

        @pl.loop(0, nf)
        def _(home):
            for c in range(spans):
                dq_sum[home, c] = add_slots(home, c, dq_home)

        for step in range(1, nf):
            peer = lax.rem(fs + step, nf)
            move = remote(dq_sum.at[peer], cols(gq, fs, width), ys.at[step], yr.at[step], "fsdp", peer)
            move.start()
            moves.append(move)
        put = pltpu.make_async_copy(dq_sum.at[fs], cols(gq, fs, width), own.at[5])
        put.start()
        puts.append(put)

    nz = nd // 2
    x_at, z_at = dp // nz, lax.rem(dp, nz)
    across = lax.rem(dp + nz, nd)
    z_places = [lax.rem(z_at + step, nz) for step in range(1, nz)]
    z_peers = [x_at * nz + place for place in z_places]
    blocks = []
    flying = {}

    def along_z(turn):
        return turn % 2 == 0

    def launch(turn, stage, copies):
        sent = []
        for i, (source, target, peer) in enumerate(copies):
            place = stage * (nz - 1) + i
            move = remote(source, target, ts.at[turn, place], tr.at[turn, place], "dp", peer)
            move.start()
            sent.append(move)
        flying[turn, stage] = sent

    def arrive(turn, stage):
        for move in flying[turn, stage]:
            move.wait_recv()

    def project(turn, block):
        blocks.append(block)

        @pl.loop(0, columns // tile)
        def _(t):
            at = pl.ds(pl.multiple_of(t * tile, tile), tile)
            value = dot(att_all[block], cot_vm[:, at], TN).astype(jnp.bfloat16)
            term[turn, :, :, at] = value.reshape(nd, share, tile)

        half = turn // 2
        if along_z(turn):
            launch(turn, 0, [
                (term.at[turn, pl.ds(2 * place, 2)], first_z.at[half, i], p)
                for i, (place, p) in enumerate(zip(z_places, z_peers))
            ])
        else:
            launch(turn, 0, [(term.at[turn, pl.ds((1 - x_at) * nz, nz)], first_x.at[half], across)])

    def add_first(turn):
        arrive(turn, 0)
        half = turn // 2
        if along_z(turn):
            def total_of(place):
                value = term[turn, 2 * z_at + place].astype(jnp.float32)
                for i in range(nz - 1):
                    value += first_z[half, i, place].astype(jnp.float32)
                return value

            keep[turn] = total_of(x_at)
            middle[turn, 0] = total_of(1 - x_at).astype(jnp.bfloat16)
            launch(turn, 1, [(middle.at[turn, 0], second.at[turn, 0], across)])
        else:
            def total_of(place):
                value = term[turn, x_at * nz + place].astype(jnp.float32)
                return value + first_x[half, place].astype(jnp.float32)

            keep[turn] = total_of(z_at)
            for i, place in enumerate(z_places):
                middle[turn, i] = total_of(place).astype(jnp.bfloat16)
            launch(turn, 1, [
                (middle.at[turn, i], second.at[turn, i], p) for i, p in enumerate(z_peers)
            ])

    def rows_of(turn, part, parts):
        start = pl.multiple_of(blocks[turn] * width + part * share, share)
        return gp.at[pl.ds(start, parts * share)]

    owned = {}

    def add_second(turn):
        arrive(turn, 1)
        value = keep[turn]
        for i in range(len(flying[turn, 1])):
            value += second[turn, i].astype(jnp.float32)
        total[turn] = value.astype(jnp.bfloat16)
        part = 2 * z_at + x_at if along_z(turn) else dp
        here = rows_of(turn, part, 1)
        owned[turn] = pltpu.make_async_copy(total.at[turn], here, load.at[1 + turn])
        owned[turn].start()
        to = [across] if along_z(turn) else z_peers
        launch(turn, 2, [(total.at[turn], here, p) for p in to])

    def share_all(turn):
        owned[turn].wait()
        arrive(turn, 2)
        if along_z(turn):
            here = rows_of(turn, 2 * z_at, 2)
            launch(turn, 3, [(here, here, p) for p in z_peers])
        else:
            here = rows_of(turn, x_at * nz, nz)
            launch(turn, 3, [(here, here, across)])

    def advance(turn):
        for lag, act in ((2, add_first), (3, add_second), (4, share_all)):
            if 0 <= turn - lag < nf:
                act(turn - lag)

    project(0, fs)
    to_sibling[0].wait_recv()
    project(1, sibling)
    for move in backs:
        move.start()
    turn = 2
    order = [0, chips - 2] + list(range(1, chips - 2))
    for step in order:
        back = lax.rem(chip + chips - step - 1, chips) * 2
        around[step].wait_recv()
        move = remote(
            att_all.at[back + core], att_all.at[back + core], fa.at[step], ga.at[step], "fsdp", sibling
        )
        move.start()
        to_sibling.append(move)
        project(turn, back + core)
        advance(turn)
        move.wait_recv()
        project(turn + 1, back + 1 - core)
        advance(turn + 1)
        if turn == 4:
            add_dq()
        turn += 2
    for later in range(turn, turn + 4):
        advance(later)
    tokens = spans * SPAN
    for block in range(nf):
        here = pl.ds(pl.multiple_of(fs * tokens, tokens), tokens)
        put = pltpu.make_async_copy(
            att_all.at[block, here], ga_out.at[:, pl.ds(block * width, width)], last_sem.at[block]
        )
        put.start()
        puts.append(put)
    for move in outs + backs + to_sibling + around:
        move.wait_send()
    for (_, stage), sent in flying.items():
        for move in sent:
            if stage == 3:
                move.wait_recv()
            move.wait_send()
    for move in moves:
        move.wait()
    for put in puts:
        put.wait()


def dma(*shape):
    return pltpu.SemaphoreType.DMA(shape)


def comm(number, mib=BIG):
    return pltpu.CompilerParams(collective_id=number, has_side_effects=True, vmem_limit_bytes=mib)


def local(queries, nbr_keys, nbr_values, out_proj, nbr_source, nbr_index, nbr_count, cotangent):
    nd, nf = lax.axis_size("dp"), lax.axis_size("fsdp")
    bf, f32, i32 = jnp.bfloat16, jnp.float32, jnp.int32
    token_rows, full_width = queries.shape
    spans = token_rows // SPAN
    nbrs, piece, _ = nbr_keys.shape
    width = full_width // nf
    rows, columns = cotangent.shape
    refs_all = nd * nf
    chips = nf // 2
    sources, indices = nbr_source.T, nbr_index.T
    share = width // nd

    kt, vt, qg, ug, hs, tab = pl.pallas_call(
        lambda *a: spread_kernel(nd, nf, width, *a),
        in_specs=[SM, SM, SM, ANY, ANY, ANY, ANY, ANY],
        out_specs=[ANY, ANY, ANY, ANY, ANY, SM],
        out_shape=[
            jax.ShapeDtypeStruct((nf, nbrs, piece, width), bf),
            jax.ShapeDtypeStruct((nf, nbrs, piece, width), bf),
            jax.ShapeDtypeStruct((nd, nf, SPAN, width), bf),
            jax.ShapeDtypeStruct((nd, nf, SPAN, width), bf),
            jax.ShapeDtypeStruct((nd, SPAN, 128), f32),
            jax.ShapeDtypeStruct((3 * refs_all,), i32),
        ],
        scratch_shapes=[
            pltpu.VMEM((nf, spans, SPAN, width), bf),
            pltpu.VMEM((2, nd, nf, SPAN, width), bf),
            pltpu.VMEM((nf, nbrs, piece, width), bf),
            pltpu.VMEM((nf, nbrs, piece, HEAD_DIM), bf),
            pltpu.VMEM((nf, nbrs, piece, HEAD_DIM), bf),
            pltpu.VMEM((nd, nf, SPAN, width), bf),
            pltpu.VMEM((nd, nf, SPAN, width), bf),
            pltpu.VMEM((nf * spans, SPAN, width), bf),
            pltpu.VMEM((rows, columns), bf),
            pltpu.VMEM((full_width, columns), bf),
            pltpu.VMEM((chips, rows, width), bf),
            pltpu.VMEM((chips, rows, width), bf),
            pltpu.VMEM((chips, rows, width), f32),
            pltpu.VMEM((chips - 1, rows, width), bf),
            pltpu.VMEM((chips - 1, rows, width), bf),
            pltpu.VMEM((width // HEAD_DIM, refs_all, SPAN, nf * piece), f32),
            pltpu.VMEM((nd, SPAN, 128), f32),
            pltpu.VMEM((nd, SPAN, 128), f32),
            pltpu.VMEM((SPAN, 128), f32),
            pltpu.SMEM((refs_all,), i32),
            dma(nf), dma(nf), dma(nf), dma(nf), dma(2 * nf), dma(2 * nf), dma(nd), dma(nd), dma(nd), dma(nd),
            dma(chips), dma(chips), dma(chips), dma(chips), dma(nd), dma(nd), dma(nd), dma(nd), dma(13), dma(2),
        ],
        compiler_params=comm(1),
        name="spread",
    )(
        sources, indices, nbr_count, queries.reshape(spans, SPAN, full_width), nbr_keys, nbr_values,
        cotangent, out_proj,
    )

    o, dq, dk, dv = pl.pallas_call(
        lambda *a: backward_kernel(nf, *a),
        in_specs=[SM, ANY, ANY, ANY, ANY, ANY],
        out_specs=[ANY, ANY, ANY, ANY],
        out_shape=[
            jax.ShapeDtypeStruct((refs_all, SPAN, width), bf),
            jax.ShapeDtypeStruct((refs_all, SPAN, width), bf),
            jax.ShapeDtypeStruct((nf, nbrs, piece, width), bf),
            jax.ShapeDtypeStruct((nf, nbrs, piece, width), bf),
        ],
        scratch_shapes=[
            pltpu.VMEM((refs_all, SPAN, width), bf),
            pltpu.VMEM((refs_all, SPAN, width), bf),
            pltpu.VMEM((nd, SPAN, 128), f32),
            pltpu.VMEM((nf, nbrs, piece, width), bf),
            pltpu.VMEM((nf, nbrs, piece, width), bf),
            pltpu.VMEM((refs_all, SPAN, width), bf),
            pltpu.VMEM((refs_all, SPAN, width), bf),
            pltpu.VMEM((nf, nbrs, piece, width), bf),
            pltpu.VMEM((nf, nbrs, piece, width), bf),
            pltpu.VMEM((nbrs + 1, nf * piece, width), f32),
            pltpu.VMEM((nbrs + 1, nf * piece, width), f32),
            pltpu.SMEM((refs_all,), i32),
            dma(9),
        ],
        compiler_params=pltpu.CompilerParams(vmem_limit_bytes=BIG),
        name="backward",
    )(tab, qg.reshape(refs_all, SPAN, width), ug.reshape(refs_all, SPAN, width), hs, kt, vt)

    attended, gq, gk, gv, grad_proj = pl.pallas_call(
        lambda *a: return_kernel(nd, nf, width, spans, *a),
        in_specs=[SM, SM, ANY, ANY, ANY, ANY, ANY],
        out_specs=[ANY, ANY, ANY, ANY, ANY],
        out_shape=[
            jax.ShapeDtypeStruct((token_rows, full_width), bf),
            jax.ShapeDtypeStruct((spans, SPAN, full_width), bf),
            jax.ShapeDtypeStruct((nbrs, piece, full_width), bf),
            jax.ShapeDtypeStruct((nbrs, piece, full_width), bf),
            jax.ShapeDtypeStruct((full_width, columns), bf),
        ],
        scratch_shapes=[
            pltpu.VMEM((nf, rows, width), bf),
            pltpu.VMEM((nd, nf, SPAN, width), bf),
            pltpu.VMEM((nd, nf, SPAN, width), bf),
            pltpu.VMEM((nf, spans, SPAN, width), bf),
            pltpu.VMEM((nbrs, piece, width), bf),
            pltpu.VMEM((nbrs, piece, width), bf),
            pltpu.VMEM((rows, columns), bf),
            pltpu.VMEM((nf, nd, share, columns), bf),
            pltpu.VMEM((nf // 2, nd // 2 - 1, 2, share, columns), bf),
            pltpu.VMEM((nf // 2, nd // 2, share, columns), bf),
            pltpu.VMEM((nf, nd // 2 - 1, share, columns), bf),
            pltpu.VMEM((nf, nd // 2 - 1, share, columns), bf),
            pltpu.VMEM((nf, share, columns), f32),
            pltpu.VMEM((nf, share, columns), bf),
            dma(nd), dma(nd), dma(nd), dma(nd), dma(nf), dma(nf), dma(nf), dma(nf), dma(nf), dma(nf),
            dma(chips), dma(chips), dma(chips), dma(chips),
            dma(nf, 2 * nd), dma(nf, 2 * nd), dma(7), dma(1 + nf), dma(nf),
        ],
        compiler_params=comm(3),
        name="giveback",
    )(
        sources, nbr_count, o.reshape(nd, nf, SPAN, width), cotangent,
        dq.reshape(nd, nf, SPAN, width), dk, dv,
    )
    results = [grad_proj, gk, gv, attended, gq.reshape(token_rows, full_width)]
    grad_proj, gk, gv, attended, gq = pl.pallas_call(
        finish_kernel,
        in_specs=[ANY] * len(results),
        out_specs=[ANY] * len(results),
        out_shape=[jax.ShapeDtypeStruct(value.shape, value.dtype) for value in results],
        scratch_shapes=[pltpu.VMEM(value.shape, value.dtype) for value in results] + [dma(2, len(results), 4)],
        compiler_params=pltpu.CompilerParams(vmem_limit_bytes=BIG),
        name="finish",
    )(*results)
    return (attended, gq, gk, gv, grad_proj)


def solution(mesh):
    placed = (
        P(("dp", "fsdp"), "enc"),
        P("dp", "fsdp", "enc"),
        P("dp", "fsdp", "enc"),
        P("enc", "fsdp"),
        P(),
        P(),
        P(),
        P("dp", "fsdp"),
    )
    return jax.shard_map(
        local,
        mesh=mesh,
        in_specs=placed,
        out_specs=(
            P(("dp", "fsdp"), "enc"),
            P(("dp", "fsdp"), "enc"),
            P("dp", "fsdp", "enc"),
            P("dp", "fsdp", "enc"),
            P("enc", "fsdp"),
        ),
        check_vma=False,
    )
```

```python
import math

import jax
import jax.numpy as jnp
from jax import lax
from jax.experimental import pallas as pl
from jax.experimental.pallas import tpu as pltpu
from jax.sharding import PartitionSpec as P

HEAD_DIM = 128
SPAN = 64
SLOTS = 2
MESH = pl.DeviceIdType.MESH
ANY = pl.BlockSpec(memory_space=pl.ANY)
VM = pl.BlockSpec(memory_space=pltpu.VMEM)
SM = pl.BlockSpec(memory_space=pltpu.SMEM)
NT = (((1,), (1,)), ((), ()))
TN = (((0,), (0,)), ((), ()))
NN = (((1,), (0,)), ((), ()))
SCALE = 1.0 / math.sqrt(HEAD_DIM)
BIG = 60 << 20


def dot(a, b, dims):
    return lax.dot_general(a, b, dims, preferred_element_type=jnp.float32)


def enter(axes):
    barrier = pltpu.get_barrier_semaphore()
    total = 0
    for axis, size in axes:
        here = lax.axis_index(axis)
        for step in range(1, size):
            pl.semaphore_signal(
                barrier, inc=1, device_id={axis: lax.rem(here + step, size)}, device_id_type=MESH
            )
            total += 1
    pl.semaphore_wait(barrier, total)


def remote(src, dst, send, recv, axis, peer):
    return pltpu.make_async_remote_copy(
        src_ref=src, dst_ref=dst, send_sem=send, recv_sem=recv, device_id={axis: peer}, device_id_type=MESH
    )


def cols(ref, place, width):
    return ref.at[:, :, pl.ds(pl.multiple_of(place * width, width), width)]


def spread_kernel(
    nd, nf, width, src, idx, cnt, q, k, v, cot, proj, kt, vt, qg, ug, hs_out, tab,
    q_heads, send, kt_vm, vt_a, vt_b, qg_vm, ug_vm, u_vm, cot_vm, proj_vm, sib_send, sib_recv, mine, ring_send,
    ring_recv, probs, st, st_home, hs, sel,
    qs, qr, ks, kr, vs, vr, gs, gr, us, ur, bs, br, rs, rr, ss, sr, hsn, hr, own, load,
):
    dp, fs = lax.axis_index("dp"), lax.axis_index("fsdp")
    chips = nf // 2
    chip, core = fs // 2, lax.rem(fs, 2)
    sibling = chip * 2 + 1 - core
    spans = q_heads.shape[1]
    slots = SLOTS * spans
    heads = width // HEAD_DIM
    peers = [lax.rem(dp + step, nd) for step in range(1, nd)]
    loads = [
        pltpu.make_async_copy(cot, cot_vm, load.at[0]),
        pltpu.make_async_copy(proj, proj_vm, load.at[1]),
    ]
    for copy in loads:
        copy.start()
    enter((("dp", nd), ("fsdp", nf)))
    vt_vm = (vt_a, vt_b)

    def v_part(place, head):
        at = pl.multiple_of(place * width + head * HEAD_DIM, HEAD_DIM)
        return v.at[:, :, pl.ds(at, HEAD_DIM)]

    owns = [
        pltpu.make_async_copy(cols(q, fs, width), q_heads.at[fs], own.at[0]),
        pltpu.make_async_copy(cols(k, fs, width), kt_vm.at[fs], own.at[1]),
    ] + [
        pltpu.make_async_copy(v_part(fs, head), vt_vm[head].at[fs], own.at[(2, 11)[head]]) for head in range(heads)
    ]
    for copy in owns:
        copy.start()

    def spread(ref, out, s_sem, r_sem, head=None):
        moves = []
        for step in range(1, nf):
            peer = lax.rem(fs + step, nf)
            if head is None:
                source, target, place = cols(ref, peer, width), out.at[fs], step
            else:
                source, target = v_part(peer, head), vt_vm[head].at[fs]
                place = head * nf + step
            move = remote(source, target, s_sem.at[place], r_sem.at[place], "fsdp", peer)
            move.start()
            moves.append(move)
        return moves

    q_moves = spread(q, q_heads, qs, qr)
    nbr_half = kt_vm.shape[1] // 2

    def spread_keys(part):
        here = pl.ds(part * nbr_half, nbr_half)
        moves = []
        for step in range(1, nf):
            peer = lax.rem(fs + step, nf)
            at = pl.ds(pl.multiple_of(peer * width, width), width)
            place = part * nf + step
            move = remote(k.at[here, :, at], kt_vm.at[fs, here], ks.at[place], kr.at[place], "fsdp", peer)
            move.start()
            moves.append(move)
        return moves

    k_moves = spread_keys(0)
    for copy in loads:
        copy.wait()
    rows = cot_vm.shape[0]
    tile = 512
    sib_moves = {}
    for turn, step in enumerate((1, 0, 2, 3)):
        there = lax.rem(chip + step + 1, chips)
        for which in (1 - core, core):
            block = pl.multiple_of((there * 2 + which) * width, width)
            first = len(sib_moves) == turn

            @pl.loop(0, rows // tile)
            def _(t):
                at = pl.multiple_of(t * tile, tile)
                value = dot(cot_vm[pl.ds(at, tile), :], proj_vm[pl.ds(block, width), :], NT)
                if first:
                    sib_send[step, pl.ds(at, tile), :] = value.astype(jnp.bfloat16)
                else:
                    mine[step, pl.ds(at, tile), :] = value

            if first:
                move = remote(sib_send.at[step], sib_recv.at[step], bs.at[step], br.at[step], "fsdp", sibling)
                move.start()
                sib_moves[step] = move
    half = rows // 2
    piece = 256
    halves = [pl.ds(0, half), pl.ds(half, half)]
    ring_moves = []

    def add_part(step, part, relayed):
        @pl.loop(0, half // piece)
        def _(t):
            at = pl.ds(pl.multiple_of(part * half + t * piece, piece), piece)
            value = mine[step, at, :] + sib_recv[step, at, :].astype(jnp.float32)
            if relayed:
                value += ring_recv[1, at, :].astype(jnp.float32)
            ring_send[step, at, :] = value.astype(jnp.bfloat16)

    def pass_on(step, part, forward):
        there = lax.rem(chip + (1 if forward else chips - 1), chips) * 2 + core
        here = halves[part]
        place = len(ring_moves)
        move = remote(
            ring_send.at[step, here], ring_recv.at[step, here], rs.at[place], rr.at[place], "fsdp", there
        )
        move.start()
        ring_moves.append(move)

    sib_moves[1].wait_recv()
    for part in (0, 1):
        add_part(1, part, False)
        pass_on(1, part, part == 0)
    sib_moves[0].wait_recv()
    add_part(0, 1, False)
    pass_on(0, 1, True)
    sib_moves[2].wait_recv()
    add_part(2, 0, False)
    pass_on(2, 0, False)
    k_moves += spread_keys(1)

    @pl.loop(0, nd)
    def _(group):
        @pl.loop(0, nf)
        def _(home):
            base = (dp * nf + home) * spans
            span = jnp.int32(0)
            for t in range(slots):
                span = jnp.where(src[t % SLOTS, base + t // SLOTS] == group, t // SLOTS, span)
            sel[group * nf + home] = span
            r = group * nf + home
            number, where, live = jnp.int32(0), jnp.int32(0), jnp.int32(0)
            for t in range(slots):
                hit = jnp.logical_and(
                    src[t % SLOTS, r * spans + t // SLOTS] == dp,
                    t % SLOTS < cnt[r * spans + t // SLOTS],
                )
                number = jnp.where(hit, idx[t % SLOTS, r * spans + t // SLOTS], number)
                where = jnp.where(hit, t // SLOTS, where)
                live = jnp.where(hit, 1, live)
            tab[r] = number
            tab[nd * nf + r] = where
            tab[2 * nd * nf + r] = live

    owns[0].wait()
    for move in q_moves:
        move.wait_recv()
    puts = []

    def deliver(kind, source, out, s_sem, r_sem):
        @pl.loop(0, nd)
        def _(group):
            @pl.loop(0, nf)
            def _(home):
                send[kind, group, home] = source(home, sel[group * nf + home])

        moves = [
            remote(send.at[kind, p], out.at[dp], s_sem.at[i], r_sem.at[i], "dp", p)
            for i, p in enumerate(peers)
        ]
        for move in moves:
            move.start()
        put = pltpu.make_async_copy(send.at[kind, dp], out.at[dp], own.at[3 + kind])
        put.start()
        return moves, put

    def store(source, out, number):
        put = pltpu.make_async_copy(source, out, own.at[number])
        put.start()
        puts.append(put)

    q_there, q_put = deliver(0, lambda home, c: q_heads[home, c], qg_vm, gs, gr)
    for part, step in ((0, 0), (1, 2)):
        ring_moves[part].wait_recv()
        add_part(step, part, True)
        pass_on(step, part, step == 0)
    v_moves = [spread(v, None, vs, vr, head) for head in range(heads)]
    q_put.wait()
    for move in q_there:
        move.wait_recv()
    owns[1].wait()
    for move in k_moves:
        move.wait_recv()
    store(qg_vm, qg, 5)
    store(kt_vm, kt, 6)
    lane = lax.broadcasted_iota(jnp.int32, (SPAN, 128), 1)
    length = kt_vm.shape[0] * kt_vm.shape[2]
    group_lanes = heads * nf

    @pl.loop(0, nd)
    def _(d):
        marks = jnp.zeros((SPAN, 128), jnp.float32)
        for f in range(nf):
            n = tab[d * nf + f]
            for h in range(heads):
                part = slice(h * HEAD_DIM, (h + 1) * HEAD_DIM)
                keys = kt_vm[:, n, :, part].reshape(length, HEAD_DIM)
                scores = dot(qg_vm[d, f, :, part], keys, NT) * SCALE
                peak = jnp.max(scores, axis=1, keepdims=True)
                expo = jnp.exp(scores - peak)
                probs[h, d * nf + f] = expo
                marks = jnp.where(lane == heads * f + h, peak, marks)
                total = jnp.sum(expo, axis=1, keepdims=True)
                marks = jnp.where(lane == group_lanes + heads * f + h, total, marks)
        st[d] = marks

    sib_moves[chips - 1].wait_recv()
    for move in ring_moves[2:]:
        move.wait_recv()

    @pl.loop(0, rows // SPAN)
    def _(i):
        at = pl.ds(pl.multiple_of(i * SPAN, SPAN), SPAN)
        value = mine[chips - 1, at, :] + sib_recv[chips - 1, at, :].astype(jnp.float32)
        for step in (0, 2):
            value += ring_recv[step, at, :].astype(jnp.float32)
        u_vm[i] = value.astype(jnp.bfloat16)

    u_there, u_put = deliver(1, lambda home, c: u_vm[home * spans + c], ug_vm, us, ur)
    u_put.wait()
    for move in u_there:
        move.wait_recv()
    store(ug_vm, ug, 7)
    for h in range(heads):
        owns[2 + h].wait()
        for move in v_moves[h]:
            move.wait_recv()
        part = slice(h * HEAD_DIM, (h + 1) * HEAD_DIM)

        @pl.loop(0, nd)
        def _(d):
            marks = st[d]
            for f in range(nf):
                n = tab[d * nf + f]
                values = vt_vm[h][:, n].reshape(length, HEAD_DIM)
                dprobs = dot(ug_vm[d, f, :, part], values, NT)
                mean = jnp.sum(probs[h, d * nf + f] * dprobs, axis=1, keepdims=True)
                marks = jnp.where(lane == 2 * group_lanes + heads * f + h, mean, marks)
            st[d] = marks

    for h in range(heads):
        store(vt_vm[h], vt.at[:, :, :, pl.ds(h * HEAD_DIM, HEAD_DIM)], 8 + 4 * h)
    stats = [
        remote(st.at[p], st_home.at[dp], ss.at[i], sr.at[i], "dp", p) for i, p in enumerate(peers)
    ]
    for move in stats:
        move.start()
    st_put = pltpu.make_async_copy(st.at[dp], st_home.at[dp], own.at[9])
    st_put.start()
    row = lax.broadcasted_iota(jnp.int32, (1, 128), 1)
    place = lax.rem(row, group_lanes) // heads
    sources = []
    both = []
    for t in range(slots):
        values = jnp.zeros((1, 128), jnp.int32)
        for f in range(nf):
            values = jnp.where(place == f, src[t % SLOTS, (dp * nf + f) * spans + t // SLOTS], values)
        sources.append(values)
    for c in range(spans):
        values = jnp.zeros((1, 128), jnp.int32)
        for f in range(nf):
            values = jnp.where(place == f, cnt[(dp * nf + f) * spans + c], values)
        both.append(values > 1)
    st_put.wait()
    for move in stats:
        move.wait_recv()
    table = jnp.zeros((SPAN, 128), jnp.float32)
    for c in range(spans):
        pair = []
        for slot in range(SLOTS):
            found = jnp.zeros((SPAN, 128), jnp.float32)
            for g in range(nd):
                found = jnp.where(sources[SLOTS * c + slot] == g, st_home[g], found)
            pair.append(
                [found] + [pltpu.roll(found, 128 - group_lanes * i, axis=1) for i in (1, 2)]
            )
        (m0, l0, e0), (m1, l1, e1) = pair
        m1 = jnp.where(both[c], m1, -1e30)
        l1, e1 = jnp.where(both[c], l1, 0.0), jnp.where(both[c], e1, 0.0)
        peak = jnp.maximum(m0, m1)
        a0, a1 = jnp.exp(m0 - peak), jnp.exp(m1 - peak)
        total = a0 * l0 + a1 * l1
        log_total = peak + jnp.log(total)
        centre = (a0 * e0 + a1 * e1) / total
        for value, at in ((log_total, c * group_lanes), (centre, 64 + c * group_lanes)):
            moved = pltpu.roll(value, at, axis=1) if at else value
            inside = jnp.logical_and(lane >= at, lane < at + group_lanes)
            table = jnp.where(inside, moved, table)
    hs[...] = table
    gives = [
        remote(hs, hs_out.at[dp], hsn.at[i], hr.at[i], "dp", p) for i, p in enumerate(peers)
    ]
    for move in gives:
        move.start()
    store(hs, hs_out.at[dp], 10)
    for move in q_moves + k_moves + list(sib_moves.values()) + ring_moves + q_there + u_there + stats + sum(v_moves, []):
        move.wait_send()
    for move in gives:
        move.wait()
    for put in puts:
        put.wait()


UNROLL = 4


def backward_kernel(
    nf, tab, q_any, u_any, hs_any, kt_any, vt_any, o_any, dq_any, dk_any, dv_any,
    q, u, hs, kt, vt, o_ref, dq_ref, dk_ref, dv_ref, k_acc, v_acc, listed, sems,
):
    pairs = ((q_any, q), (u_any, u), (hs_any, hs), (kt_any, kt), (vt_any, vt))
    loads = [pltpu.make_async_copy(a, b, sems.at[i]) for i, (a, b) in enumerate(pairs)]
    for copy in loads:
        copy.start()
    lane = lax.broadcasted_iota(jnp.int32, (SPAN, 128), 1)
    pieces, nbrs, piece = kt.shape[0], kt.shape[1], kt.shape[2]
    length = pieces * piece
    heads = kt.shape[3] // HEAD_DIM
    refs = q.shape[0]

    def place(r, ends):
        low, high = ends
        live = tab[2 * refs + r]
        listed[jnp.where(live > 0, low, high)] = r
        return low + live, high - 1 + live

    count, _ = lax.fori_loop(0, refs, place, (jnp.int32(0), jnp.int32(refs - 1)))

    @pl.loop(0, nbrs)
    def _(n):
        k_acc[n] = jnp.zeros(k_acc.shape[1:], jnp.float32)
        v_acc[n] = jnp.zeros(v_acc.shape[1:], jnp.float32)

    for copy in loads:
        copy.wait()

    def pick(array, at):
        return jnp.sum(jnp.where(lane == at, array, 0.0), axis=1, keepdims=True)

    @pl.loop(0, (count + UNROLL - 1) // UNROLL)
    def _(step):
        done = []
        for more in range(UNROLL):
            r = listed[step * UNROLL + more]
            n, c, live = tab[r], tab[refs + r], tab[2 * refs + r]
            into = jnp.where(live > 0, n, nbrs)
            keys = kt[:, n].reshape(length, -1)
            values = vt[:, n].reshape(length, -1)
            query, up, table = q[r], u[r], hs[r // nf]
            at = heads * (nf * c + r % nf)
            outs, dqs, dks, dvs = [], [], [], []
            for h in range(heads):
                part = slice(h * HEAD_DIM, (h + 1) * HEAD_DIM)
                scores = dot(query[:, part], keys[:, part], NT) * SCALE
                probs = jnp.exp(scores - pick(table, at + h))
                rounded = probs.astype(jnp.bfloat16)
                dprobs = dot(up[:, part], values[:, part], NT)
                ds = (probs * (dprobs - pick(table, 64 + at + h)) * SCALE).astype(jnp.bfloat16)
                outs.append(dot(rounded, values[:, part], NN).astype(jnp.bfloat16))
                dqs.append(dot(ds, keys[:, part], NN).astype(jnp.bfloat16))
                dks.append(dot(ds, query[:, part], TN))
                dvs.append(dot(rounded, up[:, part], TN))
            done.append((r, into, outs, dqs, dks, dvs))
        for r, into, outs, dqs, dks, dvs in done:
            o_ref[r] = jnp.concatenate(outs, axis=1)
            dq_ref[r] = jnp.concatenate(dqs, axis=1)
            k_acc[into] += jnp.concatenate(dks, axis=1)
            v_acc[into] += jnp.concatenate(dvs, axis=1)

    puts = [
        pltpu.make_async_copy(o_ref, o_any, sems.at[5]),
        pltpu.make_async_copy(dq_ref, dq_any, sems.at[6]),
    ]
    for put in puts:
        put.start()
    for i, (acc, out, put_to) in enumerate(((k_acc, dk_ref, dk_any), (v_acc, dv_ref, dv_any))):
        @pl.loop(0, nbrs)
        def _(n):
            out[:, n] = acc[n].reshape(pieces, piece, -1).astype(jnp.bfloat16)

        put = pltpu.make_async_copy(out, put_to, sems.at[7 + i])
        put.start()
        puts.append(put)
    for put in puts:
        put.wait()


def finish_kernel(*refs):
    count = len(refs) // 3
    sems = refs[-1]
    takes = []
    for i in range(count):
        source, held = refs[i], refs[2 * count + i]
        pieces = 4 if source.shape[0] % 4 == 0 else 1
        size = source.shape[0] // pieces
        for j in range(pieces):
            part = pl.ds(j * size, size)
            take = pltpu.make_async_copy(source.at[part], held.at[part], sems.at[0, i, j])
            take.start()
            takes.append((i, j, part, take))
    puts = []
    for i, j, part, take in takes:
        take.wait()
        put = pltpu.make_async_copy(refs[2 * count + i].at[part], refs[count + i].at[part], sems.at[1, i, j])
        put.start()
        puts.append(put)
    for put in puts:
        put.wait()


def return_kernel(
    nd, nf, width, spans, src, cnt, o, cot, dq, dk, dv, ga_out, gq, gk, gv, gp, att_all,
    o_a, o_b, dq_home, dq_sum, k_own, v_own, cot_vm, term, first_z, first_x, second, middle, keep, total,
    os, orr, qs, qr, ks, kr, vs, vr, ys, yr, fa, ga, ba, ca, ts, tr, own, load, last_sem,
):
    dp, fs = lax.axis_index("dp"), lax.axis_index("fsdp")
    chips = nf // 2
    chip, core = fs // 2, lax.rem(fs, 2)
    sibling = chip * 2 + 1 - core
    load_cot = pltpu.make_async_copy(cot, cot_vm, load.at[0])
    load_cot.start()
    enter((("dp", nd), ("fsdp", nf)))
    peers = [lax.rem(dp + step, nd) for step in range(1, nd)]
    halves = [pl.ds(0, nf // 2), pl.ds(nf // 2, nf // 2)]
    firsts = [
        pltpu.make_async_copy(o.at[dp, halves[0]], o_a.at[dp], own.at[6]),
        pltpu.make_async_copy(o.at[dp, halves[1]], o_b.at[dp], own.at[7]),
        pltpu.make_async_copy(dq.at[dp], dq_home.at[dp], own.at[0]),
        pltpu.make_async_copy(dk.at[fs], k_own, own.at[1]),
        pltpu.make_async_copy(dv.at[fs], v_own, own.at[2]),
    ]
    for copy in firsts:
        copy.start()
    outs = [
        [
            remote(o.at[p, halves[h]], held.at[dp], os.at[h * nd + i], orr.at[h * nd + i], "dp", p)
            for i, p in enumerate(peers)
        ]
        for h, held in enumerate((o_a, o_b))
    ]
    backs = [
        remote(dq.at[p], dq_home.at[dp], qs.at[i], qr.at[i], "dp", p) for i, p in enumerate(peers)
    ]
    for move in outs[0] + outs[1]:
        move.start()
    moves = []

    nbrs = dk.shape[1]
    early = nbrs // 3

    def give(ref, out, s_sem, r_sem, start, size, base):
        here = pl.ds(start, size)
        for step in range(1, nf):
            peer = lax.rem(fs + step, nf)
            at = pl.ds(pl.multiple_of(fs * width, width), width)
            place = base + step
            move = remote(ref.at[peer, here], out.at[here, :, at], s_sem.at[place], r_sem.at[place], "fsdp", peer)
            move.start()
            moves.append(move)

    give(dk, gk, ks, kr, 0, early, 0)
    for copy in firsts:
        copy.wait()
    puts = [
        pltpu.make_async_copy(k_own, cols(gk, fs, width), own.at[3]),
        pltpu.make_async_copy(v_own, cols(gv, fs, width), own.at[4]),
    ]
    for put in puts:
        put.start()

    def add_slots(home, place, c, parts):
        span = (dp * nf + home) * spans + c
        first = parts[src[0, span], place].astype(jnp.float32)
        second = parts[src[1, span], place].astype(jnp.float32)
        both = cnt[span] > 1
        return (first + jnp.where(both, second, 0.0)).astype(jnp.bfloat16)

    to_sibling, around = [], []
    per_half = (nf // 2) * spans * SPAN
    for h, held in enumerate((o_a, o_b)):
        for move in outs[h]:
            move.wait_recv()

        @pl.loop(0, nf // 2)
        def _(place):
            home = h * (nf // 2) + place
            for c in range(spans):
                at = pl.multiple_of((home * spans + c) * SPAN, SPAN)
                att_all[fs, pl.ds(at, SPAN), :] = add_slots(home, place, c, held)

        att = att_all.at[fs, pl.ds(h * per_half, per_half)]
        move = remote(att, att, fa.at[chips - 1 + h], ga.at[chips - 1 + h], "fsdp", sibling)
        move.start()
        to_sibling.append(move)
        for step in range(chips - 1):
            there = lax.rem(chip + step + 1, chips) * 2 + core
            place = h * (chips - 1) + step
            move = remote(att, att, ba.at[place], ca.at[place], "fsdp", there)
            move.start()
            around.append(move)
    give(dk, gk, ks, kr, early, nbrs - early, nf)
    give(dv, gv, vs, vr, 0, nbrs, 0)
    load_cot.wait()
    share = width // nd
    columns = cot_vm.shape[1]
    tile = 256

    def add_dq():
        for move in backs:
            move.wait_recv()

        @pl.loop(0, nf)
        def _(home):
            for c in range(spans):
                dq_sum[home, c] = add_slots(home, home, c, dq_home)

        for step in range(1, nf):
            peer = lax.rem(fs + step, nf)
            move = remote(dq_sum.at[peer], cols(gq, fs, width), ys.at[step], yr.at[step], "fsdp", peer)
            move.start()
            moves.append(move)
        put = pltpu.make_async_copy(dq_sum.at[fs], cols(gq, fs, width), own.at[5])
        put.start()
        puts.append(put)

    nz = nd // 2
    x_at, z_at = dp // nz, lax.rem(dp, nz)
    across = lax.rem(dp + nz, nd)
    z_places = [lax.rem(z_at + step, nz) for step in range(1, nz)]
    z_peers = [x_at * nz + place for place in z_places]
    blocks = []
    flying = {}

    def along_z(turn):
        return turn % 2 == 0

    def launch(turn, stage, copies):
        sent = []
        for i, (source, target, peer) in enumerate(copies):
            place = stage * (nz - 1) + i
            move = remote(source, target, ts.at[turn, place], tr.at[turn, place], "dp", peer)
            move.start()
            sent.append(move)
        flying[turn, stage] = sent

    def arrive(turn, stage):
        for move in flying[turn, stage]:
            move.wait_recv()

    def project(turn, block):
        blocks.append(block)

        @pl.loop(0, columns // tile)
        def _(t):
            at = pl.ds(pl.multiple_of(t * tile, tile), tile)
            value = dot(att_all[block], cot_vm[:, at], TN).astype(jnp.bfloat16)
            term[turn, :, :, at] = value.reshape(nd, share, tile)

        half = turn // 2
        if along_z(turn):
            launch(turn, 0, [
                (term.at[turn, pl.ds(2 * place, 2)], first_z.at[half, i], p)
                for i, (place, p) in enumerate(zip(z_places, z_peers))
            ])
        else:
            launch(turn, 0, [(term.at[turn, pl.ds((1 - x_at) * nz, nz)], first_x.at[half], across)])

    def add_first(turn):
        arrive(turn, 0)
        half = turn // 2
        if along_z(turn):
            def total_of(place):
                value = term[turn, 2 * z_at + place].astype(jnp.float32)
                for i in range(nz - 1):
                    value += first_z[half, i, place].astype(jnp.float32)
                return value

            keep[turn] = total_of(x_at)
            middle[turn, 0] = total_of(1 - x_at).astype(jnp.bfloat16)
            launch(turn, 1, [(middle.at[turn, 0], second.at[turn, 0], across)])
        else:
            def total_of(place):
                value = term[turn, x_at * nz + place].astype(jnp.float32)
                return value + first_x[half, place].astype(jnp.float32)

            keep[turn] = total_of(z_at)
            for i, place in enumerate(z_places):
                middle[turn, i] = total_of(place).astype(jnp.bfloat16)
            launch(turn, 1, [
                (middle.at[turn, i], second.at[turn, i], p) for i, p in enumerate(z_peers)
            ])

    def rows_of(turn, part, parts):
        start = pl.multiple_of(blocks[turn] * width + part * share, share)
        return gp.at[pl.ds(start, parts * share)]

    owned = {}

    def add_second(turn):
        arrive(turn, 1)
        value = keep[turn]
        for i in range(len(flying[turn, 1])):
            value += second[turn, i].astype(jnp.float32)
        total[turn] = value.astype(jnp.bfloat16)
        part = 2 * z_at + x_at if along_z(turn) else dp
        here = rows_of(turn, part, 1)
        owned[turn] = pltpu.make_async_copy(total.at[turn], here, load.at[1 + turn])
        owned[turn].start()
        to = [across] if along_z(turn) else z_peers
        launch(turn, 2, [(total.at[turn], here, p) for p in to])

    def share_all(turn):
        owned[turn].wait()
        arrive(turn, 2)
        if along_z(turn):
            here = rows_of(turn, 2 * z_at, 2)
            launch(turn, 3, [(here, here, p) for p in z_peers])
        else:
            here = rows_of(turn, x_at * nz, nz)
            launch(turn, 3, [(here, here, across)])

    def advance(turn):
        for lag, act in ((2, add_first), (3, add_second), (4, share_all)):
            if 0 <= turn - lag < nf:
                act(turn - lag)

    project(0, fs)
    for move in to_sibling[:2]:
        move.wait_recv()
    project(1, sibling)
    for move in backs:
        move.start()
    turn = 2
    order = [0, chips - 2] + list(range(1, chips - 2))
    for step in order:
        back = lax.rem(chip + chips - step - 1, chips) * 2
        around[step].wait_recv()
        around[chips - 1 + step].wait_recv()
        move = remote(
            att_all.at[back + core], att_all.at[back + core], fa.at[step], ga.at[step], "fsdp", sibling
        )
        move.start()
        to_sibling.append(move)
        project(turn, back + core)
        advance(turn)
        move.wait_recv()
        project(turn + 1, back + 1 - core)
        advance(turn + 1)
        if turn == 4:
            add_dq()
        turn += 2
    for later in range(turn, turn + 4):
        advance(later)
    tokens = spans * SPAN
    for block in range(nf):
        here = pl.ds(pl.multiple_of(fs * tokens, tokens), tokens)
        put = pltpu.make_async_copy(
            att_all.at[block, here], ga_out.at[:, pl.ds(block * width, width)], last_sem.at[block]
        )
        put.start()
        puts.append(put)
    for move in outs[0] + outs[1] + backs + to_sibling + around:
        move.wait_send()
    for (_, stage), sent in flying.items():
        for move in sent:
            if stage == 3:
                move.wait_recv()
            move.wait_send()
    for move in moves:
        move.wait()
    for put in puts:
        put.wait()


def dma(*shape):
    return pltpu.SemaphoreType.DMA(shape)


def comm(number, mib=BIG):
    return pltpu.CompilerParams(collective_id=number, has_side_effects=True, vmem_limit_bytes=mib)


def local(queries, nbr_keys, nbr_values, out_proj, nbr_source, nbr_index, nbr_count, cotangent):
    nd, nf = lax.axis_size("dp"), lax.axis_size("fsdp")
    bf, f32, i32 = jnp.bfloat16, jnp.float32, jnp.int32
    token_rows, full_width = queries.shape
    spans = token_rows // SPAN
    nbrs, piece, _ = nbr_keys.shape
    width = full_width // nf
    rows, columns = cotangent.shape
    refs_all = nd * nf
    chips = nf // 2
    sources, indices = nbr_source.T, nbr_index.T
    share = width // nd

    kt, vt, qg, ug, hs, tab = pl.pallas_call(
        lambda *a: spread_kernel(nd, nf, width, *a),
        in_specs=[SM, SM, SM, ANY, ANY, ANY, ANY, ANY],
        out_specs=[ANY, ANY, ANY, ANY, ANY, SM],
        out_shape=[
            jax.ShapeDtypeStruct((nf, nbrs, piece, width), bf),
            jax.ShapeDtypeStruct((nf, nbrs, piece, width), bf),
            jax.ShapeDtypeStruct((nd, nf, SPAN, width), bf),
            jax.ShapeDtypeStruct((nd, nf, SPAN, width), bf),
            jax.ShapeDtypeStruct((nd, SPAN, 128), f32),
            jax.ShapeDtypeStruct((3 * refs_all,), i32),
        ],
        scratch_shapes=[
            pltpu.VMEM((nf, spans, SPAN, width), bf),
            pltpu.VMEM((2, nd, nf, SPAN, width), bf),
            pltpu.VMEM((nf, nbrs, piece, width), bf),
            pltpu.VMEM((nf, nbrs, piece, HEAD_DIM), bf),
            pltpu.VMEM((nf, nbrs, piece, HEAD_DIM), bf),
            pltpu.VMEM((nd, nf, SPAN, width), bf),
            pltpu.VMEM((nd, nf, SPAN, width), bf),
            pltpu.VMEM((nf * spans, SPAN, width), bf),
            pltpu.VMEM((rows, columns), bf),
            pltpu.VMEM((full_width, columns), bf),
            pltpu.VMEM((chips, rows, width), bf),
            pltpu.VMEM((chips, rows, width), bf),
            pltpu.VMEM((chips, rows, width), f32),
            pltpu.VMEM((chips - 1, rows, width), bf),
            pltpu.VMEM((chips - 1, rows, width), bf),
            pltpu.VMEM((width // HEAD_DIM, refs_all, SPAN, nf * piece), f32),
            pltpu.VMEM((nd, SPAN, 128), f32),
            pltpu.VMEM((nd, SPAN, 128), f32),
            pltpu.VMEM((SPAN, 128), f32),
            pltpu.SMEM((refs_all,), i32),
            dma(nf), dma(nf), dma(2 * nf), dma(2 * nf), dma(2 * nf), dma(2 * nf), dma(nd), dma(nd), dma(nd), dma(nd),
            dma(chips), dma(chips), dma(6), dma(6), dma(nd), dma(nd), dma(nd), dma(nd), dma(13), dma(2),
        ],
        compiler_params=comm(1),
        name="spread",
    )(
        sources, indices, nbr_count, queries.reshape(spans, SPAN, full_width), nbr_keys, nbr_values,
        cotangent, out_proj,
    )

    o, dq, dk, dv = pl.pallas_call(
        lambda *a: backward_kernel(nf, *a),
        in_specs=[SM, ANY, ANY, ANY, ANY, ANY],
        out_specs=[ANY, ANY, ANY, ANY],
        out_shape=[
            jax.ShapeDtypeStruct((refs_all, SPAN, width), bf),
            jax.ShapeDtypeStruct((refs_all, SPAN, width), bf),
            jax.ShapeDtypeStruct((nf, nbrs, piece, width), bf),
            jax.ShapeDtypeStruct((nf, nbrs, piece, width), bf),
        ],
        scratch_shapes=[
            pltpu.VMEM((refs_all, SPAN, width), bf),
            pltpu.VMEM((refs_all, SPAN, width), bf),
            pltpu.VMEM((nd, SPAN, 128), f32),
            pltpu.VMEM((nf, nbrs, piece, width), bf),
            pltpu.VMEM((nf, nbrs, piece, width), bf),
            pltpu.VMEM((refs_all, SPAN, width), bf),
            pltpu.VMEM((refs_all, SPAN, width), bf),
            pltpu.VMEM((nf, nbrs, piece, width), bf),
            pltpu.VMEM((nf, nbrs, piece, width), bf),
            pltpu.VMEM((nbrs + 1, nf * piece, width), f32),
            pltpu.VMEM((nbrs + 1, nf * piece, width), f32),
            pltpu.SMEM((refs_all,), i32),
            dma(9),
        ],
        compiler_params=pltpu.CompilerParams(vmem_limit_bytes=BIG),
        name="backward",
    )(tab, qg.reshape(refs_all, SPAN, width), ug.reshape(refs_all, SPAN, width), hs, kt, vt)

    attended, gq, gk, gv, grad_proj = pl.pallas_call(
        lambda *a: return_kernel(nd, nf, width, spans, *a),
        in_specs=[SM, SM, ANY, ANY, ANY, ANY, ANY],
        out_specs=[ANY, ANY, ANY, ANY, ANY],
        out_shape=[
            jax.ShapeDtypeStruct((token_rows, full_width), bf),
            jax.ShapeDtypeStruct((spans, SPAN, full_width), bf),
            jax.ShapeDtypeStruct((nbrs, piece, full_width), bf),
            jax.ShapeDtypeStruct((nbrs, piece, full_width), bf),
            jax.ShapeDtypeStruct((full_width, columns), bf),
        ],
        scratch_shapes=[
            pltpu.VMEM((nf, rows, width), bf),
            pltpu.VMEM((nd, nf // 2, SPAN, width), bf),
            pltpu.VMEM((nd, nf // 2, SPAN, width), bf),
            pltpu.VMEM((nd, nf, SPAN, width), bf),
            pltpu.VMEM((nf, spans, SPAN, width), bf),
            pltpu.VMEM((nbrs, piece, width), bf),
            pltpu.VMEM((nbrs, piece, width), bf),
            pltpu.VMEM((rows, columns), bf),
            pltpu.VMEM((nf, nd, share, columns), bf),
            pltpu.VMEM((nf // 2, nd // 2 - 1, 2, share, columns), bf),
            pltpu.VMEM((nf // 2, nd // 2, share, columns), bf),
            pltpu.VMEM((nf, nd // 2 - 1, share, columns), bf),
            pltpu.VMEM((nf, nd // 2 - 1, share, columns), bf),
            pltpu.VMEM((nf, share, columns), f32),
            pltpu.VMEM((nf, share, columns), bf),
            dma(2 * nd), dma(2 * nd), dma(nd), dma(nd), dma(2 * nf), dma(2 * nf), dma(nf), dma(nf), dma(nf), dma(nf),
            dma(chips + 1), dma(chips + 1), dma(2 * chips), dma(2 * chips),
            dma(nf, 2 * nd), dma(nf, 2 * nd), dma(8), dma(1 + nf), dma(nf),
        ],
        compiler_params=comm(3),
        name="giveback",
    )(
        sources, nbr_count, o.reshape(nd, nf, SPAN, width), cotangent,
        dq.reshape(nd, nf, SPAN, width), dk, dv,
    )
    results = [grad_proj, gk, gv, attended, gq.reshape(token_rows, full_width)]
    grad_proj, gk, gv, attended, gq = pl.pallas_call(
        finish_kernel,
        in_specs=[ANY] * len(results),
        out_specs=[ANY] * len(results),
        out_shape=[jax.ShapeDtypeStruct(value.shape, value.dtype) for value in results],
        scratch_shapes=[pltpu.VMEM(value.shape, value.dtype) for value in results] + [dma(2, len(results), 4)],
        compiler_params=pltpu.CompilerParams(vmem_limit_bytes=BIG),
        name="finish",
    )(*results)
    return (attended, gq, gk, gv, grad_proj)


def solution(mesh):
    placed = (
        P(("dp", "fsdp"), "enc"),
        P("dp", "fsdp", "enc"),
        P("dp", "fsdp", "enc"),
        P("enc", "fsdp"),
        P(),
        P(),
        P(),
        P("dp", "fsdp"),
    )
    return jax.shard_map(
        local,
        mesh=mesh,
        in_specs=placed,
        out_specs=(
            P(("dp", "fsdp"), "enc"),
            P(("dp", "fsdp"), "enc"),
            P("dp", "fsdp", "enc"),
            P("dp", "fsdp", "enc"),
            P("enc", "fsdp"),
        ),
        check_vma=False,
    )
```

```python
import math

import jax
import jax.numpy as jnp
from jax import lax
from jax.experimental import pallas as pl
from jax.experimental.pallas import tpu as pltpu
from jax.sharding import PartitionSpec as P

HEAD_DIM = 128
SPAN = 64
SLOTS = 2
MESH = pl.DeviceIdType.MESH
ANY = pl.BlockSpec(memory_space=pl.ANY)
VM = pl.BlockSpec(memory_space=pltpu.VMEM)
SM = pl.BlockSpec(memory_space=pltpu.SMEM)
NT = (((1,), (1,)), ((), ()))
TN = (((0,), (0,)), ((), ()))
NN = (((1,), (0,)), ((), ()))
SCALE = 1.0 / math.sqrt(HEAD_DIM)
BIG = 60 << 20


def dot(a, b, dims):
    return lax.dot_general(a, b, dims, preferred_element_type=jnp.float32)


def enter(axes):
    barrier = pltpu.get_barrier_semaphore()
    total = 0
    for axis, size in axes:
        here = lax.axis_index(axis)
        for step in range(1, size):
            pl.semaphore_signal(
                barrier, inc=1, device_id={axis: lax.rem(here + step, size)}, device_id_type=MESH
            )
            total += 1
    pl.semaphore_wait(barrier, total)


def remote(src, dst, send, recv, axis, peer):
    return pltpu.make_async_remote_copy(
        src_ref=src, dst_ref=dst, send_sem=send, recv_sem=recv, device_id={axis: peer}, device_id_type=MESH
    )


def cols(ref, place, width):
    return ref.at[:, :, pl.ds(pl.multiple_of(place * width, width), width)]


def spread_kernel(
    nd, nf, width, src, idx, cnt, q, k, v, cot, proj, kt, vt, qg, ug, hs_out, tab, o_first, weights,
    q_heads, send, kt_vm, vt_a, vt_b, qg_vm, ug_vm, u_vm, cot_vm, proj_vm, sib_send, sib_recv, mine, ring_send,
    ring_recv, probs, st, st_home, hs, sel, o_send,
    qs, qr, ks, kr, vs, vr, gs, gr, us, ur, bs, br, rs, rr, ss, sr, hsn, hr, oss, osr, own, load,
):
    dp, fs = lax.axis_index("dp"), lax.axis_index("fsdp")
    chips = nf // 2
    chip, core = fs // 2, lax.rem(fs, 2)
    sibling = chip * 2 + 1 - core
    spans = q_heads.shape[1]
    slots = SLOTS * spans
    heads = width // HEAD_DIM
    peers = [lax.rem(dp + step, nd) for step in range(1, nd)]
    loads = [
        pltpu.make_async_copy(cot, cot_vm, load.at[0]),
        pltpu.make_async_copy(proj, proj_vm, load.at[1]),
    ]
    for copy in loads:
        copy.start()
    enter((("dp", nd), ("fsdp", nf)))
    vt_vm = (vt_a, vt_b)

    def v_part(place, head):
        at = pl.multiple_of(place * width + head * HEAD_DIM, HEAD_DIM)
        return v.at[:, :, pl.ds(at, HEAD_DIM)]

    owns = [
        pltpu.make_async_copy(cols(q, fs, width), q_heads.at[fs], own.at[0]),
        pltpu.make_async_copy(cols(k, fs, width), kt_vm.at[fs], own.at[1]),
    ] + [
        pltpu.make_async_copy(v_part(fs, head), vt_vm[head].at[fs], own.at[(2, 11)[head]]) for head in range(heads)
    ]
    for copy in owns:
        copy.start()

    def spread(ref, out, s_sem, r_sem, head=None):
        moves = []
        for step in range(1, nf):
            peer = lax.rem(fs + step, nf)
            if head is None:
                source, target, place = cols(ref, peer, width), out.at[fs], step
            else:
                source, target = v_part(peer, head), vt_vm[head].at[fs]
                place = head * nf + step
            move = remote(source, target, s_sem.at[place], r_sem.at[place], "fsdp", peer)
            move.start()
            moves.append(move)
        return moves

    q_moves = spread(q, q_heads, qs, qr)
    nbr_half = kt_vm.shape[1] // 2

    def spread_keys(part):
        here = pl.ds(part * nbr_half, nbr_half)
        moves = []
        for step in range(1, nf):
            peer = lax.rem(fs + step, nf)
            at = pl.ds(pl.multiple_of(peer * width, width), width)
            place = part * nf + step
            move = remote(k.at[here, :, at], kt_vm.at[fs, here], ks.at[place], kr.at[place], "fsdp", peer)
            move.start()
            moves.append(move)
        return moves

    k_moves = spread_keys(0)
    for copy in loads:
        copy.wait()
    rows = cot_vm.shape[0]
    tile = 512
    sib_moves = {}
    for turn, step in enumerate((1, 0, 2, 3)):
        there = lax.rem(chip + step + 1, chips)
        for which in (1 - core, core):
            block = pl.multiple_of((there * 2 + which) * width, width)
            first = len(sib_moves) == turn

            @pl.loop(0, rows // tile)
            def _(t):
                at = pl.multiple_of(t * tile, tile)
                value = dot(cot_vm[pl.ds(at, tile), :], proj_vm[pl.ds(block, width), :], NT)
                if first:
                    sib_send[step, pl.ds(at, tile), :] = value.astype(jnp.bfloat16)
                else:
                    mine[step, pl.ds(at, tile), :] = value

            if first:
                move = remote(sib_send.at[step], sib_recv.at[step], bs.at[step], br.at[step], "fsdp", sibling)
                move.start()
                sib_moves[step] = move
    half = rows // 2
    piece = 256
    halves = [pl.ds(0, half), pl.ds(half, half)]
    ring_moves = []

    def add_part(step, part, relayed):
        @pl.loop(0, half // piece)
        def _(t):
            at = pl.ds(pl.multiple_of(part * half + t * piece, piece), piece)
            value = mine[step, at, :] + sib_recv[step, at, :].astype(jnp.float32)
            if relayed:
                value += ring_recv[1, at, :].astype(jnp.float32)
            ring_send[step, at, :] = value.astype(jnp.bfloat16)

    def pass_on(step, part, forward):
        there = lax.rem(chip + (1 if forward else chips - 1), chips) * 2 + core
        here = halves[part]
        place = len(ring_moves)
        move = remote(
            ring_send.at[step, here], ring_recv.at[step, here], rs.at[place], rr.at[place], "fsdp", there
        )
        move.start()
        ring_moves.append(move)

    sib_moves[1].wait_recv()
    for part in (0, 1):
        add_part(1, part, False)
        pass_on(1, part, part == 0)
    sib_moves[0].wait_recv()
    add_part(0, 1, False)
    pass_on(0, 1, True)
    sib_moves[2].wait_recv()
    add_part(2, 0, False)
    pass_on(2, 0, False)
    k_moves += spread_keys(1)

    @pl.loop(0, nd)
    def _(group):
        @pl.loop(0, nf)
        def _(home):
            base = (dp * nf + home) * spans
            span = jnp.int32(0)
            for t in range(slots):
                span = jnp.where(src[t % SLOTS, base + t // SLOTS] == group, t // SLOTS, span)
            sel[group * nf + home] = span
            r = group * nf + home
            number, where, live = jnp.int32(0), jnp.int32(0), jnp.int32(0)
            for t in range(slots):
                hit = jnp.logical_and(
                    src[t % SLOTS, r * spans + t // SLOTS] == dp,
                    t % SLOTS < cnt[r * spans + t // SLOTS],
                )
                number = jnp.where(hit, idx[t % SLOTS, r * spans + t // SLOTS], number)
                where = jnp.where(hit, t // SLOTS, where)
                live = jnp.where(hit, 1, live)
            tab[r] = number
            tab[nd * nf + r] = where
            tab[2 * nd * nf + r] = live

    owns[0].wait()
    for move in q_moves:
        move.wait_recv()
    puts = []

    def deliver(kind, source, out, s_sem, r_sem):
        @pl.loop(0, nd)
        def _(group):
            @pl.loop(0, nf)
            def _(home):
                send[kind, group, home] = source(home, sel[group * nf + home])

        moves = [
            remote(send.at[kind, p], out.at[dp], s_sem.at[i], r_sem.at[i], "dp", p)
            for i, p in enumerate(peers)
        ]
        for move in moves:
            move.start()
        put = pltpu.make_async_copy(send.at[kind, dp], out.at[dp], own.at[3 + kind])
        put.start()
        return moves, put

    def store(source, out, number):
        put = pltpu.make_async_copy(source, out, own.at[number])
        put.start()
        puts.append(put)

    q_there, q_put = deliver(0, lambda home, c: q_heads[home, c], qg_vm, gs, gr)
    for part, step in ((0, 0), (1, 2)):
        ring_moves[part].wait_recv()
        add_part(step, part, True)
        pass_on(step, part, step == 0)
    v_moves = [spread(v, None, vs, vr, head) for head in range(heads)]
    q_put.wait()
    for move in q_there:
        move.wait_recv()
    owns[1].wait()
    for move in k_moves:
        move.wait_recv()
    store(qg_vm, qg, 5)
    store(kt_vm, kt, 6)
    lane = lax.broadcasted_iota(jnp.int32, (SPAN, 128), 1)
    length = kt_vm.shape[0] * kt_vm.shape[2]
    group_lanes = heads * nf

    @pl.loop(0, nd)
    def _(d):
        marks = jnp.zeros((SPAN, 128), jnp.float32)
        for f in range(nf):
            n = tab[d * nf + f]
            for h in range(heads):
                part = slice(h * HEAD_DIM, (h + 1) * HEAD_DIM)
                keys = kt_vm[:, n, :, part].reshape(length, HEAD_DIM)
                scores = dot(qg_vm[d, f, :, part], keys, NT) * SCALE
                peak = jnp.max(scores, axis=1, keepdims=True)
                expo = jnp.exp(scores - peak)
                probs[h, d * nf + f] = expo
                marks = jnp.where(lane == heads * f + h, peak, marks)
                total = jnp.sum(expo, axis=1, keepdims=True)
                marks = jnp.where(lane == group_lanes + heads * f + h, total, marks)
        st[d] = marks

    sib_moves[chips - 1].wait_recv()
    for move in ring_moves[2:]:
        move.wait_recv()

    @pl.loop(0, rows // SPAN)
    def _(i):
        at = pl.ds(pl.multiple_of(i * SPAN, SPAN), SPAN)
        value = mine[chips - 1, at, :] + sib_recv[chips - 1, at, :].astype(jnp.float32)
        for step in (0, 2):
            value += ring_recv[step, at, :].astype(jnp.float32)
        u_vm[i] = value.astype(jnp.bfloat16)

    u_there, u_put = deliver(1, lambda home, c: u_vm[home * spans + c], ug_vm, us, ur)
    owns[2].wait()
    for move in v_moves[0]:
        move.wait_recv()

    @pl.loop(0, nd)
    def _(d):
        for f in range(nf):
            values = vt_vm[0][:, tab[d * nf + f]].reshape(length, HEAD_DIM)
            expo = probs[0, d * nf + f].astype(jnp.bfloat16)
            o_send[d, f] = dot(expo, values, NN).astype(jnp.bfloat16)

    o_there = [
        remote(o_send.at[p], o_first.at[dp], oss.at[i], osr.at[i], "dp", p) for i, p in enumerate(peers)
    ]
    for move in o_there:
        move.start()
    store(o_send.at[dp], o_first.at[dp], 13)
    u_put.wait()
    for move in u_there:
        move.wait_recv()
    store(ug_vm, ug, 7)
    for h in range(heads):
        if h > 0:
            owns[2 + h].wait()
            for move in v_moves[h]:
                move.wait_recv()
        part = slice(h * HEAD_DIM, (h + 1) * HEAD_DIM)

        @pl.loop(0, nd)
        def _(d):
            marks = st[d]
            for f in range(nf):
                n = tab[d * nf + f]
                values = vt_vm[h][:, n].reshape(length, HEAD_DIM)
                dprobs = dot(ug_vm[d, f, :, part], values, NT)
                mean = jnp.sum(probs[h, d * nf + f] * dprobs, axis=1, keepdims=True)
                marks = jnp.where(lane == 2 * group_lanes + heads * f + h, mean, marks)
            st[d] = marks

    for h in range(heads):
        store(vt_vm[h], vt.at[:, :, :, pl.ds(h * HEAD_DIM, HEAD_DIM)], 8 + 4 * h)
    stats = [
        remote(st.at[p], st_home.at[dp], ss.at[i], sr.at[i], "dp", p) for i, p in enumerate(peers)
    ]
    for move in stats:
        move.start()
    st_put = pltpu.make_async_copy(st.at[dp], st_home.at[dp], own.at[9])
    st_put.start()
    row = lax.broadcasted_iota(jnp.int32, (1, 128), 1)
    place = lax.rem(row, group_lanes) // heads
    sources = []
    both = []
    for t in range(slots):
        values = jnp.zeros((1, 128), jnp.int32)
        for f in range(nf):
            values = jnp.where(place == f, src[t % SLOTS, (dp * nf + f) * spans + t // SLOTS], values)
        sources.append(values)
    for c in range(spans):
        values = jnp.zeros((1, 128), jnp.int32)
        for f in range(nf):
            values = jnp.where(place == f, cnt[(dp * nf + f) * spans + c], values)
        both.append(values > 1)
    st_put.wait()
    for move in stats:
        move.wait_recv()
    table = jnp.zeros((SPAN, 128), jnp.float32)
    scales = jnp.zeros((SPAN, 128), jnp.float32)
    for c in range(spans):
        pair = []
        for slot in range(SLOTS):
            found = jnp.zeros((SPAN, 128), jnp.float32)
            for g in range(nd):
                found = jnp.where(sources[SLOTS * c + slot] == g, st_home[g], found)
            pair.append(
                [found] + [pltpu.roll(found, 128 - group_lanes * i, axis=1) for i in (1, 2)]
            )
        (m0, l0, e0), (m1, l1, e1) = pair
        m1 = jnp.where(both[c], m1, -1e30)
        l1, e1 = jnp.where(both[c], l1, 0.0), jnp.where(both[c], e1, 0.0)
        peak = jnp.maximum(m0, m1)
        a0, a1 = jnp.exp(m0 - peak), jnp.exp(m1 - peak)
        total = a0 * l0 + a1 * l1
        log_total = peak + jnp.log(total)
        centre = (a0 * e0 + a1 * e1) / total
        for value, at in ((log_total, c * group_lanes), (centre, 64 + c * group_lanes)):
            moved = pltpu.roll(value, at, axis=1) if at else value
            inside = jnp.logical_and(lane >= at, lane < at + group_lanes)
            table = jnp.where(inside, moved, table)
        for slot, value in enumerate((a0 / total, a1 / total)):
            at = (SLOTS * c + slot) * group_lanes
            moved = pltpu.roll(value, at, axis=1) if at else value
            inside = jnp.logical_and(lane >= at, lane < at + group_lanes)
            scales = jnp.where(inside, moved, scales)
    weights[...] = scales
    hs[...] = table
    gives = [
        remote(hs, hs_out.at[dp], hsn.at[i], hr.at[i], "dp", p) for i, p in enumerate(peers)
    ]
    for move in gives:
        move.start()
    store(hs, hs_out.at[dp], 10)
    for move in q_moves + k_moves + list(sib_moves.values()) + ring_moves + q_there + u_there + stats + sum(v_moves, []):
        move.wait_send()
    for move in gives + o_there:
        move.wait()
    for put in puts:
        put.wait()


UNROLL = 4


def backward_kernel(
    nf, tab, q_any, u_any, hs_any, kt_any, vt_any, o_any, dq_any, dk_any, dv_any,
    q, u, hs, kt, vt, o_ref, dq_ref, dk_ref, dv_ref, k_acc, v_acc, listed, sems,
):
    pairs = ((q_any, q), (u_any, u), (hs_any, hs), (kt_any, kt), (vt_any, vt))
    loads = [pltpu.make_async_copy(a, b, sems.at[i]) for i, (a, b) in enumerate(pairs)]
    for copy in loads:
        copy.start()
    lane = lax.broadcasted_iota(jnp.int32, (SPAN, 128), 1)
    pieces, nbrs, piece = kt.shape[0], kt.shape[1], kt.shape[2]
    length = pieces * piece
    heads = kt.shape[3] // HEAD_DIM
    refs = q.shape[0]

    def place(r, ends):
        low, high = ends
        live = tab[2 * refs + r]
        listed[jnp.where(live > 0, low, high)] = r
        return low + live, high - 1 + live

    count, _ = lax.fori_loop(0, refs, place, (jnp.int32(0), jnp.int32(refs - 1)))

    @pl.loop(0, nbrs)
    def _(n):
        k_acc[n] = jnp.zeros(k_acc.shape[1:], jnp.float32)
        v_acc[n] = jnp.zeros(v_acc.shape[1:], jnp.float32)

    for copy in loads:
        copy.wait()

    def pick(array, at):
        return jnp.sum(jnp.where(lane == at, array, 0.0), axis=1, keepdims=True)

    @pl.loop(0, (count + UNROLL - 1) // UNROLL)
    def _(step):
        done = []
        for more in range(UNROLL):
            r = listed[step * UNROLL + more]
            n, c, live = tab[r], tab[refs + r], tab[2 * refs + r]
            into = jnp.where(live > 0, n, nbrs)
            keys = kt[:, n].reshape(length, -1)
            values = vt[:, n].reshape(length, -1)
            query, up, table = q[r], u[r], hs[r // nf]
            at = heads * (nf * c + r % nf)
            outs, dqs, dks, dvs = [], [], [], []
            for h in range(heads):
                part = slice(h * HEAD_DIM, (h + 1) * HEAD_DIM)
                scores = dot(query[:, part], keys[:, part], NT) * SCALE
                probs = jnp.exp(scores - pick(table, at + h))
                rounded = probs.astype(jnp.bfloat16)
                dprobs = dot(up[:, part], values[:, part], NT)
                ds = (probs * (dprobs - pick(table, 64 + at + h)) * SCALE).astype(jnp.bfloat16)
                if h > 0:
                    outs.append(dot(rounded, values[:, part], NN).astype(jnp.bfloat16))
                dqs.append(dot(ds, keys[:, part], NN).astype(jnp.bfloat16))
                dks.append(dot(ds, query[:, part], TN))
                dvs.append(dot(rounded, up[:, part], TN))
            done.append((r, into, outs, dqs, dks, dvs))
        for r, into, outs, dqs, dks, dvs in done:
            o_ref[r] = outs[0]
            dq_ref[r] = jnp.concatenate(dqs, axis=1)
            k_acc[into] += jnp.concatenate(dks, axis=1)
            v_acc[into] += jnp.concatenate(dvs, axis=1)

    puts = [
        pltpu.make_async_copy(o_ref, o_any, sems.at[5]),
        pltpu.make_async_copy(dq_ref, dq_any, sems.at[6]),
    ]
    for put in puts:
        put.start()
    for i, (acc, out, put_to) in enumerate(((k_acc, dk_ref, dk_any), (v_acc, dv_ref, dv_any))):
        @pl.loop(0, nbrs)
        def _(n):
            out[:, n] = acc[n].reshape(pieces, piece, -1).astype(jnp.bfloat16)

        put = pltpu.make_async_copy(out, put_to, sems.at[7 + i])
        put.start()
        puts.append(put)
    for put in puts:
        put.wait()


def finish_kernel(*refs):
    count = len(refs) // 3
    sems = refs[-1]
    takes = []
    for i in range(count):
        source, held = refs[i], refs[2 * count + i]
        pieces = 4 if source.shape[0] % 4 == 0 else 1
        size = source.shape[0] // pieces
        for j in range(pieces):
            part = pl.ds(j * size, size)
            take = pltpu.make_async_copy(source.at[part], held.at[part], sems.at[0, i, j])
            take.start()
            takes.append((i, j, part, take))
    puts = []
    for i, j, part, take in takes:
        take.wait()
        put = pltpu.make_async_copy(refs[2 * count + i].at[part], refs[count + i].at[part], sems.at[1, i, j])
        put.start()
        puts.append(put)
    for put in puts:
        put.wait()


def return_kernel(
    nd, nf, width, spans, src, cnt, weights, o_first, o, cot, dq, dk, dv, ga_out, gq, gk, gv, gp, att_all,
    o_a, o_b, dq_home, dq_sum, k_own, v_own, cot_vm, term, first_z, first_x, second, middle, keep, total,
    os, orr, qs, qr, ks, kr, vs, vr, ys, yr, fa, ga, ba, ca, ts, tr, own, load, last_sem,
):
    dp, fs = lax.axis_index("dp"), lax.axis_index("fsdp")
    chips = nf // 2
    chip, core = fs // 2, lax.rem(fs, 2)
    sibling = chip * 2 + 1 - core
    load_cot = pltpu.make_async_copy(cot, cot_vm, load.at[0])
    load_cot.start()
    enter((("dp", nd), ("fsdp", nf)))
    peers = [lax.rem(dp + step, nd) for step in range(1, nd)]
    firsts = [
        pltpu.make_async_copy(o_first, o_a, own.at[6]),
        pltpu.make_async_copy(o.at[dp], o_b.at[dp], own.at[7]),
        pltpu.make_async_copy(dq.at[dp], dq_home.at[dp], own.at[0]),
        pltpu.make_async_copy(dk.at[fs], k_own, own.at[1]),
        pltpu.make_async_copy(dv.at[fs], v_own, own.at[2]),
    ]
    for copy in firsts:
        copy.start()
    outs = [
        remote(o.at[p], o_b.at[dp], os.at[i], orr.at[i], "dp", p) for i, p in enumerate(peers)
    ]
    backs = [
        remote(dq.at[p], dq_home.at[dp], qs.at[i], qr.at[i], "dp", p) for i, p in enumerate(peers)
    ]
    for move in outs + backs:
        move.start()
    moves = []

    nbrs = dk.shape[1]
    early = nbrs // 3

    def give(ref, out, s_sem, r_sem, start, size, base):
        here = pl.ds(start, size)
        for step in range(1, nf):
            peer = lax.rem(fs + step, nf)
            at = pl.ds(pl.multiple_of(fs * width, width), width)
            place = base + step
            move = remote(ref.at[peer, here], out.at[here, :, at], s_sem.at[place], r_sem.at[place], "fsdp", peer)
            move.start()
            moves.append(move)

    for copy in firsts:
        copy.wait()
    puts = [
        pltpu.make_async_copy(k_own, cols(gk, fs, width), own.at[3]),
        pltpu.make_async_copy(v_own, cols(gv, fs, width), own.at[4]),
    ]
    for put in puts:
        put.start()

    def add_slots(home, place, c, parts):
        span = (dp * nf + home) * spans + c
        first = parts[src[0, span], place].astype(jnp.float32)
        second = parts[src[1, span], place].astype(jnp.float32)
        both = cnt[span] > 1
        return (first + jnp.where(both, second, 0.0)).astype(jnp.bfloat16)

    to_sibling, around = [], {}
    lane = lax.broadcasted_iota(jnp.int32, (SPAN, 128), 1)
    table = weights[...]
    heads = width // HEAD_DIM

    def head_of(block, h):
        return att_all.at[block, :, pl.ds(h * HEAD_DIM, HEAD_DIM)]

    def weigh(home, c):
        span = (dp * nf + home) * spans + c
        value = jnp.zeros((SPAN, HEAD_DIM), jnp.float32)
        for slot in range(SLOTS):
            at = heads * (nf * (SLOTS * c + slot) + home)
            scale = jnp.sum(jnp.where(lane == at, table, 0.0), axis=1, keepdims=True)
            part = scale * o_a[src[slot, span], home].astype(jnp.float32)
            value += part if slot == 0 else jnp.where(cnt[span] > slot, part, 0.0)
        return value.astype(jnp.bfloat16)

    for h in range(heads):
        if h > 0:
            for move in outs:
                move.wait_recv()

        @pl.loop(0, nf)
        def _(home):
            for c in range(spans):
                at = pl.multiple_of((home * spans + c) * SPAN, SPAN)
                value = weigh(home, c) if h == 0 else add_slots(home, home, c, o_b)
                att_all[fs, pl.ds(at, SPAN), h * HEAD_DIM : (h + 1) * HEAD_DIM] = value

        att = head_of(fs, h)
        move = remote(att, att, fa.at[chips - 1 + h], ga.at[chips - 1 + h], "fsdp", sibling)
        move.start()
        to_sibling.append(move)
        for step in (0, chips - 2):
            there = lax.rem(chip + step + 1, chips) * 2 + core
            place = h * (chips - 1) + step
            move = remote(att, att, ba.at[place], ca.at[place], "fsdp", there)
            move.start()
            around[h, step] = move
        give(dk, gk, ks, kr, h * early, early, h * nf)
    load_cot.wait()
    share = width // nd
    columns = cot_vm.shape[1]
    tile = 256

    def add_dq():
        for move in backs:
            move.wait_recv()

        @pl.loop(0, nf)
        def _(home):
            for c in range(spans):
                dq_sum[home, c] = add_slots(home, home, c, dq_home)

        for step in range(1, nf):
            peer = lax.rem(fs + step, nf)
            move = remote(dq_sum.at[peer], cols(gq, fs, width), ys.at[step], yr.at[step], "fsdp", peer)
            move.start()
            moves.append(move)
        put = pltpu.make_async_copy(dq_sum.at[fs], cols(gq, fs, width), own.at[5])
        put.start()
        puts.append(put)

    nz = nd // 2
    x_at, z_at = dp // nz, lax.rem(dp, nz)
    across = lax.rem(dp + nz, nd)
    z_places = [lax.rem(z_at + step, nz) for step in range(1, nz)]
    z_peers = [x_at * nz + place for place in z_places]
    blocks = []
    flying = {}

    def along_z(turn):
        return turn % 2 == 0

    def launch(turn, stage, copies):
        sent = []
        for i, (source, target, peer) in enumerate(copies):
            place = stage * (nz - 1) + i
            move = remote(source, target, ts.at[turn, place], tr.at[turn, place], "dp", peer)
            move.start()
            sent.append(move)
        flying[turn, stage] = sent

    def arrive(turn, stage):
        for move in flying[turn, stage]:
            move.wait_recv()

    def project(turn, block):
        blocks.append(block)

        @pl.loop(0, columns // tile)
        def _(t):
            at = pl.ds(pl.multiple_of(t * tile, tile), tile)
            value = dot(att_all[block], cot_vm[:, at], TN).astype(jnp.bfloat16)
            term[turn, :, :, at] = value.reshape(nd, share, tile)

        half = turn // 2
        if along_z(turn):
            launch(turn, 0, [
                (term.at[turn, pl.ds(2 * place, 2)], first_z.at[half, i], p)
                for i, (place, p) in enumerate(zip(z_places, z_peers))
            ])
        else:
            launch(turn, 0, [(term.at[turn, pl.ds((1 - x_at) * nz, nz)], first_x.at[half], across)])

    def add_first(turn):
        arrive(turn, 0)
        half = turn // 2
        if along_z(turn):
            def total_of(place):
                value = term[turn, 2 * z_at + place].astype(jnp.float32)
                for i in range(nz - 1):
                    value += first_z[half, i, place].astype(jnp.float32)
                return value

            keep[turn] = total_of(x_at)
            middle[turn, 0] = total_of(1 - x_at).astype(jnp.bfloat16)
            launch(turn, 1, [(middle.at[turn, 0], second.at[turn, 0], across)])
        else:
            def total_of(place):
                value = term[turn, x_at * nz + place].astype(jnp.float32)
                return value + first_x[half, place].astype(jnp.float32)

            keep[turn] = total_of(z_at)
            for i, place in enumerate(z_places):
                middle[turn, i] = total_of(place).astype(jnp.bfloat16)
            launch(turn, 1, [
                (middle.at[turn, i], second.at[turn, i], p) for i, p in enumerate(z_peers)
            ])

    def rows_of(turn, part, parts):
        start = pl.multiple_of(blocks[turn] * width + part * share, share)
        return gp.at[pl.ds(start, parts * share)]

    owned = {}

    def add_second(turn):
        arrive(turn, 1)
        value = keep[turn]
        for i in range(len(flying[turn, 1])):
            value += second[turn, i].astype(jnp.float32)
        total[turn] = value.astype(jnp.bfloat16)
        part = 2 * z_at + x_at if along_z(turn) else dp
        here = rows_of(turn, part, 1)
        owned[turn] = pltpu.make_async_copy(total.at[turn], here, load.at[1 + turn])
        owned[turn].start()
        to = [across] if along_z(turn) else z_peers
        launch(turn, 2, [(total.at[turn], here, p) for p in to])

    def share_all(turn):
        owned[turn].wait()
        arrive(turn, 2)
        if along_z(turn):
            here = rows_of(turn, 2 * z_at, 2)
            launch(turn, 3, [(here, here, p) for p in z_peers])
        else:
            here = rows_of(turn, x_at * nz, nz)
            launch(turn, 3, [(here, here, across)])

    def advance(turn):
        for lag, act in ((2, add_first), (3, add_second), (4, share_all)):
            if 0 <= turn - lag < nf:
                act(turn - lag)

    project(0, fs)
    for move in to_sibling[:2]:
        move.wait_recv()
    project(1, sibling)
    for h, step in ((0, 0), (1, chips - 2)):
        for each in range(heads):
            around[each, step].wait_recv()
        back = lax.rem(chip + chips - step - 1, chips) * 2 + core
        there = lax.rem(chip + step + 1, chips) * 2 + core
        place = h * (chips - 1) + 1
        held = head_of(back, h)
        around[h, 1] = remote(held, held, ba.at[place], ca.at[place], "fsdp", there)
        around[h, 1].start()
    give(dk, gk, ks, kr, heads * early, nbrs - heads * early, heads * nf)
    give(dv, gv, vs, vr, 0, nbrs, 0)
    turn = 2
    order = [0, chips - 2] + list(range(1, chips - 2))
    for step in order:
        back = lax.rem(chip + chips - step - 1, chips) * 2
        if step == 1:
            for each in range(heads):
                around[each, 1].wait_recv()
        move = remote(
            att_all.at[back + core], att_all.at[back + core], fa.at[step], ga.at[step], "fsdp", sibling
        )
        move.start()
        to_sibling.append(move)
        project(turn, back + core)
        advance(turn)
        move.wait_recv()
        project(turn + 1, back + 1 - core)
        advance(turn + 1)
        if turn == 4:
            add_dq()
        turn += 2
    for later in range(turn, turn + 4):
        advance(later)
    tokens = spans * SPAN
    for block in range(nf):
        here = pl.ds(pl.multiple_of(fs * tokens, tokens), tokens)
        put = pltpu.make_async_copy(
            att_all.at[block, here], ga_out.at[:, pl.ds(block * width, width)], last_sem.at[block]
        )
        put.start()
        puts.append(put)
    for move in outs + backs + to_sibling + list(around.values()):
        move.wait_send()
    for (_, stage), sent in flying.items():
        for move in sent:
            if stage == 3:
                move.wait_recv()
            move.wait_send()
    for move in moves:
        move.wait()
    for put in puts:
        put.wait()


def dma(*shape):
    return pltpu.SemaphoreType.DMA(shape)


def comm(number, mib=BIG):
    return pltpu.CompilerParams(collective_id=number, has_side_effects=True, vmem_limit_bytes=mib)


def local(queries, nbr_keys, nbr_values, out_proj, nbr_source, nbr_index, nbr_count, cotangent):
    nd, nf = lax.axis_size("dp"), lax.axis_size("fsdp")
    bf, f32, i32 = jnp.bfloat16, jnp.float32, jnp.int32
    token_rows, full_width = queries.shape
    spans = token_rows // SPAN
    nbrs, piece, _ = nbr_keys.shape
    width = full_width // nf
    rows, columns = cotangent.shape
    refs_all = nd * nf
    chips = nf // 2
    sources, indices = nbr_source.T, nbr_index.T
    share = width // nd

    kt, vt, qg, ug, hs, tab, o_first, weights = pl.pallas_call(
        lambda *a: spread_kernel(nd, nf, width, *a),
        in_specs=[SM, SM, SM, ANY, ANY, ANY, ANY, ANY],
        out_specs=[ANY, ANY, ANY, ANY, ANY, SM, ANY, VM],
        out_shape=[
            jax.ShapeDtypeStruct((nf, nbrs, piece, width), bf),
            jax.ShapeDtypeStruct((nf, nbrs, piece, width), bf),
            jax.ShapeDtypeStruct((nd, nf, SPAN, width), bf),
            jax.ShapeDtypeStruct((nd, nf, SPAN, width), bf),
            jax.ShapeDtypeStruct((nd, SPAN, 128), f32),
            jax.ShapeDtypeStruct((3 * refs_all,), i32),
            jax.ShapeDtypeStruct((nd, nf, SPAN, HEAD_DIM), bf),
            jax.ShapeDtypeStruct((SPAN, 128), f32),
        ],
        scratch_shapes=[
            pltpu.VMEM((nf, spans, SPAN, width), bf),
            pltpu.VMEM((2, nd, nf, SPAN, width), bf),
            pltpu.VMEM((nf, nbrs, piece, width), bf),
            pltpu.VMEM((nf, nbrs, piece, HEAD_DIM), bf),
            pltpu.VMEM((nf, nbrs, piece, HEAD_DIM), bf),
            pltpu.VMEM((nd, nf, SPAN, width), bf),
            pltpu.VMEM((nd, nf, SPAN, width), bf),
            pltpu.VMEM((nf * spans, SPAN, width), bf),
            pltpu.VMEM((rows, columns), bf),
            pltpu.VMEM((full_width, columns), bf),
            pltpu.VMEM((chips, rows, width), bf),
            pltpu.VMEM((chips, rows, width), bf),
            pltpu.VMEM((chips, rows, width), f32),
            pltpu.VMEM((chips - 1, rows, width), bf),
            pltpu.VMEM((chips - 1, rows, width), bf),
            pltpu.VMEM((width // HEAD_DIM, refs_all, SPAN, nf * piece), f32),
            pltpu.VMEM((nd, SPAN, 128), f32),
            pltpu.VMEM((nd, SPAN, 128), f32),
            pltpu.VMEM((SPAN, 128), f32),
            pltpu.SMEM((refs_all,), i32),
            pltpu.VMEM((nd, nf, SPAN, HEAD_DIM), bf),
            dma(nf), dma(nf), dma(2 * nf), dma(2 * nf), dma(2 * nf), dma(2 * nf), dma(nd), dma(nd), dma(nd), dma(nd),
            dma(chips), dma(chips), dma(6), dma(6), dma(nd), dma(nd), dma(nd), dma(nd), dma(nd), dma(nd), dma(14), dma(2),
        ],
        compiler_params=comm(1),
        name="spread",
    )(
        sources, indices, nbr_count, queries.reshape(spans, SPAN, full_width), nbr_keys, nbr_values,
        cotangent, out_proj,
    )

    o, dq, dk, dv = pl.pallas_call(
        lambda *a: backward_kernel(nf, *a),
        in_specs=[SM, ANY, ANY, ANY, ANY, ANY],
        out_specs=[ANY, ANY, ANY, ANY],
        out_shape=[
            jax.ShapeDtypeStruct((refs_all, SPAN, HEAD_DIM), bf),
            jax.ShapeDtypeStruct((refs_all, SPAN, width), bf),
            jax.ShapeDtypeStruct((nf, nbrs, piece, width), bf),
            jax.ShapeDtypeStruct((nf, nbrs, piece, width), bf),
        ],
        scratch_shapes=[
            pltpu.VMEM((refs_all, SPAN, width), bf),
            pltpu.VMEM((refs_all, SPAN, width), bf),
            pltpu.VMEM((nd, SPAN, 128), f32),
            pltpu.VMEM((nf, nbrs, piece, width), bf),
            pltpu.VMEM((nf, nbrs, piece, width), bf),
            pltpu.VMEM((refs_all, SPAN, HEAD_DIM), bf),
            pltpu.VMEM((refs_all, SPAN, width), bf),
            pltpu.VMEM((nf, nbrs, piece, width), bf),
            pltpu.VMEM((nf, nbrs, piece, width), bf),
            pltpu.VMEM((nbrs + 1, nf * piece, width), f32),
            pltpu.VMEM((nbrs + 1, nf * piece, width), f32),
            pltpu.SMEM((refs_all,), i32),
            dma(9),
        ],
        compiler_params=pltpu.CompilerParams(vmem_limit_bytes=BIG),
        name="backward",
    )(tab, qg.reshape(refs_all, SPAN, width), ug.reshape(refs_all, SPAN, width), hs, kt, vt)

    attended, gq, gk, gv, grad_proj = pl.pallas_call(
        lambda *a: return_kernel(nd, nf, width, spans, *a),
        in_specs=[SM, SM, VM, ANY, ANY, ANY, ANY, ANY, ANY],
        out_specs=[ANY, ANY, ANY, ANY, ANY],
        out_shape=[
            jax.ShapeDtypeStruct((token_rows, full_width), bf),
            jax.ShapeDtypeStruct((spans, SPAN, full_width), bf),
            jax.ShapeDtypeStruct((nbrs, piece, full_width), bf),
            jax.ShapeDtypeStruct((nbrs, piece, full_width), bf),
            jax.ShapeDtypeStruct((full_width, columns), bf),
        ],
        scratch_shapes=[
            pltpu.VMEM((nf, rows, width), bf),
            pltpu.VMEM((nd, nf, SPAN, HEAD_DIM), bf),
            pltpu.VMEM((nd, nf, SPAN, HEAD_DIM), bf),
            pltpu.VMEM((nd, nf, SPAN, width), bf),
            pltpu.VMEM((nf, spans, SPAN, width), bf),
            pltpu.VMEM((nbrs, piece, width), bf),
            pltpu.VMEM((nbrs, piece, width), bf),
            pltpu.VMEM((rows, columns), bf),
            pltpu.VMEM((nf, nd, share, columns), bf),
            pltpu.VMEM((nf // 2, nd // 2 - 1, 2, share, columns), bf),
            pltpu.VMEM((nf // 2, nd // 2, share, columns), bf),
            pltpu.VMEM((nf, nd // 2 - 1, share, columns), bf),
            pltpu.VMEM((nf, nd // 2 - 1, share, columns), bf),
            pltpu.VMEM((nf, share, columns), f32),
            pltpu.VMEM((nf, share, columns), bf),
            dma(nd), dma(nd), dma(nd), dma(nd), dma(3 * nf), dma(3 * nf), dma(nf), dma(nf), dma(nf), dma(nf),
            dma(chips + 1), dma(chips + 1), dma(2 * chips), dma(2 * chips),
            dma(nf, 2 * nd), dma(nf, 2 * nd), dma(8), dma(1 + nf), dma(nf),
        ],
        compiler_params=comm(3),
        name="giveback",
    )(
        sources, nbr_count, weights, o_first, o.reshape(nd, nf, SPAN, HEAD_DIM), cotangent,
        dq.reshape(nd, nf, SPAN, width), dk, dv,
    )
    results = [grad_proj, gk, gv, attended, gq.reshape(token_rows, full_width)]
    grad_proj, gk, gv, attended, gq = pl.pallas_call(
        finish_kernel,
        in_specs=[ANY] * len(results),
        out_specs=[ANY] * len(results),
        out_shape=[jax.ShapeDtypeStruct(value.shape, value.dtype) for value in results],
        scratch_shapes=[pltpu.VMEM(value.shape, value.dtype) for value in results] + [dma(2, len(results), 4)],
        compiler_params=pltpu.CompilerParams(vmem_limit_bytes=BIG),
        name="finish",
    )(*results)
    return (attended, gq, gk, gv, grad_proj)


def solution(mesh):
    placed = (
        P(("dp", "fsdp"), "enc"),
        P("dp", "fsdp", "enc"),
        P("dp", "fsdp", "enc"),
        P("enc", "fsdp"),
        P(),
        P(),
        P(),
        P("dp", "fsdp"),
    )
    return jax.shard_map(
        local,
        mesh=mesh,
        in_specs=placed,
        out_specs=(
            P(("dp", "fsdp"), "enc"),
            P(("dp", "fsdp"), "enc"),
            P("dp", "fsdp", "enc"),
            P("dp", "fsdp", "enc"),
            P("enc", "fsdp"),
        ),
        check_vma=False,
    )
```

```python
import math

import jax
import jax.numpy as jnp
from jax import lax
from jax.experimental import pallas as pl
from jax.experimental.pallas import tpu as pltpu
from jax.sharding import PartitionSpec as P

HEAD_DIM = 128
SPAN = 64
SLOTS = 2
MESH = pl.DeviceIdType.MESH
ANY = pl.BlockSpec(memory_space=pl.ANY)
VM = pl.BlockSpec(memory_space=pltpu.VMEM)
SM = pl.BlockSpec(memory_space=pltpu.SMEM)
NT = (((1,), (1,)), ((), ()))
TN = (((0,), (0,)), ((), ()))
NN = (((1,), (0,)), ((), ()))
SCALE = 1.0 / math.sqrt(HEAD_DIM)
BIG = 60 << 20


def dot(a, b, dims):
    return lax.dot_general(a, b, dims, preferred_element_type=jnp.float32)


def enter(axes):
    barrier = pltpu.get_barrier_semaphore()
    total = 0
    for axis, size in axes:
        here = lax.axis_index(axis)
        for step in range(1, size):
            pl.semaphore_signal(
                barrier, inc=1, device_id={axis: lax.rem(here + step, size)}, device_id_type=MESH
            )
            total += 1
    pl.semaphore_wait(barrier, total)


def remote(src, dst, send, recv, axis, peer):
    return pltpu.make_async_remote_copy(
        src_ref=src, dst_ref=dst, send_sem=send, recv_sem=recv, device_id={axis: peer}, device_id_type=MESH
    )


def cols(ref, place, width):
    return ref.at[:, :, pl.ds(pl.multiple_of(place * width, width), width)]


def spread_kernel(
    nd, nf, width, src, idx, cnt, q, k, v, cot, proj, kt, vt, qg, ug, hs_out, tab, o_first, weights,
    q_heads, send, kt_vm, vt_a, vt_b, qg_vm, ug_vm, u_vm, cot_vm, proj_vm, sib_send, sib_recv, mine, ring_send,
    ring_recv, probs, st, st_home, hs, sel, o_send,
    qs, qr, ks, kr, vs, vr, gs, gr, us, ur, bs, br, rs, rr, ss, sr, hsn, hr, oss, osr, own, load,
):
    dp, fs = lax.axis_index("dp"), lax.axis_index("fsdp")
    chips = nf // 2
    chip, core = fs // 2, lax.rem(fs, 2)
    sibling = chip * 2 + 1 - core
    spans = q_heads.shape[1]
    slots = SLOTS * spans
    heads = width // HEAD_DIM
    peers = [lax.rem(dp + step, nd) for step in range(1, nd)]
    loads = [
        pltpu.make_async_copy(cot, cot_vm, load.at[0]),
        pltpu.make_async_copy(proj, proj_vm, load.at[1]),
    ]
    for copy in loads:
        copy.start()
    enter((("dp", nd), ("fsdp", nf)))
    vt_vm = (vt_a, vt_b)

    def v_part(place, head):
        at = pl.multiple_of(place * width + head * HEAD_DIM, HEAD_DIM)
        return v.at[:, :, pl.ds(at, HEAD_DIM)]

    owns = [
        pltpu.make_async_copy(cols(q, fs, width), q_heads.at[fs], own.at[0]),
        pltpu.make_async_copy(cols(k, fs, width), kt_vm.at[fs], own.at[1]),
    ] + [
        pltpu.make_async_copy(v_part(fs, head), vt_vm[head].at[fs], own.at[(2, 11)[head]]) for head in range(heads)
    ]
    for copy in owns:
        copy.start()

    def spread(ref, out, s_sem, r_sem, head=None):
        moves = []
        for step in range(1, nf):
            peer = lax.rem(fs + step, nf)
            if head is None:
                source, target, place = cols(ref, peer, width), out.at[fs], step
            else:
                source, target = v_part(peer, head), vt_vm[head].at[fs]
                place = head * nf + step
            move = remote(source, target, s_sem.at[place], r_sem.at[place], "fsdp", peer)
            move.start()
            moves.append(move)
        return moves

    q_moves = spread(q, q_heads, qs, qr)
    nbr_half = kt_vm.shape[1] // 2

    def spread_keys(part):
        here = pl.ds(part * nbr_half, nbr_half)
        moves = []
        for step in range(1, nf):
            peer = lax.rem(fs + step, nf)
            at = pl.ds(pl.multiple_of(peer * width, width), width)
            place = part * nf + step
            move = remote(k.at[here, :, at], kt_vm.at[fs, here], ks.at[place], kr.at[place], "fsdp", peer)
            move.start()
            moves.append(move)
        return moves

    k_moves = spread_keys(0)
    for copy in loads:
        copy.wait()
    rows = cot_vm.shape[0]
    tile = 512
    sib_moves = {}
    for turn, step in enumerate((1, 0, 2, 3)):
        there = lax.rem(chip + step + 1, chips)
        for which in (1 - core, core):
            block = pl.multiple_of((there * 2 + which) * width, width)
            first = len(sib_moves) == turn

            @pl.loop(0, rows // tile)
            def _(t):
                at = pl.multiple_of(t * tile, tile)
                value = dot(cot_vm[pl.ds(at, tile), :], proj_vm[pl.ds(block, width), :], NT)
                if first:
                    sib_send[step, pl.ds(at, tile), :] = value.astype(jnp.bfloat16)
                else:
                    mine[step, pl.ds(at, tile), :] = value

            if first:
                move = remote(sib_send.at[step], sib_recv.at[step], bs.at[step], br.at[step], "fsdp", sibling)
                move.start()
                sib_moves[step] = move
    half = rows // 2
    piece = 256
    halves = [pl.ds(0, half), pl.ds(half, half)]
    ring_moves = []

    def add_part(step, part, relayed):
        @pl.loop(0, half // piece)
        def _(t):
            at = pl.ds(pl.multiple_of(part * half + t * piece, piece), piece)
            value = mine[step, at, :] + sib_recv[step, at, :].astype(jnp.float32)
            if relayed:
                value += ring_recv[1, at, :].astype(jnp.float32)
            ring_send[step, at, :] = value.astype(jnp.bfloat16)

    def pass_on(step, part, forward):
        there = lax.rem(chip + (1 if forward else chips - 1), chips) * 2 + core
        here = halves[part]
        place = len(ring_moves)
        move = remote(
            ring_send.at[step, here], ring_recv.at[step, here], rs.at[place], rr.at[place], "fsdp", there
        )
        move.start()
        ring_moves.append(move)

    sib_moves[1].wait_recv()
    for part in (0, 1):
        add_part(1, part, False)
        pass_on(1, part, part == 0)
    sib_moves[0].wait_recv()
    add_part(0, 1, False)
    pass_on(0, 1, True)
    sib_moves[2].wait_recv()
    add_part(2, 0, False)
    pass_on(2, 0, False)
    k_moves += spread_keys(1)

    @pl.loop(0, nd)
    def _(group):
        @pl.loop(0, nf)
        def _(home):
            base = (dp * nf + home) * spans
            span = jnp.int32(0)
            for t in range(slots):
                span = jnp.where(src[t % SLOTS, base + t // SLOTS] == group, t // SLOTS, span)
            sel[group * nf + home] = span
            r = group * nf + home
            number, where, live = jnp.int32(0), jnp.int32(0), jnp.int32(0)
            for t in range(slots):
                hit = jnp.logical_and(
                    src[t % SLOTS, r * spans + t // SLOTS] == dp,
                    t % SLOTS < cnt[r * spans + t // SLOTS],
                )
                number = jnp.where(hit, idx[t % SLOTS, r * spans + t // SLOTS], number)
                where = jnp.where(hit, t // SLOTS, where)
                live = jnp.where(hit, 1, live)
            tab[r] = number
            tab[nd * nf + r] = where
            tab[2 * nd * nf + r] = live

    owns[0].wait()
    for move in q_moves:
        move.wait_recv()
    puts = []

    def deliver(kind, source, out, s_sem, r_sem):
        @pl.loop(0, nd)
        def _(group):
            @pl.loop(0, nf)
            def _(home):
                send[kind, group, home] = source(home, sel[group * nf + home])

        moves = [
            remote(send.at[kind, p], out.at[dp], s_sem.at[i], r_sem.at[i], "dp", p)
            for i, p in enumerate(peers)
        ]
        for move in moves:
            move.start()
        put = pltpu.make_async_copy(send.at[kind, dp], out.at[dp], own.at[3 + kind])
        put.start()
        return moves, put

    def store(source, out, number):
        put = pltpu.make_async_copy(source, out, own.at[number])
        put.start()
        puts.append(put)

    q_there, q_put = deliver(0, lambda home, c: q_heads[home, c], qg_vm, gs, gr)
    for part, step in ((0, 0), (1, 2)):
        ring_moves[part].wait_recv()
        add_part(step, part, True)
        pass_on(step, part, step == 0)
    v_moves = [spread(v, None, vs, vr, head) for head in range(heads)]
    q_put.wait()
    for move in q_there:
        move.wait_recv()
    owns[1].wait()
    for move in k_moves:
        move.wait_recv()
    store(qg_vm, qg, 5)
    store(kt_vm, kt, 6)
    lane = lax.broadcasted_iota(jnp.int32, (SPAN, 128), 1)
    length = kt_vm.shape[0] * kt_vm.shape[2]
    group_lanes = heads * nf

    @pl.loop(0, nd)
    def _(d):
        marks = jnp.zeros((SPAN, 128), jnp.float32)
        for f in range(nf):
            n = tab[d * nf + f]
            for h in range(heads):
                part = slice(h * HEAD_DIM, (h + 1) * HEAD_DIM)
                keys = kt_vm[:, n, :, part].reshape(length, HEAD_DIM)
                scores = dot(qg_vm[d, f, :, part], keys, NT) * SCALE
                peak = jnp.max(scores, axis=1, keepdims=True)
                expo = jnp.exp(scores - peak)
                probs[h, d * nf + f] = expo
                marks = jnp.where(lane == heads * f + h, peak, marks)
                total = jnp.sum(expo, axis=1, keepdims=True)
                marks = jnp.where(lane == group_lanes + heads * f + h, total, marks)
        st[d] = marks

    sib_moves[chips - 1].wait_recv()
    for move in ring_moves[2:]:
        move.wait_recv()

    @pl.loop(0, rows // SPAN)
    def _(i):
        at = pl.ds(pl.multiple_of(i * SPAN, SPAN), SPAN)
        value = mine[chips - 1, at, :] + sib_recv[chips - 1, at, :].astype(jnp.float32)
        for step in (0, 2):
            value += ring_recv[step, at, :].astype(jnp.float32)
        u_vm[i] = value.astype(jnp.bfloat16)

    u_there, u_put = deliver(1, lambda home, c: u_vm[home * spans + c], ug_vm, us, ur)
    owns[2].wait()
    for move in v_moves[0]:
        move.wait_recv()

    @pl.loop(0, nd)
    def _(d):
        for f in range(nf):
            values = vt_vm[0][:, tab[d * nf + f]].reshape(length, HEAD_DIM)
            expo = probs[0, d * nf + f].astype(jnp.bfloat16)
            o_send[d, f] = dot(expo, values, NN).astype(jnp.bfloat16)

    o_there = [
        remote(o_send.at[p], o_first.at[dp], oss.at[i], osr.at[i], "dp", p) for i, p in enumerate(peers)
    ]
    for move in o_there:
        move.start()
    store(o_send.at[dp], o_first.at[dp], 13)
    u_put.wait()
    for move in u_there:
        move.wait_recv()
    store(ug_vm, ug, 7)
    for h in range(heads):
        if h > 0:
            owns[2 + h].wait()
            for move in v_moves[h]:
                move.wait_recv()
        part = slice(h * HEAD_DIM, (h + 1) * HEAD_DIM)

        @pl.loop(0, nd)
        def _(d):
            marks = st[d]
            for f in range(nf):
                n = tab[d * nf + f]
                values = vt_vm[h][:, n].reshape(length, HEAD_DIM)
                dprobs = dot(ug_vm[d, f, :, part], values, NT)
                mean = jnp.sum(probs[h, d * nf + f] * dprobs, axis=1, keepdims=True)
                marks = jnp.where(lane == 2 * group_lanes + heads * f + h, mean, marks)
            st[d] = marks

    for h in range(heads):
        store(vt_vm[h], vt.at[:, :, :, pl.ds(h * HEAD_DIM, HEAD_DIM)], 8 + 4 * h)
    stats = [
        remote(st.at[p], st_home.at[dp], ss.at[i], sr.at[i], "dp", p) for i, p in enumerate(peers)
    ]
    for move in stats:
        move.start()
    st_put = pltpu.make_async_copy(st.at[dp], st_home.at[dp], own.at[9])
    st_put.start()
    row = lax.broadcasted_iota(jnp.int32, (1, 128), 1)
    place = lax.rem(row, group_lanes) // heads
    sources = []
    both = []
    for t in range(slots):
        values = jnp.zeros((1, 128), jnp.int32)
        for f in range(nf):
            values = jnp.where(place == f, src[t % SLOTS, (dp * nf + f) * spans + t // SLOTS], values)
        sources.append(values)
    for c in range(spans):
        values = jnp.zeros((1, 128), jnp.int32)
        for f in range(nf):
            values = jnp.where(place == f, cnt[(dp * nf + f) * spans + c], values)
        both.append(values > 1)
    st_put.wait()
    for move in stats:
        move.wait_recv()
    table = jnp.zeros((SPAN, 128), jnp.float32)
    scales = jnp.zeros((SPAN, 128), jnp.float32)
    for c in range(spans):
        pair = []
        for slot in range(SLOTS):
            found = jnp.zeros((SPAN, 128), jnp.float32)
            for g in range(nd):
                found = jnp.where(sources[SLOTS * c + slot] == g, st_home[g], found)
            pair.append(
                [found] + [pltpu.roll(found, 128 - group_lanes * i, axis=1) for i in (1, 2)]
            )
        (m0, l0, e0), (m1, l1, e1) = pair
        m1 = jnp.where(both[c], m1, -1e30)
        l1, e1 = jnp.where(both[c], l1, 0.0), jnp.where(both[c], e1, 0.0)
        peak = jnp.maximum(m0, m1)
        a0, a1 = jnp.exp(m0 - peak), jnp.exp(m1 - peak)
        total = a0 * l0 + a1 * l1
        log_total = peak + jnp.log(total)
        centre = (a0 * e0 + a1 * e1) / total
        for value, at in ((log_total, c * group_lanes), (centre, 64 + c * group_lanes)):
            moved = pltpu.roll(value, at, axis=1) if at else value
            inside = jnp.logical_and(lane >= at, lane < at + group_lanes)
            table = jnp.where(inside, moved, table)
        for slot, value in enumerate((a0 / total, a1 / total)):
            at = (SLOTS * c + slot) * group_lanes
            moved = pltpu.roll(value, at, axis=1) if at else value
            inside = jnp.logical_and(lane >= at, lane < at + group_lanes)
            scales = jnp.where(inside, moved, scales)
    weights[...] = scales
    hs[...] = table
    gives = [
        remote(hs, hs_out.at[dp], hsn.at[i], hr.at[i], "dp", p) for i, p in enumerate(peers)
    ]
    for move in gives:
        move.start()
    store(hs, hs_out.at[dp], 10)
    for move in q_moves + k_moves + list(sib_moves.values()) + ring_moves + q_there + u_there + stats + sum(v_moves, []):
        move.wait_send()
    for move in gives + o_there:
        move.wait()
    for put in puts:
        put.wait()


UNROLL = 4


def backward_kernel(
    nf, tab, q_any, u_any, hs_any, kt_any, vt_any, o_any, dq_any, dk_any, dv_any,
    q, u, hs, kt, vt, o_ref, dq_ref, dk_ref, dv_ref, k_acc, v_acc, listed, sems,
):
    pairs = ((q_any, q), (u_any, u), (hs_any, hs), (kt_any, kt), (vt_any, vt))
    loads = [pltpu.make_async_copy(a, b, sems.at[i]) for i, (a, b) in enumerate(pairs)]
    for copy in loads:
        copy.start()
    lane = lax.broadcasted_iota(jnp.int32, (SPAN, 128), 1)
    pieces, nbrs, piece = kt.shape[0], kt.shape[1], kt.shape[2]
    length = pieces * piece
    heads = kt.shape[3] // HEAD_DIM
    refs = q.shape[0]

    def place(r, ends):
        low, high = ends
        live = tab[2 * refs + r]
        listed[jnp.where(live > 0, low, high)] = r
        return low + live, high - 1 + live

    count, _ = lax.fori_loop(0, refs, place, (jnp.int32(0), jnp.int32(refs - 1)))

    @pl.loop(0, nbrs)
    def _(n):
        k_acc[n] = jnp.zeros(k_acc.shape[1:], jnp.float32)
        v_acc[n] = jnp.zeros(v_acc.shape[1:], jnp.float32)

    for copy in loads:
        copy.wait()

    def pick(array, at):
        return jnp.sum(jnp.where(lane == at, array, 0.0), axis=1, keepdims=True)

    @pl.loop(0, (count + UNROLL - 1) // UNROLL)
    def _(step):
        items = []
        for more in range(UNROLL):
            r = listed[step * UNROLL + more]
            n, c, live = tab[r], tab[refs + r], tab[2 * refs + r]
            into = jnp.where(live > 0, n, nbrs)
            items.append((r, n, into, heads * (nf * c + r % nf)))
        pairs = [(i, h) for i in range(UNROLL) for h in range(heads)]
        parts = [slice(h * HEAD_DIM, (h + 1) * HEAD_DIM) for h in range(heads)]

        def rows_of(ref, i, h):
            return ref[:, items[i][1], :, parts[h]].reshape(length, HEAD_DIM)

        def mark(i, h, offset):
            return pick(hs[items[i][0] // nf], offset + items[i][3] + h)

        scores = [dot(q[items[i][0], :, parts[h]], rows_of(kt, i, h), NT) for i, h in pairs]
        dprobs = [dot(u[items[i][0], :, parts[h]], rows_of(vt, i, h), NT) for i, h in pairs]
        probs = [jnp.exp(s * SCALE - mark(i, h, 0)) for s, (i, h) in zip(scores, pairs)]
        rounded = [value.astype(jnp.bfloat16) for value in probs]
        slopes = [
            (value * (d - mark(i, h, 64)) * SCALE).astype(jnp.bfloat16)
            for value, d, (i, h) in zip(probs, dprobs, pairs)
        ]
        for value, (i, h) in zip(rounded, pairs):
            if h > 0:
                o_ref[items[i][0]] = dot(value, rows_of(vt, i, h), NN).astype(jnp.bfloat16)
        dqs = [dot(value, rows_of(kt, i, h), NN) for value, (i, h) in zip(slopes, pairs)]
        for value, (i, h) in zip(dqs, pairs):
            dq_ref[items[i][0], :, parts[h]] = value.astype(jnp.bfloat16)
        dks = [dot(value, q[items[i][0], :, parts[h]], TN) for value, (i, h) in zip(slopes, pairs)]
        for value, (i, h) in zip(dks, pairs):
            k_acc[items[i][2], :, parts[h]] += value
        dvs = [dot(value, u[items[i][0], :, parts[h]], TN) for value, (i, h) in zip(rounded, pairs)]
        for value, (i, h) in zip(dvs, pairs):
            v_acc[items[i][2], :, parts[h]] += value

    puts = [
        pltpu.make_async_copy(o_ref, o_any, sems.at[5]),
        pltpu.make_async_copy(dq_ref, dq_any, sems.at[6]),
    ]
    for put in puts:
        put.start()
    for i, (acc, out, put_to) in enumerate(((k_acc, dk_ref, dk_any), (v_acc, dv_ref, dv_any))):
        @pl.loop(0, nbrs)
        def _(n):
            out[:, n] = acc[n].reshape(pieces, piece, -1).astype(jnp.bfloat16)

        put = pltpu.make_async_copy(out, put_to, sems.at[7 + i])
        put.start()
        puts.append(put)
    for put in puts:
        put.wait()


def finish_kernel(*refs):
    count = len(refs) // 3
    sems = refs[-1]
    takes = []
    for i in range(count):
        source, held = refs[i], refs[2 * count + i]
        pieces = 4 if source.shape[0] % 4 == 0 else 1
        size = source.shape[0] // pieces
        for j in range(pieces):
            part = pl.ds(j * size, size)
            take = pltpu.make_async_copy(source.at[part], held.at[part], sems.at[0, i, j])
            take.start()
            takes.append((i, j, part, take))
    puts = []
    for i, j, part, take in takes:
        take.wait()
        put = pltpu.make_async_copy(refs[2 * count + i].at[part], refs[count + i].at[part], sems.at[1, i, j])
        put.start()
        puts.append(put)
    for put in puts:
        put.wait()


def return_kernel(
    nd, nf, width, spans, src, cnt, weights, o_first, o, cot, dq, dk, dv, ga_out, gq, gk, gv, gp, att_all,
    o_a, o_b, dq_home, dq_sum, k_own, v_own, cot_vm, term, first_z, first_x, second, middle, keep, total,
    os, orr, qs, qr, ks, kr, vs, vr, ys, yr, fa, ga, ba, ca, ts, tr, own, load, last_sem,
):
    dp, fs = lax.axis_index("dp"), lax.axis_index("fsdp")
    chips = nf // 2
    chip, core = fs // 2, lax.rem(fs, 2)
    sibling = chip * 2 + 1 - core
    load_cot = pltpu.make_async_copy(cot, cot_vm, load.at[0])
    load_cot.start()
    enter((("dp", nd), ("fsdp", nf)))
    peers = [lax.rem(dp + step, nd) for step in range(1, nd)]
    firsts = [
        pltpu.make_async_copy(o_first, o_a, own.at[6]),
        pltpu.make_async_copy(o.at[dp], o_b.at[dp], own.at[7]),
        pltpu.make_async_copy(dq.at[dp], dq_home.at[dp], own.at[0]),
        pltpu.make_async_copy(dk.at[fs], k_own, own.at[1]),
        pltpu.make_async_copy(dv.at[fs], v_own, own.at[2]),
    ]
    for copy in firsts:
        copy.start()
    outs = [
        remote(o.at[p], o_b.at[dp], os.at[i], orr.at[i], "dp", p) for i, p in enumerate(peers)
    ]
    backs = [
        remote(dq.at[p], dq_home.at[dp], qs.at[i], qr.at[i], "dp", p) for i, p in enumerate(peers)
    ]
    for move in outs + backs:
        move.start()
    moves = []

    nbrs = dk.shape[1]
    early = nbrs // 3

    def give(ref, out, s_sem, r_sem, start, size, base):
        here = pl.ds(start, size)
        for step in range(1, nf):
            peer = lax.rem(fs + step, nf)
            at = pl.ds(pl.multiple_of(fs * width, width), width)
            place = base + step
            move = remote(ref.at[peer, here], out.at[here, :, at], s_sem.at[place], r_sem.at[place], "fsdp", peer)
            move.start()
            moves.append(move)

    for copy in firsts:
        copy.wait()
    puts = [
        pltpu.make_async_copy(k_own, cols(gk, fs, width), own.at[3]),
        pltpu.make_async_copy(v_own, cols(gv, fs, width), own.at[4]),
    ]
    for put in puts:
        put.start()

    def add_slots(home, place, c, parts):
        span = (dp * nf + home) * spans + c
        first = parts[src[0, span], place].astype(jnp.float32)
        second = parts[src[1, span], place].astype(jnp.float32)
        both = cnt[span] > 1
        return (first + jnp.where(both, second, 0.0)).astype(jnp.bfloat16)

    to_sibling, around = [], {}
    lane = lax.broadcasted_iota(jnp.int32, (SPAN, 128), 1)
    table = weights[...]
    heads = width // HEAD_DIM

    def head_of(block, h):
        return att_all.at[block, :, pl.ds(h * HEAD_DIM, HEAD_DIM)]

    def weigh(home, c):
        span = (dp * nf + home) * spans + c
        value = jnp.zeros((SPAN, HEAD_DIM), jnp.float32)
        for slot in range(SLOTS):
            at = heads * (nf * (SLOTS * c + slot) + home)
            scale = jnp.sum(jnp.where(lane == at, table, 0.0), axis=1, keepdims=True)
            part = scale * o_a[src[slot, span], home].astype(jnp.float32)
            value += part if slot == 0 else jnp.where(cnt[span] > slot, part, 0.0)
        return value.astype(jnp.bfloat16)

    for h in range(heads):
        if h > 0:
            for move in outs:
                move.wait_recv()

        @pl.loop(0, nf)
        def _(home):
            for c in range(spans):
                at = pl.multiple_of((home * spans + c) * SPAN, SPAN)
                value = weigh(home, c) if h == 0 else add_slots(home, home, c, o_b)
                att_all[fs, pl.ds(at, SPAN), h * HEAD_DIM : (h + 1) * HEAD_DIM] = value

        att = head_of(fs, h)
        move = remote(att, att, fa.at[chips - 1 + h], ga.at[chips - 1 + h], "fsdp", sibling)
        move.start()
        to_sibling.append(move)
        for step in (0, chips - 2):
            there = lax.rem(chip + step + 1, chips) * 2 + core
            place = h * (chips - 1) + step
            move = remote(att, att, ba.at[place], ca.at[place], "fsdp", there)
            move.start()
            around[h, step] = move
        give(dk, gk, ks, kr, h * early, early, h * nf)
    load_cot.wait()
    share = width // nd
    columns = cot_vm.shape[1]
    tile = 256

    def add_dq():
        for move in backs:
            move.wait_recv()

        @pl.loop(0, nf)
        def _(home):
            for c in range(spans):
                dq_sum[home, c] = add_slots(home, home, c, dq_home)

        for step in range(1, nf):
            peer = lax.rem(fs + step, nf)
            move = remote(dq_sum.at[peer], cols(gq, fs, width), ys.at[step], yr.at[step], "fsdp", peer)
            move.start()
            moves.append(move)
        put = pltpu.make_async_copy(dq_sum.at[fs], cols(gq, fs, width), own.at[5])
        put.start()
        puts.append(put)

    nz = nd // 2
    x_at, z_at = dp // nz, lax.rem(dp, nz)
    across = lax.rem(dp + nz, nd)
    z_places = [lax.rem(z_at + step, nz) for step in range(1, nz)]
    z_peers = [x_at * nz + place for place in z_places]
    blocks = []
    flying = {}

    def along_z(turn):
        return turn % 2 == 0

    def launch(turn, stage, copies):
        sent = []
        for i, (source, target, peer) in enumerate(copies):
            place = stage * (nz - 1) + i
            move = remote(source, target, ts.at[turn, place], tr.at[turn, place], "dp", peer)
            move.start()
            sent.append(move)
        flying[turn, stage] = sent

    def arrive(turn, stage):
        for move in flying[turn, stage]:
            move.wait_recv()

    def project(turn, block):
        blocks.append(block)

        @pl.loop(0, columns // tile)
        def _(t):
            at = pl.ds(pl.multiple_of(t * tile, tile), tile)
            value = dot(att_all[block], cot_vm[:, at], TN).astype(jnp.bfloat16)
            term[turn, :, :, at] = value.reshape(nd, share, tile)

        half = turn // 2
        if along_z(turn):
            launch(turn, 0, [
                (term.at[turn, pl.ds(2 * place, 2)], first_z.at[half, i], p)
                for i, (place, p) in enumerate(zip(z_places, z_peers))
            ])
        else:
            launch(turn, 0, [(term.at[turn, pl.ds((1 - x_at) * nz, nz)], first_x.at[half], across)])

    def add_first(turn):
        arrive(turn, 0)
        half = turn // 2
        if along_z(turn):
            def total_of(place):
                value = term[turn, 2 * z_at + place].astype(jnp.float32)
                for i in range(nz - 1):
                    value += first_z[half, i, place].astype(jnp.float32)
                return value

            keep[turn] = total_of(x_at)
            middle[turn, 0] = total_of(1 - x_at).astype(jnp.bfloat16)
            launch(turn, 1, [(middle.at[turn, 0], second.at[turn, 0], across)])
        else:
            def total_of(place):
                value = term[turn, x_at * nz + place].astype(jnp.float32)
                return value + first_x[half, place].astype(jnp.float32)

            keep[turn] = total_of(z_at)
            for i, place in enumerate(z_places):
                middle[turn, i] = total_of(place).astype(jnp.bfloat16)
            launch(turn, 1, [
                (middle.at[turn, i], second.at[turn, i], p) for i, p in enumerate(z_peers)
            ])

    def rows_of(turn, part, parts):
        start = pl.multiple_of(blocks[turn] * width + part * share, share)
        return gp.at[pl.ds(start, parts * share)]

    owned = {}

    def add_second(turn):
        arrive(turn, 1)
        value = keep[turn]
        for i in range(len(flying[turn, 1])):
            value += second[turn, i].astype(jnp.float32)
        total[turn] = value.astype(jnp.bfloat16)
        part = 2 * z_at + x_at if along_z(turn) else dp
        here = rows_of(turn, part, 1)
        owned[turn] = pltpu.make_async_copy(total.at[turn], here, load.at[1 + turn])
        owned[turn].start()
        to = [across] if along_z(turn) else z_peers
        launch(turn, 2, [(total.at[turn], here, p) for p in to])

    def share_all(turn):
        owned[turn].wait()
        arrive(turn, 2)
        if along_z(turn):
            here = rows_of(turn, 2 * z_at, 2)
            launch(turn, 3, [(here, here, p) for p in z_peers])
        else:
            here = rows_of(turn, x_at * nz, nz)
            launch(turn, 3, [(here, here, across)])

    def advance(turn):
        for lag, act in ((2, add_first), (3, add_second), (4, share_all)):
            if 0 <= turn - lag < nf:
                act(turn - lag)

    project(0, fs)
    for move in to_sibling[:2]:
        move.wait_recv()
    project(1, sibling)
    for h, step in ((0, 0), (1, chips - 2)):
        for each in range(heads):
            around[each, step].wait_recv()
        back = lax.rem(chip + chips - step - 1, chips) * 2 + core
        there = lax.rem(chip + step + 1, chips) * 2 + core
        place = h * (chips - 1) + 1
        held = head_of(back, h)
        around[h, 1] = remote(held, held, ba.at[place], ca.at[place], "fsdp", there)
        around[h, 1].start()
    give(dk, gk, ks, kr, heads * early, nbrs - heads * early, heads * nf)
    give(dv, gv, vs, vr, 0, nbrs, 0)
    turn = 2
    order = [0, chips - 2] + list(range(1, chips - 2))
    for step in order:
        back = lax.rem(chip + chips - step - 1, chips) * 2
        if step == 1:
            for each in range(heads):
                around[each, 1].wait_recv()
        move = remote(
            att_all.at[back + core], att_all.at[back + core], fa.at[step], ga.at[step], "fsdp", sibling
        )
        move.start()
        to_sibling.append(move)
        project(turn, back + core)
        advance(turn)
        move.wait_recv()
        project(turn + 1, back + 1 - core)
        advance(turn + 1)
        if turn == 4:
            add_dq()
        turn += 2
    for later in range(turn, turn + 4):
        advance(later)
    tokens = spans * SPAN
    for block in range(nf):
        here = pl.ds(pl.multiple_of(fs * tokens, tokens), tokens)
        put = pltpu.make_async_copy(
            att_all.at[block, here], ga_out.at[:, pl.ds(block * width, width)], last_sem.at[block]
        )
        put.start()
        puts.append(put)
    for move in outs + backs + to_sibling + list(around.values()):
        move.wait_send()
    for (_, stage), sent in flying.items():
        for move in sent:
            if stage == 3:
                move.wait_recv()
            move.wait_send()
    for move in moves:
        move.wait()
    for put in puts:
        put.wait()


def dma(*shape):
    return pltpu.SemaphoreType.DMA(shape)


def comm(number, mib=BIG):
    return pltpu.CompilerParams(collective_id=number, has_side_effects=True, vmem_limit_bytes=mib)


def local(queries, nbr_keys, nbr_values, out_proj, nbr_source, nbr_index, nbr_count, cotangent):
    nd, nf = lax.axis_size("dp"), lax.axis_size("fsdp")
    bf, f32, i32 = jnp.bfloat16, jnp.float32, jnp.int32
    token_rows, full_width = queries.shape
    spans = token_rows // SPAN
    nbrs, piece, _ = nbr_keys.shape
    width = full_width // nf
    rows, columns = cotangent.shape
    refs_all = nd * nf
    chips = nf // 2
    sources, indices = nbr_source.T, nbr_index.T
    share = width // nd

    kt, vt, qg, ug, hs, tab, o_first, weights = pl.pallas_call(
        lambda *a: spread_kernel(nd, nf, width, *a),
        in_specs=[SM, SM, SM, ANY, ANY, ANY, ANY, ANY],
        out_specs=[ANY, ANY, ANY, ANY, ANY, SM, ANY, VM],
        out_shape=[
            jax.ShapeDtypeStruct((nf, nbrs, piece, width), bf),
            jax.ShapeDtypeStruct((nf, nbrs, piece, width), bf),
            jax.ShapeDtypeStruct((nd, nf, SPAN, width), bf),
            jax.ShapeDtypeStruct((nd, nf, SPAN, width), bf),
            jax.ShapeDtypeStruct((nd, SPAN, 128), f32),
            jax.ShapeDtypeStruct((3 * refs_all,), i32),
            jax.ShapeDtypeStruct((nd, nf, SPAN, HEAD_DIM), bf),
            jax.ShapeDtypeStruct((SPAN, 128), f32),
        ],
        scratch_shapes=[
            pltpu.VMEM((nf, spans, SPAN, width), bf),
            pltpu.VMEM((2, nd, nf, SPAN, width), bf),
            pltpu.VMEM((nf, nbrs, piece, width), bf),
            pltpu.VMEM((nf, nbrs, piece, HEAD_DIM), bf),
            pltpu.VMEM((nf, nbrs, piece, HEAD_DIM), bf),
            pltpu.VMEM((nd, nf, SPAN, width), bf),
            pltpu.VMEM((nd, nf, SPAN, width), bf),
            pltpu.VMEM((nf * spans, SPAN, width), bf),
            pltpu.VMEM((rows, columns), bf),
            pltpu.VMEM((full_width, columns), bf),
            pltpu.VMEM((chips, rows, width), bf),
            pltpu.VMEM((chips, rows, width), bf),
            pltpu.VMEM((chips, rows, width), f32),
            pltpu.VMEM((chips - 1, rows, width), bf),
            pltpu.VMEM((chips - 1, rows, width), bf),
            pltpu.VMEM((width // HEAD_DIM, refs_all, SPAN, nf * piece), f32),
            pltpu.VMEM((nd, SPAN, 128), f32),
            pltpu.VMEM((nd, SPAN, 128), f32),
            pltpu.VMEM((SPAN, 128), f32),
            pltpu.SMEM((refs_all,), i32),
            pltpu.VMEM((nd, nf, SPAN, HEAD_DIM), bf),
            dma(nf), dma(nf), dma(2 * nf), dma(2 * nf), dma(2 * nf), dma(2 * nf), dma(nd), dma(nd), dma(nd), dma(nd),
            dma(chips), dma(chips), dma(6), dma(6), dma(nd), dma(nd), dma(nd), dma(nd), dma(nd), dma(nd), dma(14), dma(2),
        ],
        compiler_params=comm(1),
        name="spread",
    )(
        sources, indices, nbr_count, queries.reshape(spans, SPAN, full_width), nbr_keys, nbr_values,
        cotangent, out_proj,
    )

    o, dq, dk, dv = pl.pallas_call(
        lambda *a: backward_kernel(nf, *a),
        in_specs=[SM, ANY, ANY, ANY, ANY, ANY],
        out_specs=[ANY, ANY, ANY, ANY],
        out_shape=[
            jax.ShapeDtypeStruct((refs_all, SPAN, HEAD_DIM), bf),
            jax.ShapeDtypeStruct((refs_all, SPAN, width), bf),
            jax.ShapeDtypeStruct((nf, nbrs, piece, width), bf),
            jax.ShapeDtypeStruct((nf, nbrs, piece, width), bf),
        ],
        scratch_shapes=[
            pltpu.VMEM((refs_all, SPAN, width), bf),
            pltpu.VMEM((refs_all, SPAN, width), bf),
            pltpu.VMEM((nd, SPAN, 128), f32),
            pltpu.VMEM((nf, nbrs, piece, width), bf),
            pltpu.VMEM((nf, nbrs, piece, width), bf),
            pltpu.VMEM((refs_all, SPAN, HEAD_DIM), bf),
            pltpu.VMEM((refs_all, SPAN, width), bf),
            pltpu.VMEM((nf, nbrs, piece, width), bf),
            pltpu.VMEM((nf, nbrs, piece, width), bf),
            pltpu.VMEM((nbrs + 1, nf * piece, width), f32),
            pltpu.VMEM((nbrs + 1, nf * piece, width), f32),
            pltpu.SMEM((refs_all,), i32),
            dma(9),
        ],
        compiler_params=pltpu.CompilerParams(vmem_limit_bytes=BIG),
        name="backward",
    )(tab, qg.reshape(refs_all, SPAN, width), ug.reshape(refs_all, SPAN, width), hs, kt, vt)

    attended, gq, gk, gv, grad_proj = pl.pallas_call(
        lambda *a: return_kernel(nd, nf, width, spans, *a),
        in_specs=[SM, SM, VM, ANY, ANY, ANY, ANY, ANY, ANY],
        out_specs=[ANY, ANY, ANY, ANY, ANY],
        out_shape=[
            jax.ShapeDtypeStruct((token_rows, full_width), bf),
            jax.ShapeDtypeStruct((spans, SPAN, full_width), bf),
            jax.ShapeDtypeStruct((nbrs, piece, full_width), bf),
            jax.ShapeDtypeStruct((nbrs, piece, full_width), bf),
            jax.ShapeDtypeStruct((full_width, columns), bf),
        ],
        scratch_shapes=[
            pltpu.VMEM((nf, rows, width), bf),
            pltpu.VMEM((nd, nf, SPAN, HEAD_DIM), bf),
            pltpu.VMEM((nd, nf, SPAN, HEAD_DIM), bf),
            pltpu.VMEM((nd, nf, SPAN, width), bf),
            pltpu.VMEM((nf, spans, SPAN, width), bf),
            pltpu.VMEM((nbrs, piece, width), bf),
            pltpu.VMEM((nbrs, piece, width), bf),
            pltpu.VMEM((rows, columns), bf),
            pltpu.VMEM((nf, nd, share, columns), bf),
            pltpu.VMEM((nf // 2, nd // 2 - 1, 2, share, columns), bf),
            pltpu.VMEM((nf // 2, nd // 2, share, columns), bf),
            pltpu.VMEM((nf, nd // 2 - 1, share, columns), bf),
            pltpu.VMEM((nf, nd // 2 - 1, share, columns), bf),
            pltpu.VMEM((nf, share, columns), f32),
            pltpu.VMEM((nf, share, columns), bf),
            dma(nd), dma(nd), dma(nd), dma(nd), dma(3 * nf), dma(3 * nf), dma(nf), dma(nf), dma(nf), dma(nf),
            dma(chips + 1), dma(chips + 1), dma(2 * chips), dma(2 * chips),
            dma(nf, 2 * nd), dma(nf, 2 * nd), dma(8), dma(1 + nf), dma(nf),
        ],
        compiler_params=comm(3),
        name="giveback",
    )(
        sources, nbr_count, weights, o_first, o.reshape(nd, nf, SPAN, HEAD_DIM), cotangent,
        dq.reshape(nd, nf, SPAN, width), dk, dv,
    )
    results = [grad_proj, gk, gv, attended, gq.reshape(token_rows, full_width)]
    grad_proj, gk, gv, attended, gq = pl.pallas_call(
        finish_kernel,
        in_specs=[ANY] * len(results),
        out_specs=[ANY] * len(results),
        out_shape=[jax.ShapeDtypeStruct(value.shape, value.dtype) for value in results],
        scratch_shapes=[pltpu.VMEM(value.shape, value.dtype) for value in results] + [dma(2, len(results), 4)],
        compiler_params=pltpu.CompilerParams(vmem_limit_bytes=BIG),
        name="finish",
    )(*results)
    return (attended, gq, gk, gv, grad_proj)


def solution(mesh):
    placed = (
        P(("dp", "fsdp"), "enc"),
        P("dp", "fsdp", "enc"),
        P("dp", "fsdp", "enc"),
        P("enc", "fsdp"),
        P(),
        P(),
        P(),
        P("dp", "fsdp"),
    )
    return jax.shard_map(
        local,
        mesh=mesh,
        in_specs=placed,
        out_specs=(
            P(("dp", "fsdp"), "enc"),
            P(("dp", "fsdp"), "enc"),
            P("dp", "fsdp", "enc"),
            P("dp", "fsdp", "enc"),
            P("enc", "fsdp"),
        ),
        check_vma=False,
    )
```

```python
import math

import jax
import jax.numpy as jnp
from jax import lax
from jax.experimental import pallas as pl
from jax.experimental.pallas import tpu as pltpu
from jax.sharding import PartitionSpec as P

HEAD_DIM = 128
SPAN = 64
SLOTS = 2
MESH = pl.DeviceIdType.MESH
ANY = pl.BlockSpec(memory_space=pl.ANY)
VM = pl.BlockSpec(memory_space=pltpu.VMEM)
SM = pl.BlockSpec(memory_space=pltpu.SMEM)
NT = (((1,), (1,)), ((), ()))
TN = (((0,), (0,)), ((), ()))
NN = (((1,), (0,)), ((), ()))
SCALE = 1.0 / math.sqrt(HEAD_DIM)
BIG = 60 << 20


def dot(a, b, dims):
    return lax.dot_general(a, b, dims, preferred_element_type=jnp.float32)


def enter(axes):
    barrier = pltpu.get_barrier_semaphore()
    total = 0
    for axis, size in axes:
        here = lax.axis_index(axis)
        for step in range(1, size):
            pl.semaphore_signal(
                barrier, inc=1, device_id={axis: lax.rem(here + step, size)}, device_id_type=MESH
            )
            total += 1
    pl.semaphore_wait(barrier, total)


def remote(src, dst, send, recv, axis, peer):
    return pltpu.make_async_remote_copy(
        src_ref=src, dst_ref=dst, send_sem=send, recv_sem=recv, device_id={axis: peer}, device_id_type=MESH
    )


def cols(ref, place, width):
    return ref.at[:, :, pl.ds(pl.multiple_of(place * width, width), width)]


def spread_kernel(
    nd, nf, width, src, idx, cnt, q, k, v, cot, proj, kt, vt, qg, ug, hs_out, tab, o_first, weights,
    q_heads, send, kt_vm, vt_a, vt_b, qg_vm, ug_vm, u_vm, cot_vm, proj_vm, sib_send, sib_recv, mine, ring_send,
    ring_recv, probs, st, st_home, hs, sel, o_send,
    qs, qr, ks, kr, vs, vr, gs, gr, us, ur, bs, br, rs, rr, ss, sr, hsn, hr, oss, osr, own, load,
):
    dp, fs = lax.axis_index("dp"), lax.axis_index("fsdp")
    chips = nf // 2
    chip, core = fs // 2, lax.rem(fs, 2)
    sibling = chip * 2 + 1 - core
    spans = q_heads.shape[1]
    slots = SLOTS * spans
    heads = width // HEAD_DIM
    peers = [lax.rem(dp + step, nd) for step in range(1, nd)]
    loads = [
        pltpu.make_async_copy(cot, cot_vm, load.at[0]),
        pltpu.make_async_copy(proj, proj_vm, load.at[1]),
    ]
    for copy in loads:
        copy.start()
    enter((("dp", nd), ("fsdp", nf)))
    vt_vm = (vt_a, vt_b)

    def v_part(place, head):
        at = pl.multiple_of(place * width + head * HEAD_DIM, HEAD_DIM)
        return v.at[:, :, pl.ds(at, HEAD_DIM)]

    owns = [
        pltpu.make_async_copy(cols(q, fs, width), q_heads.at[fs], own.at[0]),
        pltpu.make_async_copy(cols(k, fs, width), kt_vm.at[fs], own.at[1]),
    ] + [
        pltpu.make_async_copy(v_part(fs, head), vt_vm[head].at[fs], own.at[(2, 11)[head]]) for head in range(heads)
    ]
    for copy in owns:
        copy.start()

    def spread(ref, out, s_sem, r_sem, head=None):
        moves = []
        for step in range(1, nf):
            peer = lax.rem(fs + step, nf)
            if head is None:
                source, target, place = cols(ref, peer, width), out.at[fs], step
            else:
                source, target = v_part(peer, head), vt_vm[head].at[fs]
                place = head * nf + step
            move = remote(source, target, s_sem.at[place], r_sem.at[place], "fsdp", peer)
            move.start()
            moves.append(move)
        return moves

    q_moves = spread(q, q_heads, qs, qr)
    nbr_half = kt_vm.shape[1] // 2

    def spread_keys(part):
        here = pl.ds(part * nbr_half, nbr_half)
        moves = []
        for step in range(1, nf):
            peer = lax.rem(fs + step, nf)
            at = pl.ds(pl.multiple_of(peer * width, width), width)
            place = part * nf + step
            move = remote(k.at[here, :, at], kt_vm.at[fs, here], ks.at[place], kr.at[place], "fsdp", peer)
            move.start()
            moves.append(move)
        return moves

    k_moves = spread_keys(0)
    for copy in loads:
        copy.wait()
    rows = cot_vm.shape[0]
    tile = 512
    sib_moves = {}
    for turn, step in enumerate((1, 0, 2, 3)):
        there = lax.rem(chip + step + 1, chips)
        for which in (1 - core, core):
            block = pl.multiple_of((there * 2 + which) * width, width)
            first = len(sib_moves) == turn

            @pl.loop(0, rows // tile)
            def _(t):
                at = pl.multiple_of(t * tile, tile)
                value = dot(cot_vm[pl.ds(at, tile), :], proj_vm[pl.ds(block, width), :], NT)
                if first:
                    sib_send[step, pl.ds(at, tile), :] = value.astype(jnp.bfloat16)
                else:
                    mine[step, pl.ds(at, tile), :] = value

            if first:
                move = remote(sib_send.at[step], sib_recv.at[step], bs.at[step], br.at[step], "fsdp", sibling)
                move.start()
                sib_moves[step] = move
    half = rows // 2
    piece = 256
    halves = [pl.ds(0, half), pl.ds(half, half)]
    ring_moves = []

    def add_part(step, part, relayed):
        @pl.loop(0, half // piece)
        def _(t):
            at = pl.ds(pl.multiple_of(part * half + t * piece, piece), piece)
            value = mine[step, at, :] + sib_recv[step, at, :].astype(jnp.float32)
            if relayed:
                value += ring_recv[1, at, :].astype(jnp.float32)
            ring_send[step, at, :] = value.astype(jnp.bfloat16)

    def pass_on(step, part, forward):
        there = lax.rem(chip + (1 if forward else chips - 1), chips) * 2 + core
        here = halves[part]
        place = len(ring_moves)
        move = remote(
            ring_send.at[step, here], ring_recv.at[step, here], rs.at[place], rr.at[place], "fsdp", there
        )
        move.start()
        ring_moves.append(move)

    sib_moves[1].wait_recv()
    for part in (0, 1):
        add_part(1, part, False)
        pass_on(1, part, part == 0)
    sib_moves[0].wait_recv()
    add_part(0, 1, False)
    pass_on(0, 1, True)
    sib_moves[2].wait_recv()
    add_part(2, 0, False)
    pass_on(2, 0, False)
    k_moves += spread_keys(1)

    @pl.loop(0, nd)
    def _(group):
        @pl.loop(0, nf)
        def _(home):
            base = (dp * nf + home) * spans
            span = jnp.int32(0)
            for t in range(slots):
                span = jnp.where(src[t % SLOTS, base + t // SLOTS] == group, t // SLOTS, span)
            sel[group * nf + home] = span
            r = group * nf + home
            number, where, live = jnp.int32(0), jnp.int32(0), jnp.int32(0)
            for t in range(slots):
                hit = jnp.logical_and(
                    src[t % SLOTS, r * spans + t // SLOTS] == dp,
                    t % SLOTS < cnt[r * spans + t // SLOTS],
                )
                number = jnp.where(hit, idx[t % SLOTS, r * spans + t // SLOTS], number)
                where = jnp.where(hit, t // SLOTS, where)
                live = jnp.where(hit, 1, live)
            tab[r] = number
            tab[nd * nf + r] = where
            tab[2 * nd * nf + r] = live

    owns[0].wait()
    for move in q_moves:
        move.wait_recv()
    puts = []

    def deliver(kind, source, out, s_sem, r_sem):
        @pl.loop(0, nd)
        def _(group):
            @pl.loop(0, nf)
            def _(home):
                send[kind, group, home] = source(home, sel[group * nf + home])

        moves = [
            remote(send.at[kind, p], out.at[dp], s_sem.at[i], r_sem.at[i], "dp", p)
            for i, p in enumerate(peers)
        ]
        for move in moves:
            move.start()
        put = pltpu.make_async_copy(send.at[kind, dp], out.at[dp], own.at[3 + kind])
        put.start()
        return moves, put

    def store(source, out, number):
        put = pltpu.make_async_copy(source, out, own.at[number])
        put.start()
        puts.append(put)

    q_there, q_put = deliver(0, lambda home, c: q_heads[home, c], qg_vm, gs, gr)
    for part, step in ((0, 0), (1, 2)):
        ring_moves[part].wait_recv()
        add_part(step, part, True)
        pass_on(step, part, step == 0)
    v_moves = [spread(v, None, vs, vr, head) for head in range(heads)]
    q_put.wait()
    for move in q_there:
        move.wait_recv()
    owns[1].wait()
    for move in k_moves:
        move.wait_recv()
    store(qg_vm, qg, 5)
    store(kt_vm, kt, 6)
    lane = lax.broadcasted_iota(jnp.int32, (SPAN, 128), 1)
    length = kt_vm.shape[0] * kt_vm.shape[2]
    group_lanes = heads * nf

    @pl.loop(0, nd)
    def _(d):
        marks = jnp.zeros((SPAN, 128), jnp.float32)
        for f in range(nf):
            n = tab[d * nf + f]
            for h in range(heads):
                part = slice(h * HEAD_DIM, (h + 1) * HEAD_DIM)
                keys = kt_vm[:, n, :, part].reshape(length, HEAD_DIM)
                scores = dot(qg_vm[d, f, :, part], keys, NT) * SCALE
                peak = jnp.max(scores, axis=1, keepdims=True)
                expo = jnp.exp(scores - peak)
                probs[h, d * nf + f] = expo
                marks = jnp.where(lane == heads * f + h, peak, marks)
                total = jnp.sum(expo, axis=1, keepdims=True)
                marks = jnp.where(lane == group_lanes + heads * f + h, total, marks)
        st[d] = marks

    sib_moves[chips - 1].wait_recv()
    for move in ring_moves[2:]:
        move.wait_recv()

    @pl.loop(0, rows // SPAN)
    def _(i):
        at = pl.ds(pl.multiple_of(i * SPAN, SPAN), SPAN)
        value = mine[chips - 1, at, :] + sib_recv[chips - 1, at, :].astype(jnp.float32)
        for step in (0, 2):
            value += ring_recv[step, at, :].astype(jnp.float32)
        u_vm[i] = value.astype(jnp.bfloat16)

    u_there, u_put = deliver(1, lambda home, c: u_vm[home * spans + c], ug_vm, us, ur)
    owns[2].wait()
    for move in v_moves[0]:
        move.wait_recv()

    @pl.loop(0, nd)
    def _(d):
        for f in range(nf):
            values = vt_vm[0][:, tab[d * nf + f]].reshape(length, HEAD_DIM)
            expo = probs[0, d * nf + f].astype(jnp.bfloat16)
            o_send[d, f] = dot(expo, values, NN).astype(jnp.bfloat16)

    o_there = [
        remote(o_send.at[p], o_first.at[dp], oss.at[i], osr.at[i], "dp", p) for i, p in enumerate(peers)
    ]
    for move in o_there:
        move.start()
    store(o_send.at[dp], o_first.at[dp], 13)
    u_put.wait()
    for move in u_there:
        move.wait_recv()
    store(ug_vm, ug, 7)
    for h in range(heads):
        if h > 0:
            owns[2 + h].wait()
            for move in v_moves[h]:
                move.wait_recv()
        part = slice(h * HEAD_DIM, (h + 1) * HEAD_DIM)

        @pl.loop(0, nd)
        def _(d):
            marks = st[d]
            dprobs = [
                dot(ug_vm[d, f, :, part], vt_vm[h][:, tab[d * nf + f]].reshape(length, HEAD_DIM), NT)
                for f in range(nf)
            ]
            means = [
                jnp.sum(probs[h, d * nf + f] * dprobs[f], axis=1, keepdims=True) for f in range(nf)
            ]
            for f, mean in enumerate(means):
                marks = jnp.where(lane == 2 * group_lanes + heads * f + h, mean, marks)
            st[d] = marks

    for h in range(heads):
        store(vt_vm[h], vt.at[:, :, :, pl.ds(h * HEAD_DIM, HEAD_DIM)], 8 + 4 * h)
    stats = [
        remote(st.at[p], st_home.at[dp], ss.at[i], sr.at[i], "dp", p) for i, p in enumerate(peers)
    ]
    for move in stats:
        move.start()
    st_put = pltpu.make_async_copy(st.at[dp], st_home.at[dp], own.at[9])
    st_put.start()
    row = lax.broadcasted_iota(jnp.int32, (1, 128), 1)
    place = lax.rem(row, group_lanes) // heads
    sources = []
    both = []
    for t in range(slots):
        values = jnp.zeros((1, 128), jnp.int32)
        for f in range(nf):
            values = jnp.where(place == f, src[t % SLOTS, (dp * nf + f) * spans + t // SLOTS], values)
        sources.append(values)
    for c in range(spans):
        values = jnp.zeros((1, 128), jnp.int32)
        for f in range(nf):
            values = jnp.where(place == f, cnt[(dp * nf + f) * spans + c], values)
        both.append(values > 1)
    st_put.wait()
    for move in stats:
        move.wait_recv()
    table = jnp.zeros((SPAN, 128), jnp.float32)
    scales = jnp.zeros((SPAN, 128), jnp.float32)
    for c in range(spans):
        pair = []
        for slot in range(SLOTS):
            found = jnp.zeros((SPAN, 128), jnp.float32)
            for g in range(nd):
                found = jnp.where(sources[SLOTS * c + slot] == g, st_home[g], found)
            pair.append(
                [found] + [pltpu.roll(found, 128 - group_lanes * i, axis=1) for i in (1, 2)]
            )
        (m0, l0, e0), (m1, l1, e1) = pair
        m1 = jnp.where(both[c], m1, -1e30)
        l1, e1 = jnp.where(both[c], l1, 0.0), jnp.where(both[c], e1, 0.0)
        peak = jnp.maximum(m0, m1)
        a0, a1 = jnp.exp(m0 - peak), jnp.exp(m1 - peak)
        total = a0 * l0 + a1 * l1
        log_total = peak + jnp.log(total)
        centre = (a0 * e0 + a1 * e1) / total
        for value, at in ((log_total, c * group_lanes), (centre, 64 + c * group_lanes)):
            moved = pltpu.roll(value, at, axis=1) if at else value
            inside = jnp.logical_and(lane >= at, lane < at + group_lanes)
            table = jnp.where(inside, moved, table)
        for slot, value in enumerate((a0 / total, a1 / total)):
            at = (SLOTS * c + slot) * group_lanes
            moved = pltpu.roll(value, at, axis=1) if at else value
            inside = jnp.logical_and(lane >= at, lane < at + group_lanes)
            scales = jnp.where(inside, moved, scales)
    weights[...] = scales
    hs[...] = table
    gives = [
        remote(hs, hs_out.at[dp], hsn.at[i], hr.at[i], "dp", p) for i, p in enumerate(peers)
    ]
    for move in gives:
        move.start()
    store(hs, hs_out.at[dp], 10)
    for move in q_moves + k_moves + list(sib_moves.values()) + ring_moves + q_there + u_there + stats + sum(v_moves, []):
        move.wait_send()
    for move in gives + o_there:
        move.wait()
    for put in puts:
        put.wait()


UNROLL = 4


def backward_kernel(
    nf, tab, q_any, u_any, hs_any, kt_any, vt_any, o_any, dq_any, dk_any, dv_any,
    q, u, hs, kt, vt, o_ref, dq_ref, dk_ref, dv_ref, k_acc, v_acc, listed, sems,
):
    pairs = ((q_any, q), (u_any, u), (hs_any, hs), (kt_any, kt), (vt_any, vt))
    loads = [pltpu.make_async_copy(a, b, sems.at[i]) for i, (a, b) in enumerate(pairs)]
    for copy in loads:
        copy.start()
    lane = lax.broadcasted_iota(jnp.int32, (SPAN, 128), 1)
    pieces, nbrs, piece = kt.shape[0], kt.shape[1], kt.shape[2]
    length = pieces * piece
    heads = kt.shape[3] // HEAD_DIM
    refs = q.shape[0]

    def place(r, ends):
        low, high = ends
        live = tab[2 * refs + r]
        listed[jnp.where(live > 0, low, high)] = r
        return low + live, high - 1 + live

    count, _ = lax.fori_loop(0, refs, place, (jnp.int32(0), jnp.int32(refs - 1)))

    @pl.loop(0, nbrs)
    def _(n):
        k_acc[n] = jnp.zeros(k_acc.shape[1:], jnp.float32)
        v_acc[n] = jnp.zeros(v_acc.shape[1:], jnp.float32)

    for copy in loads:
        copy.wait()

    def pick(array, at):
        return jnp.sum(jnp.where(lane == at, array, 0.0), axis=1, keepdims=True)

    @pl.loop(0, (count + UNROLL - 1) // UNROLL)
    def _(step):
        items = []
        for more in range(UNROLL):
            r = listed[step * UNROLL + more]
            n, c, live = tab[r], tab[refs + r], tab[2 * refs + r]
            into = jnp.where(live > 0, n, nbrs)
            items.append((r, n, into, heads * (nf * c + r % nf)))
        pairs = [(i, h) for i in range(UNROLL) for h in range(heads)]
        parts = [slice(h * HEAD_DIM, (h + 1) * HEAD_DIM) for h in range(heads)]

        def rows_of(ref, i, h):
            return ref[:, items[i][1], :, parts[h]].reshape(length, HEAD_DIM)

        def mark(i, h, offset):
            return pick(hs[items[i][0] // nf], offset + items[i][3] + h)

        scores = [dot(q[items[i][0], :, parts[h]], rows_of(kt, i, h), NT) for i, h in pairs]
        dprobs = [dot(u[items[i][0], :, parts[h]], rows_of(vt, i, h), NT) for i, h in pairs]
        probs = [jnp.exp(s * SCALE - mark(i, h, 0)) for s, (i, h) in zip(scores, pairs)]
        rounded = [value.astype(jnp.bfloat16) for value in probs]
        slopes = [
            (value * (d - mark(i, h, 64)) * SCALE).astype(jnp.bfloat16)
            for value, d, (i, h) in zip(probs, dprobs, pairs)
        ]
        for value, (i, h) in zip(rounded, pairs):
            if h > 0:
                o_ref[items[i][0]] = dot(value, rows_of(vt, i, h), NN).astype(jnp.bfloat16)
        dqs = [dot(value, rows_of(kt, i, h), NN) for value, (i, h) in zip(slopes, pairs)]
        for value, (i, h) in zip(dqs, pairs):
            dq_ref[items[i][0], :, parts[h]] = value.astype(jnp.bfloat16)
        dks = [dot(value, q[items[i][0], :, parts[h]], TN) for value, (i, h) in zip(slopes, pairs)]
        for value, (i, h) in zip(dks, pairs):
            k_acc[items[i][2], :, parts[h]] += value
        dvs = [dot(value, u[items[i][0], :, parts[h]], TN) for value, (i, h) in zip(rounded, pairs)]
        for value, (i, h) in zip(dvs, pairs):
            v_acc[items[i][2], :, parts[h]] += value

    puts = [
        pltpu.make_async_copy(o_ref, o_any, sems.at[5]),
        pltpu.make_async_copy(dq_ref, dq_any, sems.at[6]),
    ]
    for put in puts:
        put.start()
    for i, (acc, out, put_to) in enumerate(((k_acc, dk_ref, dk_any), (v_acc, dv_ref, dv_any))):
        @pl.loop(0, nbrs)
        def _(n):
            out[:, n] = acc[n].reshape(pieces, piece, -1).astype(jnp.bfloat16)

        put = pltpu.make_async_copy(out, put_to, sems.at[7 + i])
        put.start()
        puts.append(put)
    for put in puts:
        put.wait()


def finish_kernel(*refs):
    count = len(refs) // 3
    sems = refs[-1]
    takes = []
    for i in range(count):
        source, held = refs[i], refs[2 * count + i]
        pieces = 4 if source.shape[0] % 4 == 0 else 1
        size = source.shape[0] // pieces
        for j in range(pieces):
            part = pl.ds(j * size, size)
            take = pltpu.make_async_copy(source.at[part], held.at[part], sems.at[0, i, j])
            take.start()
            takes.append((i, j, part, take))
    puts = []
    for i, j, part, take in takes:
        take.wait()
        put = pltpu.make_async_copy(refs[2 * count + i].at[part], refs[count + i].at[part], sems.at[1, i, j])
        put.start()
        puts.append(put)
    for put in puts:
        put.wait()


def return_kernel(
    nd, nf, width, spans, src, cnt, weights, o_first, o, cot, dq, dk, dv, ga_out, gq, gk, gv, gp, att_all,
    o_a, o_b, dq_home, dq_sum, k_own, v_own, cot_vm, term, first_z, first_x, second, middle, keep, total,
    os, orr, qs, qr, ks, kr, vs, vr, ys, yr, fa, ga, ba, ca, ts, tr, own, load, last_sem,
):
    dp, fs = lax.axis_index("dp"), lax.axis_index("fsdp")
    chips = nf // 2
    chip, core = fs // 2, lax.rem(fs, 2)
    sibling = chip * 2 + 1 - core
    load_cot = pltpu.make_async_copy(cot, cot_vm, load.at[0])
    load_cot.start()
    enter((("dp", nd), ("fsdp", nf)))
    peers = [lax.rem(dp + step, nd) for step in range(1, nd)]
    firsts = [
        pltpu.make_async_copy(o_first, o_a, own.at[6]),
        pltpu.make_async_copy(o.at[dp], o_b.at[dp], own.at[7]),
        pltpu.make_async_copy(dq.at[dp], dq_home.at[dp], own.at[0]),
        pltpu.make_async_copy(dk.at[fs], k_own, own.at[1]),
        pltpu.make_async_copy(dv.at[fs], v_own, own.at[2]),
    ]
    for copy in firsts:
        copy.start()
    outs = [
        remote(o.at[p], o_b.at[dp], os.at[i], orr.at[i], "dp", p) for i, p in enumerate(peers)
    ]
    backs = [
        remote(dq.at[p], dq_home.at[dp], qs.at[i], qr.at[i], "dp", p) for i, p in enumerate(peers)
    ]
    for move in outs + backs:
        move.start()
    moves = []

    nbrs = dk.shape[1]
    early = nbrs // 4

    def give(ref, out, s_sem, r_sem, start, size, base):
        here = pl.ds(start, size)
        for step in range(1, nf):
            peer = lax.rem(fs + step, nf)
            at = pl.ds(pl.multiple_of(fs * width, width), width)
            place = base + step
            move = remote(ref.at[peer, here], out.at[here, :, at], s_sem.at[place], r_sem.at[place], "fsdp", peer)
            move.start()
            moves.append(move)

    give(dk, gk, ks, kr, 0, 8, 3 * nf)
    for copy in firsts:
        copy.wait()
    puts = [
        pltpu.make_async_copy(k_own, cols(gk, fs, width), own.at[3]),
        pltpu.make_async_copy(v_own, cols(gv, fs, width), own.at[4]),
    ]
    for put in puts:
        put.start()

    def add_slots(home, place, c, parts):
        span = (dp * nf + home) * spans + c
        first = parts[src[0, span], place].astype(jnp.float32)
        second = parts[src[1, span], place].astype(jnp.float32)
        both = cnt[span] > 1
        return (first + jnp.where(both, second, 0.0)).astype(jnp.bfloat16)

    to_sibling, around = [], {}
    lane = lax.broadcasted_iota(jnp.int32, (SPAN, 128), 1)
    table = weights[...]
    heads = width // HEAD_DIM

    def head_of(block, h):
        return att_all.at[block, :, pl.ds(h * HEAD_DIM, HEAD_DIM)]

    def weigh(home, c):
        span = (dp * nf + home) * spans + c
        value = jnp.zeros((SPAN, HEAD_DIM), jnp.float32)
        for slot in range(SLOTS):
            at = heads * (nf * (SLOTS * c + slot) + home)
            scale = jnp.sum(jnp.where(lane == at, table, 0.0), axis=1, keepdims=True)
            part = scale * o_a[src[slot, span], home].astype(jnp.float32)
            value += part if slot == 0 else jnp.where(cnt[span] > slot, part, 0.0)
        return value.astype(jnp.bfloat16)

    for h in range(heads):
        if h > 0:
            for move in outs:
                move.wait_recv()

        @pl.loop(0, nf)
        def _(home):
            for c in range(spans):
                at = pl.multiple_of((home * spans + c) * SPAN, SPAN)
                value = weigh(home, c) if h == 0 else add_slots(home, home, c, o_b)
                att_all[fs, pl.ds(at, SPAN), h * HEAD_DIM : (h + 1) * HEAD_DIM] = value

        att = head_of(fs, h)
        move = remote(att, att, fa.at[chips - 1 + h], ga.at[chips - 1 + h], "fsdp", sibling)
        move.start()
        to_sibling.append(move)
        for step in (0, chips - 2):
            there = lax.rem(chip + step + 1, chips) * 2 + core
            place = h * (chips - 1) + step
            move = remote(att, att, ba.at[place], ca.at[place], "fsdp", there)
            move.start()
            around[h, step] = move
        give(dk, gk, ks, kr, 8 + h * early, early, h * nf)
    load_cot.wait()
    share = width // nd
    columns = cot_vm.shape[1]
    tile = 256

    def add_dq():
        for move in backs:
            move.wait_recv()

        @pl.loop(0, nf)
        def _(home):
            for c in range(spans):
                dq_sum[home, c] = add_slots(home, home, c, dq_home)

        for step in range(1, nf):
            peer = lax.rem(fs + step, nf)
            move = remote(dq_sum.at[peer], cols(gq, fs, width), ys.at[step], yr.at[step], "fsdp", peer)
            move.start()
            moves.append(move)
        put = pltpu.make_async_copy(dq_sum.at[fs], cols(gq, fs, width), own.at[5])
        put.start()
        puts.append(put)

    nz = nd // 2
    x_at, z_at = dp // nz, lax.rem(dp, nz)
    across = lax.rem(dp + nz, nd)
    z_places = [lax.rem(z_at + step, nz) for step in range(1, nz)]
    z_peers = [x_at * nz + place for place in z_places]
    blocks = []
    flying = {}

    def along_z(turn):
        return turn % 2 == 0

    def launch(turn, stage, copies):
        sent = []
        for i, (source, target, peer) in enumerate(copies):
            place = stage * (nz - 1) + i
            move = remote(source, target, ts.at[turn, place], tr.at[turn, place], "dp", peer)
            move.start()
            sent.append(move)
        flying[turn, stage] = sent

    def arrive(turn, stage):
        for move in flying[turn, stage]:
            move.wait_recv()

    def project(turn, block):
        blocks.append(block)

        @pl.loop(0, columns // tile)
        def _(t):
            at = pl.ds(pl.multiple_of(t * tile, tile), tile)
            value = dot(att_all[block], cot_vm[:, at], TN).astype(jnp.bfloat16)
            term[turn, :, :, at] = value.reshape(nd, share, tile)

        half = turn // 2
        if along_z(turn):
            launch(turn, 0, [
                (term.at[turn, pl.ds(2 * place, 2)], first_z.at[half, i], p)
                for i, (place, p) in enumerate(zip(z_places, z_peers))
            ])
        else:
            launch(turn, 0, [(term.at[turn, pl.ds((1 - x_at) * nz, nz)], first_x.at[half], across)])

    def add_first(turn):
        arrive(turn, 0)
        half = turn // 2
        if along_z(turn):
            def total_of(place):
                value = term[turn, 2 * z_at + place].astype(jnp.float32)
                for i in range(nz - 1):
                    value += first_z[half, i, place].astype(jnp.float32)
                return value

            keep[turn] = total_of(x_at)
            middle[turn, 0] = total_of(1 - x_at).astype(jnp.bfloat16)
            launch(turn, 1, [(middle.at[turn, 0], second.at[turn, 0], across)])
        else:
            def total_of(place):
                value = term[turn, x_at * nz + place].astype(jnp.float32)
                return value + first_x[half, place].astype(jnp.float32)

            keep[turn] = total_of(z_at)
            for i, place in enumerate(z_places):
                middle[turn, i] = total_of(place).astype(jnp.bfloat16)
            launch(turn, 1, [
                (middle.at[turn, i], second.at[turn, i], p) for i, p in enumerate(z_peers)
            ])

    def rows_of(turn, part, parts):
        start = pl.multiple_of(blocks[turn] * width + part * share, share)
        return gp.at[pl.ds(start, parts * share)]

    owned = {}

    def add_second(turn):
        arrive(turn, 1)
        value = keep[turn]
        for i in range(len(flying[turn, 1])):
            value += second[turn, i].astype(jnp.float32)
        total[turn] = value.astype(jnp.bfloat16)
        part = 2 * z_at + x_at if along_z(turn) else dp
        here = rows_of(turn, part, 1)
        owned[turn] = pltpu.make_async_copy(total.at[turn], here, load.at[1 + turn])
        owned[turn].start()
        to = [across] if along_z(turn) else z_peers
        launch(turn, 2, [(total.at[turn], here, p) for p in to])

    def share_all(turn):
        owned[turn].wait()
        arrive(turn, 2)
        if along_z(turn):
            here = rows_of(turn, 2 * z_at, 2)
            launch(turn, 3, [(here, here, p) for p in z_peers])
        else:
            here = rows_of(turn, x_at * nz, nz)
            launch(turn, 3, [(here, here, across)])

    def advance(turn):
        for lag, act in ((2, add_first), (3, add_second), (4, share_all)):
            if 0 <= turn - lag < nf:
                act(turn - lag)

    project(0, fs)
    for move in to_sibling[:2]:
        move.wait_recv()
    project(1, sibling)
    for h, step in ((0, 0), (1, chips - 2)):
        for each in range(heads):
            around[each, step].wait_recv()
        back = lax.rem(chip + chips - step - 1, chips) * 2 + core
        there = lax.rem(chip + step + 1, chips) * 2 + core
        place = h * (chips - 1) + 1
        held = head_of(back, h)
        around[h, 1] = remote(held, held, ba.at[place], ca.at[place], "fsdp", there)
        around[h, 1].start()
    give(dk, gk, ks, kr, 8 + heads * early, nbrs - 8 - heads * early, heads * nf)
    give(dv, gv, vs, vr, 0, nbrs, 0)
    turn = 2
    order = [0, chips - 2] + list(range(1, chips - 2))
    for step in order:
        back = lax.rem(chip + chips - step - 1, chips) * 2
        if step == 1:
            for each in range(heads):
                around[each, 1].wait_recv()
        move = remote(
            att_all.at[back + core], att_all.at[back + core], fa.at[step], ga.at[step], "fsdp", sibling
        )
        move.start()
        to_sibling.append(move)
        project(turn, back + core)
        advance(turn)
        move.wait_recv()
        project(turn + 1, back + 1 - core)
        advance(turn + 1)
        if turn == 4:
            add_dq()
        turn += 2
    for later in range(turn, turn + 4):
        advance(later)
    tokens = spans * SPAN
    for block in range(nf):
        here = pl.ds(pl.multiple_of(fs * tokens, tokens), tokens)
        put = pltpu.make_async_copy(
            att_all.at[block, here], ga_out.at[:, pl.ds(block * width, width)], last_sem.at[block]
        )
        put.start()
        puts.append(put)
    for move in outs + backs + to_sibling + list(around.values()):
        move.wait_send()
    for (_, stage), sent in flying.items():
        for move in sent:
            if stage == 3:
                move.wait_recv()
            move.wait_send()
    for move in moves:
        move.wait()
    for put in puts:
        put.wait()


def dma(*shape):
    return pltpu.SemaphoreType.DMA(shape)


def comm(number, mib=BIG):
    return pltpu.CompilerParams(collective_id=number, has_side_effects=True, vmem_limit_bytes=mib)


def local(queries, nbr_keys, nbr_values, out_proj, nbr_source, nbr_index, nbr_count, cotangent):
    nd, nf = lax.axis_size("dp"), lax.axis_size("fsdp")
    bf, f32, i32 = jnp.bfloat16, jnp.float32, jnp.int32
    token_rows, full_width = queries.shape
    spans = token_rows // SPAN
    nbrs, piece, _ = nbr_keys.shape
    width = full_width // nf
    rows, columns = cotangent.shape
    refs_all = nd * nf
    chips = nf // 2
    sources, indices = nbr_source.T, nbr_index.T
    share = width // nd

    kt, vt, qg, ug, hs, tab, o_first, weights = pl.pallas_call(
        lambda *a: spread_kernel(nd, nf, width, *a),
        in_specs=[SM, SM, SM, ANY, ANY, ANY, ANY, ANY],
        out_specs=[ANY, ANY, ANY, ANY, ANY, SM, ANY, VM],
        out_shape=[
            jax.ShapeDtypeStruct((nf, nbrs, piece, width), bf),
            jax.ShapeDtypeStruct((nf, nbrs, piece, width), bf),
            jax.ShapeDtypeStruct((nd, nf, SPAN, width), bf),
            jax.ShapeDtypeStruct((nd, nf, SPAN, width), bf),
            jax.ShapeDtypeStruct((nd, SPAN, 128), f32),
            jax.ShapeDtypeStruct((3 * refs_all,), i32),
            jax.ShapeDtypeStruct((nd, nf, SPAN, HEAD_DIM), bf),
            jax.ShapeDtypeStruct((SPAN, 128), f32),
        ],
        scratch_shapes=[
            pltpu.VMEM((nf, spans, SPAN, width), bf),
            pltpu.VMEM((2, nd, nf, SPAN, width), bf),
            pltpu.VMEM((nf, nbrs, piece, width), bf),
            pltpu.VMEM((nf, nbrs, piece, HEAD_DIM), bf),
            pltpu.VMEM((nf, nbrs, piece, HEAD_DIM), bf),
            pltpu.VMEM((nd, nf, SPAN, width), bf),
            pltpu.VMEM((nd, nf, SPAN, width), bf),
            pltpu.VMEM((nf * spans, SPAN, width), bf),
            pltpu.VMEM((rows, columns), bf),
            pltpu.VMEM((full_width, columns), bf),
            pltpu.VMEM((chips, rows, width), bf),
            pltpu.VMEM((chips, rows, width), bf),
            pltpu.VMEM((chips, rows, width), f32),
            pltpu.VMEM((chips - 1, rows, width), bf),
            pltpu.VMEM((chips - 1, rows, width), bf),
            pltpu.VMEM((width // HEAD_DIM, refs_all, SPAN, nf * piece), f32),
            pltpu.VMEM((nd, SPAN, 128), f32),
            pltpu.VMEM((nd, SPAN, 128), f32),
            pltpu.VMEM((SPAN, 128), f32),
            pltpu.SMEM((refs_all,), i32),
            pltpu.VMEM((nd, nf, SPAN, HEAD_DIM), bf),
            dma(nf), dma(nf), dma(2 * nf), dma(2 * nf), dma(2 * nf), dma(2 * nf), dma(nd), dma(nd), dma(nd), dma(nd),
            dma(chips), dma(chips), dma(6), dma(6), dma(nd), dma(nd), dma(nd), dma(nd), dma(nd), dma(nd), dma(14), dma(2),
        ],
        compiler_params=comm(1),
        name="spread",
    )(
        sources, indices, nbr_count, queries.reshape(spans, SPAN, full_width), nbr_keys, nbr_values,
        cotangent, out_proj,
    )

    o, dq, dk, dv = pl.pallas_call(
        lambda *a: backward_kernel(nf, *a),
        in_specs=[SM, ANY, ANY, ANY, ANY, ANY],
        out_specs=[ANY, ANY, ANY, ANY],
        out_shape=[
            jax.ShapeDtypeStruct((refs_all, SPAN, HEAD_DIM), bf),
            jax.ShapeDtypeStruct((refs_all, SPAN, width), bf),
            jax.ShapeDtypeStruct((nf, nbrs, piece, width), bf),
            jax.ShapeDtypeStruct((nf, nbrs, piece, width), bf),
        ],
        scratch_shapes=[
            pltpu.VMEM((refs_all, SPAN, width), bf),
            pltpu.VMEM((refs_all, SPAN, width), bf),
            pltpu.VMEM((nd, SPAN, 128), f32),
            pltpu.VMEM((nf, nbrs, piece, width), bf),
            pltpu.VMEM((nf, nbrs, piece, width), bf),
            pltpu.VMEM((refs_all, SPAN, HEAD_DIM), bf),
            pltpu.VMEM((refs_all, SPAN, width), bf),
            pltpu.VMEM((nf, nbrs, piece, width), bf),
            pltpu.VMEM((nf, nbrs, piece, width), bf),
            pltpu.VMEM((nbrs + 1, nf * piece, width), f32),
            pltpu.VMEM((nbrs + 1, nf * piece, width), f32),
            pltpu.SMEM((refs_all,), i32),
            dma(9),
        ],
        compiler_params=pltpu.CompilerParams(vmem_limit_bytes=BIG),
        name="backward",
    )(tab, qg.reshape(refs_all, SPAN, width), ug.reshape(refs_all, SPAN, width), hs, kt, vt)

    attended, gq, gk, gv, grad_proj = pl.pallas_call(
        lambda *a: return_kernel(nd, nf, width, spans, *a),
        in_specs=[SM, SM, VM, ANY, ANY, ANY, ANY, ANY, ANY],
        out_specs=[ANY, ANY, ANY, ANY, ANY],
        out_shape=[
            jax.ShapeDtypeStruct((token_rows, full_width), bf),
            jax.ShapeDtypeStruct((spans, SPAN, full_width), bf),
            jax.ShapeDtypeStruct((nbrs, piece, full_width), bf),
            jax.ShapeDtypeStruct((nbrs, piece, full_width), bf),
            jax.ShapeDtypeStruct((full_width, columns), bf),
        ],
        scratch_shapes=[
            pltpu.VMEM((nf, rows, width), bf),
            pltpu.VMEM((nd, nf, SPAN, HEAD_DIM), bf),
            pltpu.VMEM((nd, nf, SPAN, HEAD_DIM), bf),
            pltpu.VMEM((nd, nf, SPAN, width), bf),
            pltpu.VMEM((nf, spans, SPAN, width), bf),
            pltpu.VMEM((nbrs, piece, width), bf),
            pltpu.VMEM((nbrs, piece, width), bf),
            pltpu.VMEM((rows, columns), bf),
            pltpu.VMEM((nf, nd, share, columns), bf),
            pltpu.VMEM((nf // 2, nd // 2 - 1, 2, share, columns), bf),
            pltpu.VMEM((nf // 2, nd // 2, share, columns), bf),
            pltpu.VMEM((nf, nd // 2 - 1, share, columns), bf),
            pltpu.VMEM((nf, nd // 2 - 1, share, columns), bf),
            pltpu.VMEM((nf, share, columns), f32),
            pltpu.VMEM((nf, share, columns), bf),
            dma(nd), dma(nd), dma(nd), dma(nd), dma(4 * nf), dma(4 * nf), dma(nf), dma(nf), dma(nf), dma(nf),
            dma(chips + 1), dma(chips + 1), dma(2 * chips), dma(2 * chips),
            dma(nf, 2 * nd), dma(nf, 2 * nd), dma(8), dma(1 + nf), dma(nf),
        ],
        compiler_params=comm(3),
        name="giveback",
    )(
        sources, nbr_count, weights, o_first, o.reshape(nd, nf, SPAN, HEAD_DIM), cotangent,
        dq.reshape(nd, nf, SPAN, width), dk, dv,
    )
    results = [grad_proj, gk, gv, attended, gq.reshape(token_rows, full_width)]
    grad_proj, gk, gv, attended, gq = pl.pallas_call(
        finish_kernel,
        in_specs=[ANY] * len(results),
        out_specs=[ANY] * len(results),
        out_shape=[jax.ShapeDtypeStruct(value.shape, value.dtype) for value in results],
        scratch_shapes=[pltpu.VMEM(value.shape, value.dtype) for value in results] + [dma(2, len(results), 4)],
        compiler_params=pltpu.CompilerParams(vmem_limit_bytes=BIG),
        name="finish",
    )(*results)
    return (attended, gq, gk, gv, grad_proj)


def solution(mesh):
    placed = (
        P(("dp", "fsdp"), "enc"),
        P("dp", "fsdp", "enc"),
        P("dp", "fsdp", "enc"),
        P("enc", "fsdp"),
        P(),
        P(),
        P(),
        P("dp", "fsdp"),
    )
    return jax.shard_map(
        local,
        mesh=mesh,
        in_specs=placed,
        out_specs=(
            P(("dp", "fsdp"), "enc"),
            P(("dp", "fsdp"), "enc"),
            P("dp", "fsdp", "enc"),
            P("dp", "fsdp", "enc"),
            P("enc", "fsdp"),
        ),
        check_vma=False,
    )
```
